32 devices in a mesh: obs: 8 (over z, y), cell: 4 (over x, core).
Axes of the slice: x: 2, y: 2, z: 4, core: 2. Of those that a mesh axis runs over, the one named last changes fastest.
Arguments:
- footprint: bfloat16 [512, 16, 4096], P('obs', None, 'cell'), may hold values from -0.75 to 0.75
- block_mask: int32 [512, 32], P('obs', 'cell'), may hold values 0 or 1
- cell_coords: int32 [2, 4096], P(None, 'cell'), may hold values from 0 to 63, as said below
- cell_sigma: float32 [4096], P('cell'), may hold values from 0.3 to 3
- time_cov: float32 [16, 16], replicated, as said below
- error_var: float32 [512], P('obs'), may hold values from 0.3 to 300
- panel_index: int32 [128], replicated, may hold values from 0 to 511, as said below
Outputs:
- cov_product: bfloat16 [512, 16, 4096], P('obs', None, 'cell')
- innovation_panel: float32 [512, 128], P('obs')
The draws below stay inside these ranges and needn't reach their ends.
Inputs may be any that keep to these rules, and one draw needn't show every extreme that they name: `cell_coords`: each cell holds a distinct point of the 64 by 64 grid, and every point is held by some cell. `time_cov`: Symmetric. `panel_index`: entries are distinct; entries k * 16 to (k + 1) * 16 - 1 name observations among rows k * 64 to (k + 1) * 64 - 1.
All inputs are finite; a program needn't handle non-finite values. No bound on the sum of `block_mask` on one device may be relied on, other than what follows from the above.
Results may differ from the reference program's by a relative error of at most 0.0049.
Values may be sent and summed in bfloat16 or wider, within the bound.
No kernel may reach another device: no remote copies, remote signals or barrier semaphores. Data moves between devices by JAX's collectives and lax.ppermute only.
A program may use at most 64 MiB of HBM per device.

```python
import math
import jax
import jax.numpy as jnp
from jax import lax

GRID = 64
NT = 16
CBLK = 128
NPANEL = 128
OBS_DEV = 64
NCELL = 4096
NOBS = 512
PAN_DEV = 16


def draw_cell_coords(key, part):
    order = jax.random.permutation(key, GRID * GRID)[:NCELL].astype(jnp.int32)
    return jnp.stack([order // GRID, order % GRID]).astype(jnp.int32)


def draw_time_cov(key, part):
    base = jnp.clip(jax.random.normal(key, (NT, NT), jnp.float32), -3.0, 3.0)
    symmetric = (base + base.T) * (0.5 / math.sqrt(NT))
    return jnp.eye(NT, dtype=jnp.float32) + symmetric


def draw_panel_index(key, part):
    block_count = NOBS // OBS_DEV
    keys = jax.random.split(key, block_count)
    perms = jax.vmap(lambda single: jax.random.permutation(single, OBS_DEV))(keys)[:, :PAN_DEV].astype(jnp.int32)
    shifts = jax.random.randint(jax.random.fold_in(key, 7), (block_count,), 0, OBS_DEV).astype(jnp.int32)
    shifts = shifts.at[0].set(0).at[block_count - 1].set(OBS_DEV - 1)
    offsets = (perms - perms[:, :1] + shifts[:, None]) % OBS_DEV
    bases = jnp.arange(block_count, dtype=jnp.int32)[:, None] * OBS_DEV
    return (offsets + bases).reshape(NPANEL).astype(jnp.int32)


def touch_ends(values, stream_key, low, top_value):
    longest = values.shape.index(max(values.shape))
    spots = []
    for shift in (0, 1):
        where = [jax.random.randint(jax.random.fold_in(stream_key, axis), (), 0, length) for axis, length in enumerate(values.shape)]
        where[longest] = (where[longest] + shift) % values.shape[longest]
        spots.append(tuple(where))
    return values.at[spots[0]].set(low).at[spots[1]].set(top_value)


def block_scale(own_key, extent, pieces, least, largest):
    def one(position, parts):
        heights = jax.random.uniform(jax.random.fold_in(jax.random.fold_in(own_key, 6), position), (parts,), jnp.float32, least / len(pieces), largest / len(pieces))
        return jnp.repeat(jnp.exp(heights), extent[position] // parts).reshape((-1,) + (1,) * (len(extent) - position - 1))

    level = one(*pieces[0])
    for cut in pieces[1:]:
        level = level * one(*cut)
    return level


def normal_values(rng, extent, width, most, cuts=(), kind=jnp.bfloat16):
    values = jax.random.normal(rng, extent, jnp.float32) * width
    if len(cuts) > 0:
        values = block_scale(rng, extent, cuts, -0.22, 0.18) * values
    return jnp.clip(values, min=-most, max=most).astype(kind)


def setup_inputs(seed: int = 0) -> dict:
    arg_keys = jax.random.split(jax.random.key(seed), 8)
    footprint = normal_values(arg_keys[0], (NOBS, NT, NCELL), (4.0 / (NT * GRID) ** 0.5), 0.75, ((0, 8), (2, 4)))
    block_mask = touch_ends((jax.random.randint(arg_keys[1], (NOBS, NCELL // CBLK), 0, 2) < 1).astype(jnp.int32), jax.random.fold_in(arg_keys[1], 1), 0, 1)
    cell_coords = draw_cell_coords(jax.random.fold_in(arg_keys[7], 71), 0)
    cell_sigma = jnp.clip(jnp.exp(math.log(3.0) - 2.3025851 * jax.random.uniform(arg_keys[3], (NCELL,), jnp.float32) ** block_scale(arg_keys[3], (NCELL,), ((0, 4),), -0.2, 0.2)), 0.3, 3.0)
    time_cov = draw_time_cov(jax.random.fold_in(arg_keys[7], 71), 0)
    error_var = jnp.clip(jnp.exp(math.log(300.0) - 6.9077552 * jax.random.uniform(arg_keys[5], (NOBS,), jnp.float32) ** block_scale(arg_keys[5], (NOBS,), ((0, 8),), -0.2, 0.2)), 0.3, 300.0)
    panel_index = draw_panel_index(jax.random.fold_in(arg_keys[7], 71), 0)
    return dict(footprint=footprint, block_mask=block_mask, cell_coords=cell_coords, cell_sigma=cell_sigma, time_cov=time_cov, error_var=error_var, panel_index=panel_index)


def covariance(row_info, col_info):
    length = GRID / 16.0
    delta_x = row_info[0][:, None] - col_info[0][None, :]
    delta_y = row_info[1][:, None] - col_info[1][None, :]
    decay = jnp.exp(-jnp.sqrt(delta_x * delta_x + delta_y * delta_y + 1.0) / length)
    return (decay * (row_info[2][:, None] * col_info[2][None, :])).astype(jnp.bfloat16)

def reference(footprint, block_mask, cell_coords, cell_sigma, time_cov, error_var, panel_index):
    obs_count, time_count, cell_count = footprint.shape
    keep = block_mask.astype(jnp.bfloat16)[:, None, :, None]
    footprints = (footprint.reshape(obs_count, time_count, cell_count // CBLK, CBLK) * keep).reshape(obs_count, time_count, cell_count)
    cell_info = jnp.concatenate([cell_coords.astype(jnp.float32), cell_sigma[None, :]], axis=0)
    rows_h = footprints.reshape(obs_count * time_count, cell_count)
    col_width = min(256, cell_count)

    def column_block(col_first):
        col_info = lax.dynamic_slice_in_dim(cell_info, col_first, col_width, 1)
        spatial = jnp.dot(rows_h, covariance(cell_info, col_info), preferred_element_type=jnp.float32)
        mixed_block = jnp.einsum('ts,osc->otc', time_cov, spatial.reshape(obs_count, time_count, col_width), precision=lax.Precision.HIGHEST)
        return mixed_block.astype(jnp.bfloat16)
    starts = jnp.arange(cell_count // col_width, dtype=jnp.int32) * col_width
    blocks = lax.map(column_block, starts)
    cov_product = jnp.moveaxis(blocks, 0, 2).reshape(obs_count, time_count, cell_count)
    panel_rows = footprints[panel_index].reshape(NPANEL, time_count * cell_count)
    panel = jnp.dot(cov_product.reshape(obs_count, time_count * cell_count), panel_rows.T, preferred_element_type=jnp.float32)
    on_diagonal = (jnp.arange(obs_count, dtype=jnp.int32)[:, None] == panel_index[None, :]).astype(jnp.float32)
    return (cov_product, panel + error_var[:, None] * on_diagonal)
```

```python
import jax
import jax.numpy as jnp
from jax import lax
from jax.sharding import PartitionSpec as P

GRID = 64


def covariance(row_info, col_info):
    length = GRID / 16.0
    delta_x = row_info[0][:, None] - col_info[0][None, :]
    delta_y = row_info[1][:, None] - col_info[1][None, :]
    decay = jnp.exp(-jnp.sqrt(delta_x * delta_x + delta_y * delta_y + 1.0) / length)
    return (decay * (row_info[2][:, None] * col_info[2][None, :])).astype(jnp.bfloat16)


def temporal_mix(time_cov, spatial):
    return jnp.einsum("ts,ksc->ktc", time_cov, spatial, precision=lax.Precision.HIGHEST).astype(
        jnp.bfloat16
    )


def partner(value, axis, count):
    return lax.ppermute(value, axis, [(i, i ^ 1) for i in range(count)])


def shifted(value, axis, count, shift):
    return lax.ppermute(value, axis, [(i, (i + 2 * shift) % count) for i in range(count)])


def body(cells, observers, footprint, block_mask, cell_coords, cell_sigma, time_cov, error_var, panel_index):
    obs_rows, time_count, cell_local = footprint.shape
    block_local = block_mask.shape[1]
    keep = block_mask.astype(jnp.bfloat16)[:, None, :, None]
    footprints = (
        footprint.reshape(obs_rows, time_count, block_local, cell_local // block_local) * keep
    ).reshape(obs_rows, time_count, cell_local)
    own_info = jnp.concatenate([cell_coords.astype(jnp.float32), cell_sigma[None, :]], axis=0)
    group = lax.axis_index("obs")
    panel_each = panel_index.shape[0] // observers
    mine = lax.dynamic_slice_in_dim(panel_index, group * panel_each, panel_each) - group * obs_rows
    own_panel = jnp.take(footprints, mine, axis=0)

    sources = [(footprints, own_info)]
    for shift in range(1, cells // 2):
        sources.append(tuple(shifted(v, "cell", cells, shift) for v in sources[0]))
    sources += [tuple(partner(v, "cell", cells) for v in pair) for pair in sources]

    ring = [own_panel]
    for _ in range(1, observers // 2):
        ring.append(shifted(ring[-1], "obs", observers, 1))
    other = [partner(v, "obs", observers) for v in ring]

    order = sources[:1] + sources[cells // 2 : cells // 2 + 1] + sources[1 : cells // 2] + sources[cells // 2 + 1 :]
    running = None
    for feet, info in order:
        part = jnp.dot(
            feet.reshape(obs_rows * time_count, cell_local),
            covariance(info, own_info),
            preferred_element_type=jnp.float32,
        )
        running = part if running is None else running + part
    cov_product = temporal_mix(time_cov, running.reshape(obs_rows, time_count, cell_local))
    flat_cov = cov_product.reshape(obs_rows, time_count * cell_local)
    pieces = []
    for step in range(observers // 2):
        both = jnp.concatenate([ring[step], other[step]], axis=0)
        pieces.append(
            lax.dot_general(
                flat_cov,
                both.reshape(2 * panel_each, time_count * cell_local),
                (((1,), (1,)), ((), ())),
                preferred_element_type=jnp.float32,
            )
        )
    partial_value = jnp.stack(pieces)
    total = partial_value
    pair = partial_value + partner(partial_value, "cell", cells)
    total = pair
    for shift in range(1, cells // 2):
        total = total + shifted(pair, "cell", cells, shift)
    half = observers // 2
    hi, lo = group // 2, group % 2
    total = total.reshape(half, obs_rows, 2, panel_each)
    total = jnp.where(lo == 0, total, total[:, :, ::-1])
    total = jnp.roll(total[::-1], hi + 1, axis=0)
    summed = total.transpose(1, 0, 2, 3).reshape(obs_rows, panel_index.shape[0])
    positions = jnp.arange(obs_rows, dtype=jnp.int32)
    on_diagonal = ((group * obs_rows + positions)[:, None] == panel_index[None, :]).astype(jnp.float32)
    return (cov_product, summed + error_var[:, None] * on_diagonal)


def solution(mesh):
    in_specs = (
        P("obs", None, "cell"),
        P("obs", "cell"),
        P(None, "cell"),
        P("cell"),
        P(),
        P("obs"),
        P(),
    )
    out_specs = (P("obs", None, "cell"), P("obs", None))
    cells, observers = mesh.shape["cell"], mesh.shape["obs"]

    def per_device(*args):
        return body(cells, observers, *args)

    return jax.shard_map(
        per_device, mesh=mesh, in_specs=in_specs, out_specs=out_specs, check_vma=False
    )
```

```python
import functools
import math

import jax
import jax.numpy as jnp
from jax import lax
from jax.experimental import pallas as pl
from jax.experimental.pallas import tpu as pltpu
from jax.sharding import PartitionSpec as P

GRID = 64
LENGTH = GRID / 16.0
F32, BF16, I32 = jnp.float32, jnp.bfloat16, jnp.int32


VMEM = pl.BlockSpec(memory_space=pltpu.VMEM)
SMEM = pl.BlockSpec(memory_space=pltpu.SMEM)
ANY = pl.BlockSpec(memory_space=pl.ANY)


def shape_of(shape, dtype):
    return jax.ShapeDtypeStruct(shape, dtype)


def params(mib=40):
    return pltpu.CompilerParams(vmem_limit_bytes=mib * 2**20)


def cost(flops, moved):
    return pl.CostEstimate(flops=flops, bytes_accessed=moved, transcendentals=0)


def slot_count(tiles):
    room = tiles / 2 + 4.2 * math.sqrt(tiles / 4) + 2
    return min(tiles + 2, 8 * math.ceil(room / 8))


def pack_rows(mask_at, feet_at, rows, blocks, lanes, buf):
    slots, times, _ = buf.shape
    flat = lax.broadcasted_iota(I32, (times, lanes), 0) * lanes + lax.broadcasted_iota(I32, (times, lanes), 1)

    def one(o, carry):
        pos, head = carry
        for b in range(blocks):
            kept = mask_at(o, b)
            buf[jnp.minimum(pos, slots - 1)] = feet_at(o, b)
            pos = pos + kept
            head = jnp.where(flat == o * blocks + b, kept, head)
        return pos, head

    return lax.fori_loop(0, rows, one, (jnp.int32(1), jnp.zeros((times, lanes), I32)))


def pack_feet_kernel(mask_ref, feet_ref, out_ref):
    rows, blocks = mask_ref.shape
    lanes = feet_ref.shape[2] // blocks
    _, head = pack_rows(
        lambda o, b: mask_ref[o, b],
        lambda o, b: feet_ref[o, :, b * lanes : (b + 1) * lanes],
        rows,
        blocks,
        lanes,
        out_ref,
    )
    out_ref[0] = head.astype(F32).astype(BF16)


def pack_feet(mask, feet):
    rows, times, cells = feet.shape
    blocks = mask.shape[1]
    slots = slot_count(rows * blocks)
    out = shape_of((slots, times, cells // blocks), BF16)
    return pl.pallas_call(
        pack_feet_kernel,
        out_shape=out,
        in_specs=[SMEM, VMEM],
        out_specs=VMEM,
        compiler_params=params(16),
        cost_estimate=cost(0, 8_000_000),
        name="pack_feet",
    )(mask, feet)


def pack_panel_kernel(mask_ref, mine_ref, flag_ref, feet_ref, out_ref, rows_buf, sem):
    count = mine_ref.shape[0]
    blocks = mask_ref.shape[1]
    lanes = rows_buf.shape[2] // blocks
    copies = [pltpu.make_async_copy(feet_ref.at[mine_ref[j]], rows_buf.at[j], sem.at[j]) for j in range(count)]
    for copy in copies:
        copy.start()
    for copy in copies:
        copy.wait()
    _, head = pack_rows(
        lambda o, b: mask_ref[mine_ref[o], b],
        lambda o, b: rows_buf[o, :, b * lanes : (b + 1) * lanes],
        count,
        blocks,
        lanes,
        out_ref,
    )
    times = head.shape[0]
    last = lax.broadcasted_iota(I32, head.shape, 0) == times - 1
    head = jnp.where(last, flag_ref[0], head)
    out_ref[0] = head.astype(F32).astype(BF16)


def pack_panel(mask, mine, flag, feet):
    rows, times, cells = feet.shape
    blocks = mask.shape[1]
    count = mine.shape[0]
    slots = slot_count(count * blocks)
    return pl.pallas_call(
        pack_panel_kernel,
        out_shape=shape_of((slots, times, cells // blocks), BF16),
        in_specs=[SMEM, SMEM, SMEM, ANY],
        out_specs=VMEM,
        scratch_shapes=[pltpu.VMEM((count, times, cells), BF16), pltpu.SemaphoreType.DMA((count,))],
        compiler_params=params(16),
        cost_estimate=cost(0, 2_000_000),
        name="pack_panel",
    )(mask, mine, flag, feet)


def fetch(src, buf, sem):
    slots = src.shape[0]
    copy = pltpu.make_async_copy(src, buf.at[pl.ds(0, slots)], sem)
    copy.start()
    buf[slots] = jnp.zeros(buf.shape[1:], buf.dtype)
    return copy


def read_bits(buf, bits_v, bits_s, sem):
    bits_v[...] = buf[0].astype(F32).astype(I32)
    copy = pltpu.make_async_copy(bits_v, bits_s, sem)
    copy.start()
    copy.wait()


def expand(buf, bits, first, count, blocks, pos, store):
    slots = buf.shape[0] - 1
    lanes = buf.shape[2]

    def one(i, pos):
        base = (first + i) * blocks
        row, col = base // lanes, base % lanes
        for b in range(blocks):
            kept = bits[row, col + b]
            store(i, b, buf[jnp.where(kept > 0, jnp.minimum(pos, slots - 1), slots)])
            pos = pos + kept
        return pos

    return lax.fori_loop(0, count, one, pos)


def fill_covariance(dst, first, info_ref, own_ref, turned):
    cells = info_ref.shape[1]
    turned[...] = info_ref[...].T
    x, y, s = own_ref[0:1, :], own_ref[1:2, :], own_ref[2:3, :]

    def rows(i, _):
        at = pl.ds(pl.multiple_of(i * 16, 16), 16)
        dx = turned[at, 0:1] - x
        dy = turned[at, 1:2] - y
        square = dx * dx + dy * dy + 1.0
        decay = jnp.exp(square * lax.rsqrt(square) * (-1.0 / LENGTH))
        dst[pl.ds(pl.multiple_of(first + i * 16, 16), 16), :] = (decay * (turned[at, 2:3] * s)).astype(BF16)
        return 0

    lax.fori_loop(0, cells // 16, rows, 0)


def local_kernel(own_msg, mate_msg, own_ref, mate_ref, out_ref, buf, bits_v, bits_s, dense, cov, turned, sem):
    times, lanes = buf.shape[1:]
    rows = dense.shape[0] // times
    blocks = dense.shape[1] // lanes
    cells = dense.shape[1]
    width = min(256, cells)
    for k, (msg, info) in enumerate(((own_msg, own_ref), (mate_msg, mate_ref))):
        copy = fetch(msg, buf, sem.at[0])
        fill_covariance(cov, 0, info, own_ref, turned)
        copy.wait()
        read_bits(buf, bits_v, bits_s, sem.at[1])

        def store(i, b, tile):
            dense[pl.ds(pl.multiple_of(i * times, times), times), b * lanes : (b + 1) * lanes] = tile

        expand(buf, bits_s, 0, rows, blocks, jnp.int32(1), store)

        @pl.loop(0, cells // width)
        def _(n):
            at = pl.ds(pl.multiple_of(n * width, width), width)
            part = jnp.dot(dense[...], cov[:, at], preferred_element_type=F32)
            if k == 0:
                out_ref[:, at] = part
            else:
                out_ref[:, at] += part


def local_product(own_msg, mate_msg, own_info, mate_info, rows):
    slots, times, lanes = own_msg.shape
    cells = own_info.shape[1]
    return pl.pallas_call(
        local_kernel,
        out_shape=shape_of((rows * times, cells), F32),
        in_specs=[ANY, ANY, VMEM, VMEM],
        out_specs=VMEM,
        scratch_shapes=[
            pltpu.VMEM((slots + 1, times, lanes), BF16),
            pltpu.VMEM((times, lanes), I32),
            pltpu.SMEM((times, lanes), I32),
            pltpu.VMEM((rows * times, cells), BF16),
            pltpu.VMEM((cells, cells), BF16),
            pltpu.VMEM((cells, own_info.shape[0]), F32),
            pltpu.SemaphoreType.DMA((2,)),
        ],
        compiler_params=params(),
        cost_estimate=cost(4 * rows * times * cells * cells, 8_000_000),
        name="local_product",
    )(own_msg, mate_msg, own_info, mate_info)


def far_cov_kernel(*refs):
    *infos, own_ref, out_ref, turned = refs
    cells = own_ref.shape[1]
    for k, info in enumerate(infos):
        fill_covariance(out_ref, k * cells, info, own_ref, turned)


def far_covariance(infos, own_info):
    cells = own_info.shape[1]
    return pl.pallas_call(
        far_cov_kernel,
        out_shape=shape_of((len(infos) * cells, cells), BF16),
        in_specs=[VMEM] * (len(infos) + 1),
        out_specs=VMEM,
        scratch_shapes=[pltpu.VMEM((cells, own_info.shape[0]), F32)],
        compiler_params=params(16),
        cost_estimate=cost(30 * len(infos) * cells * cells, 4_000_000),
        name="far_covariance",
    )(*infos, own_info)


def rows_kernel(count, unit, *refs):
    msgs = refs[:count]
    cov_ref, near_ref, mix_ref, out_ref, turn_ref, bufs, bits_v, bits_s, dense, sem = refs[count:]
    times, lanes = bufs.shape[2:]
    cells = near_ref.shape[1]
    blocks = cells // lanes
    width = min(256, cells)
    rows = out_ref.shape[0]
    copies = [fetch(msg, bufs.at[k], sem.at[k]) for k, msg in enumerate(msgs)]
    for k, copy in enumerate(copies):
        copy.wait()
        read_bits(bufs.at[k], bits_v, bits_s.at[k], sem.at[count])

    def step(u, places):
        after = []
        for k in range(count):

            def store(i, b, tile):
                at = pl.ds(pl.multiple_of(i * times, times), times)
                dense[at, k * cells + b * lanes : k * cells + (b + 1) * lanes] = tile

            after.append(expand(bufs.at[k], bits_s.at[k], u * unit, unit, blocks, places[k], store))
        here = pl.ds(pl.multiple_of(u * unit * times, unit * times), unit * times)

        @pl.loop(0, cells // width)
        def _(n):
            at = pl.ds(pl.multiple_of(n * width, width), width)
            value = near_ref[here, at] + jnp.dot(dense[...], cov_ref[:, at], preferred_element_type=F32)
            high = value.astype(BF16)
            low = (value - high.astype(F32)).astype(BF16)
            mixed = jnp.dot(
                mix_ref[...], jnp.concatenate([high, low, high], axis=0), preferred_element_type=F32
            ).astype(BF16)
            rows_at = pl.ds(pl.multiple_of(u * unit, unit), unit)
            out_ref[rows_at, :, at] = mixed[: unit * times].reshape(unit, times, width)
            turn_ref[:, rows_at, at] = mixed[unit * times :].reshape(times, unit, width)

        return tuple(after)

    lax.fori_loop(0, rows // unit, step, tuple(jnp.int32(1) for _ in range(count)))


def far_rows(msgs, cov, near, mix, rows, unit):
    slots, times, lanes = msgs[0].shape
    cells = near.shape[1]
    count = len(msgs)
    return pl.pallas_call(
        functools.partial(rows_kernel, count, unit),
        out_shape=(shape_of((rows, times, cells), BF16), shape_of((times, rows, cells), BF16)),
        in_specs=[ANY] * count + [VMEM] * 3,
        out_specs=(VMEM, VMEM),
        scratch_shapes=[
            pltpu.VMEM((count, slots + 1, times, lanes), BF16),
            pltpu.VMEM((times, lanes), I32),
            pltpu.SMEM((count, times, lanes), I32),
            pltpu.VMEM((unit * times, count * cells), BF16),
            pltpu.SemaphoreType.DMA((count + 1,)),
        ],
        compiler_params=params(),
        cost_estimate=cost(2 * rows * times * cells * cells * count, 16_000_000),
        name="far_rows",
    )(*msgs, cov, near, mix)


def mixing(time_cov, unit):
    times = time_cov.shape[0]
    eye = jnp.eye(unit, dtype=F32)
    straight = jnp.einsum("ab,ts->atbs", eye, time_cov, precision=lax.Precision.HIGHEST)
    both = jnp.stack([straight.reshape(unit * times, -1), straight.transpose(1, 0, 2, 3).reshape(unit * times, -1)])
    both = both.reshape(2 * unit * times, unit * times)
    high = both.astype(BF16)
    low = (both - high.astype(F32)).astype(BF16)
    return jnp.concatenate([high, high, low], axis=1)


def panel_kernel(count, panel_each, *refs):
    msgs = refs[:count]
    swap_ref, out_ref, flag_ref, bufs, bits_v, bits_s, dense, sem = refs[count:]
    times, lanes = bufs.shape[2:]
    cells = out_ref.shape[2]
    blocks = cells // lanes
    width = min(256, cells)
    copies = [fetch(msg, bufs.at[k], sem.at[k]) for k, msg in enumerate(msgs)]
    flag = jnp.zeros((1, lanes), F32)
    for k, copy in enumerate(copies):
        copy.wait()
        read_bits(bufs.at[k], bits_v, bits_s.at[k], sem.at[count])
        flag = jnp.maximum(flag, bits_v[times - 1 : times, :].astype(F32))

        def store(i, b, tile):
            dense[pl.ds(pl.multiple_of(i * times, times), times), b * lanes : (b + 1) * lanes] = tile

        expand(bufs.at[k], bits_s.at[k], 0, panel_each, blocks, jnp.int32(1), store)

        @pl.loop(0, cells // width)
        def _(n):
            at = pl.ds(pl.multiple_of(n * width, width), width)
            turned = jnp.dot(swap_ref[...], dense[:, at], preferred_element_type=F32).astype(BF16)
            out_ref[:, k * panel_each : (k + 1) * panel_each, at] = turned.reshape(times, panel_each, width)

    flag_ref[...] = flag


def panel_rows_of(msgs, panel_each, cells):
    slots, times, lanes = msgs[0].shape
    count = len(msgs)
    size = panel_each * times
    place = jnp.arange(size, dtype=I32)
    swap = (place[None, :] == (place % panel_each * times + place // panel_each)[:, None]).astype(BF16)
    return pl.pallas_call(
        functools.partial(panel_kernel, count, panel_each),
        out_shape=(shape_of((times, count * panel_each, cells), BF16), shape_of((1, lanes), F32)),
        in_specs=[ANY] * count + [VMEM],
        out_specs=(VMEM, VMEM),
        scratch_shapes=[
            pltpu.VMEM((count, slots + 1, times, lanes), BF16),
            pltpu.VMEM((times, lanes), I32),
            pltpu.SMEM((count, times, lanes), I32),
            pltpu.VMEM((size, cells), BF16),
            pltpu.SemaphoreType.DMA((count + 1,)),
        ],
        compiler_params=params(),
        cost_estimate=cost(2 * count * size * size * cells, 8_000_000),
        name="panel_rows",
    )(*msgs, swap)


def product_kernel(turn_ref, panel_ref, out_ref):
    times = turn_ref.shape[0]
    total = None
    for t in range(times):
        part = lax.dot_general(
            turn_ref[t], panel_ref[t], (((1,), (1,)), ((), ())), preferred_element_type=F32
        )
        total = part if total is None else total + part
    out_ref[...] = total


def panel_product(turned, panel):
    times, rows, cells = turned.shape
    return pl.pallas_call(
        product_kernel,
        out_shape=shape_of((rows, panel.shape[1]), F32),
        in_specs=[VMEM, VMEM],
        out_specs=VMEM,
        compiler_params=params(16),
        cost_estimate=cost(2 * times * rows * cells * panel.shape[1], 6_000_000),
        name="panel_product",
    )(turned, panel)


def partner(value, axis, count):
    return lax.ppermute(value, axis, [(i, i ^ 1) for i in range(count)])


def shifted(value, axis, count, shift):
    return lax.ppermute(value, axis, [(i, (i + 2 * shift) % count) for i in range(count)])


def chain(value, *earlier):
    return lax.optimization_barrier((value, *earlier))[0]


def finish(parts, cells, observers, group, panel_index, error_var, obs_rows):
    half = observers // 2
    pair = parts + partner(parts, "cell", cells)
    total = pair
    for shift in range(1, cells // 2):
        total = total + shifted(pair, "cell", cells, shift)
    panel_each = panel_index.shape[0] // observers
    hi, lo = group // 2, group % 2
    column = jnp.arange(panel_index.shape[0], dtype=I32)
    step, h, j = column // (2 * panel_each), column // panel_each % 2, column % panel_each
    source = ((hi - step) % half * 2 + (lo ^ h)) * panel_each + j
    select = (source[:, None] == column[None, :]).astype(F32)
    summed = jnp.dot(total, select, precision=lax.Precision.HIGHEST, preferred_element_type=F32)
    positions = jnp.arange(obs_rows, dtype=I32)
    on_diagonal = ((group * obs_rows + positions)[:, None] == panel_index[None, :]).astype(F32)
    return summed + error_var[:, None] * on_diagonal


def dense_way(cells, observers, footprint, block_mask, own_info, time_cov, error_var, panel_index, mine):
    obs_rows, time_count, cell_local = footprint.shape
    block_local = block_mask.shape[1]
    keep = block_mask.astype(BF16)[:, None, :, None]
    feet = (
        footprint.reshape(obs_rows, time_count, block_local, cell_local // block_local) * keep
    ).reshape(obs_rows, time_count, cell_local)
    group = lax.axis_index("obs")
    panel_each = panel_index.shape[0] // observers
    column = own_info.T

    def add(carry, _):
        total, feet, info = carry
        dx = info[0][:, None] - own_info[0][None, :]
        dy = info[1][:, None] - own_info[1][None, :]
        decay = jnp.exp(-jnp.sqrt(dx * dx + dy * dy + 1.0) / LENGTH)
        cov = (decay * (info[2][:, None] * own_info[2][None, :])).astype(BF16)
        total = total + jnp.dot(feet.reshape(-1, cell_local), cov, preferred_element_type=F32)
        ring = [(i, (i + 1) % cells) for i in range(cells)]
        return (total, lax.ppermute(feet, "cell", ring), lax.ppermute(info, "cell", ring)), None

    del column
    zero = jnp.zeros((obs_rows * time_count, cell_local), F32)
    (total, _, _), _ = lax.scan(add, (zero, feet, own_info), None, length=cells)
    cov_product = jnp.einsum(
        "ts,ksc->ktc", time_cov, total.reshape(obs_rows, time_count, cell_local), precision=lax.Precision.HIGHEST
    ).astype(BF16)
    flat = cov_product.reshape(obs_rows, time_count * cell_local)

    def meet(carry, _):
        held = carry
        both = jnp.concatenate([held, partner(held, "obs", observers)], axis=0)
        part = lax.dot_general(
            flat, both.reshape(2 * panel_each, -1), (((1,), (1,)), ((), ())), preferred_element_type=F32
        )
        return shifted(held, "obs", observers, 1), part

    _, parts = lax.scan(meet, jnp.take(feet, mine, axis=0), None, length=observers // 2)
    parts = parts.transpose(1, 0, 2).reshape(obs_rows, -1)
    return cov_product, finish(parts, cells, observers, group, panel_index, error_var, obs_rows)


def body(cells, observers, footprint, block_mask, cell_coords, cell_sigma, time_cov, error_var, panel_index):
    obs_rows, time_count, cell_local = footprint.shape
    blocks = block_mask.shape[1]
    group = lax.axis_index("obs")
    panel_each = panel_index.shape[0] // observers
    mine = lax.dynamic_slice_in_dim(panel_index, group * panel_each, panel_each) - group * obs_rows
    unit = math.gcd(16, obs_rows)

    full = jnp.sum(block_mask) > slot_count(obs_rows * blocks) - 2
    panel_full = jnp.sum(jnp.take(block_mask, mine, axis=0)) > slot_count(panel_each * blocks) - 2
    over = (full | panel_full).astype(F32)
    own_info = jnp.concatenate(
        [
            cell_coords.astype(F32),
            cell_sigma[None, :],
            jnp.broadcast_to(over, (1, cell_local)),
            jnp.zeros((4, cell_local), F32),
        ],
        axis=0,
    )
    far_infos = [shifted(own_info, "cell", cells, shift) for shift in range(1, cells // 2)]
    mate_info = partner(own_info, "cell", cells)

    own_msg = pack_feet(block_mask, footprint)
    far_msgs = [shifted(own_msg, "cell", cells, shift) for shift in range(1, cells // 2)]
    mate_msg = partner(own_msg, "cell", cells)

    far_infos += [partner(info, "cell", cells) for info in far_infos]
    over = functools.reduce(jnp.maximum, [info[3, 0] for info in (own_info, mate_info, *far_infos)])
    own_panel = pack_panel(block_mask, mine, over.astype(I32)[None], footprint)
    ring = [own_panel]
    for _ in range(1, observers // 2):
        ring.append(shifted(ring[-1], "obs", observers, 1))
    messages = []
    for held in ring:
        messages += [held, partner(held, "obs", observers)]

    near = local_product(own_msg, mate_msg, own_info, mate_info, obs_rows)
    mix = mixing(time_cov, unit)
    far_cov = far_covariance(far_infos, own_info)
    far_msgs += [partner(msg, "cell", cells) for msg in far_msgs]
    cov_product, turned = far_rows(far_msgs, far_cov, near, mix, obs_rows, unit)
    panel, flags = panel_rows_of(messages, panel_each, cell_local)
    parts = panel_product(turned, panel)
    innovation = finish(parts, cells, observers, group, panel_index, error_var, obs_rows)

    def again(carry):
        return (jnp.bool_(False),) + dense_way(
            cells, observers, footprint, block_mask, own_info, time_cov, error_var, panel_index, mine
        )

    again_wanted = flags[0, 0] > 0.5
    _, cov_product, innovation = lax.while_loop(
        lambda carry: carry[0], again, (again_wanted, cov_product, innovation)
    )
    return cov_product, innovation


def solution(mesh):
    in_specs = (
        P("obs", None, "cell"),
        P("obs", "cell"),
        P(None, "cell"),
        P("cell"),
        P(),
        P("obs"),
        P(),
    )
    out_specs = (P("obs", None, "cell"), P("obs", None))
    cells, observers = mesh.shape["cell"], mesh.shape["obs"]

    def per_device(*args):
        return body(cells, observers, *args)

    return jax.shard_map(
        per_device, mesh=mesh, in_specs=in_specs, out_specs=out_specs, check_vma=False
    )
```

```python
import functools
import math

import jax
import jax.numpy as jnp
from jax import lax
from jax.experimental import pallas as pl
from jax.experimental.pallas import tpu as pltpu
from jax.sharding import PartitionSpec as P

GRID = 64
LENGTH = GRID / 16.0
F32, BF16, I32 = jnp.float32, jnp.bfloat16, jnp.int32
SHIFT = 4
INFO = 8


VMEM = pl.BlockSpec(memory_space=pltpu.VMEM)
SMEM = pl.BlockSpec(memory_space=pltpu.SMEM)
ANY = pl.BlockSpec(memory_space=pl.ANY)


def shape_of(shape, dtype):
    return jax.ShapeDtypeStruct(shape, dtype)


def params(mib):
    return pltpu.CompilerParams(vmem_limit_bytes=mib * 2**20)


def cost(micros):
    return pl.CostEstimate(flops=int(micros * 9e8), bytes_accessed=1_000_000, transcendentals=0)


def aligned(start, size):
    return pl.ds(pl.multiple_of(start, size), size)


def slot_count(tiles, extra):
    room = tiles / 2 + 4.1 * math.sqrt(tiles / 4)
    return extra + min(tiles + 1, 2 * math.ceil(room / 2) + 1)


def pack_rows(mask_at, feet_at, rows, blocks, first, buf, head_v):
    slots, times, lanes = buf.shape
    deep = -(-rows * blocks // lanes)
    row_of = lax.broadcasted_iota(I32, (8, lanes), 0)
    lane_of = lax.broadcasted_iota(I32, (8, lanes), 1)
    flat = row_of * lanes + lane_of

    def one(o, carry):
        pos, head, ends = carry
        tiles = [feet_at(o, b) for b in range(blocks)]
        for b in range(blocks):
            kept = mask_at(o, b)
            buf[jnp.minimum(pos, slots - 1)] = tiles[b]
            head = jnp.where(flat == o * blocks + b, kept * pos, head)
            pos = pos + kept
        ends = jnp.where(lane_of == o, pos, ends)
        return pos, head, ends

    zeros = jnp.zeros((8, lanes), I32)
    _, head, ends = lax.fori_loop(0, rows, one, (jnp.int32(first), zeros, zeros))
    head_v[...] = jnp.zeros_like(head_v)
    low = (1 << SHIFT) - 1
    head_v[0:deep, :] = (head >> SHIFT)[0:deep].astype(F32)
    head_v[deep : 2 * deep, :] = (head & low)[0:deep].astype(F32)
    head_v[2 * deep : 2 * deep + 1, :] = (ends >> SHIFT)[0:1].astype(F32)
    head_v[2 * deep + 1 : 2 * deep + 2, :] = (ends & low)[0:1].astype(F32)
    buf[0] = head_v[...].astype(BF16)


def pack_feet_kernel(chunks, mask_ref, coords_ref, sigma_ref, feet_ref, *rest):
    outs, (buf, head_v, sem) = rest[: len(chunks)], rest[len(chunks) :]
    rows, blocks = mask_ref.shape
    times, lanes = buf.shape[1:]
    sigma = sigma_ref[...]
    high = sigma.astype(BF16).astype(F32)
    middle = (sigma - high).astype(BF16).astype(F32)
    lowest = sigma - high - middle
    at = lax.broadcasted_iota(I32, (times, sigma.shape[1]), 0)
    info = jnp.zeros(at.shape, F32)
    for k, row in enumerate((coords_ref[0:1, :].astype(F32), coords_ref[1:2, :].astype(F32), high, middle, lowest)):
        info = jnp.where(at == k, row, info)
    info = info.astype(BF16)
    for b in range(blocks):
        buf[1 + b] = info[:, b * lanes : (b + 1) * lanes]
    pack_rows(
        lambda o, b: mask_ref[o, b],
        lambda o, b: feet_ref[o, :, b * lanes : (b + 1) * lanes],
        rows,
        blocks,
        1 + blocks,
        buf,
        head_v,
    )
    copies, first = [], 0
    for k, size in enumerate(chunks):
        copies.append(pltpu.make_async_copy(buf.at[pl.ds(first, size)], outs[k], sem.at[k]))
        first += size
    for copy in copies:
        copy.start()
    for copy in copies:
        copy.wait()


def pack_feet(mask, coords, sigma, feet, chunks):
    rows, times, cells = feet.shape
    lanes = cells // mask.shape[1]
    return pl.pallas_call(
        functools.partial(pack_feet_kernel, chunks),
        out_shape=tuple(shape_of((size, times, lanes), BF16) for size in chunks),
        in_specs=[SMEM, VMEM, VMEM, VMEM],
        out_specs=(ANY,) * len(chunks),
        scratch_shapes=[
            pltpu.VMEM((sum(chunks), times, lanes), BF16),
            pltpu.VMEM((times, lanes), F32),
            pltpu.SemaphoreType.DMA((len(chunks),)),
        ],
        compiler_params=params(12),
        cost_estimate=cost(3),
        name="pack_feet",
    )(mask, coords, sigma, feet)


def pack_panel_kernel(mask_ref, index_ref, group_ref, feet_ref, out_ref, rows_buf, head_v, sem):
    count = rows_buf.shape[0]
    blocks = mask_ref.shape[1]
    lanes = out_ref.shape[2]
    obs = mask_ref.shape[0]
    base = group_ref[0]

    def row(j):
        return jnp.clip(index_ref[base * count + j] - base * obs, 0, obs - 1)

    copies = [pltpu.make_async_copy(feet_ref.at[row(j)], rows_buf.at[j], sem.at[j]) for j in range(count)]
    for copy in copies:
        copy.start()
    for copy in copies:
        copy.wait()
    pack_rows(
        lambda o, b: mask_ref[row(o), b],
        lambda o, b: rows_buf[o, :, b * lanes : (b + 1) * lanes],
        count,
        blocks,
        1,
        out_ref,
        head_v,
    )


def pack_panel(mask, panel_index, group, feet, count, slots):
    rows, times, cells = feet.shape
    lanes = cells // mask.shape[1]
    return pl.pallas_call(
        pack_panel_kernel,
        out_shape=shape_of((slots, times, lanes), BF16),
        in_specs=[SMEM, SMEM, SMEM, ANY],
        out_specs=VMEM,
        scratch_shapes=[
            pltpu.VMEM((count, times, cells), BF16),
            pltpu.VMEM((times, lanes), F32),
            pltpu.SemaphoreType.DMA((count,)),
        ],
        compiler_params=params(8),
        cost_estimate=cost(2),
        name="pack_panel",
    )(mask, panel_index, group[None], feet)


def fetch(chunks, buf, sem):
    copies, first = [], 0
    for k, chunk in enumerate(chunks):
        copies.append(pltpu.make_async_copy(chunk, buf.at[pl.ds(first, chunk.shape[0])], sem.at[k]))
        copies[-1].start()
        first += chunk.shape[0]
    return copies


def read_head(buf, rows, blocks, bits_v):
    slots, times, lanes = buf.shape
    deep = -(-rows * blocks // lanes)
    head = buf[0].astype(F32)
    scale = float(1 << SHIFT)
    bits_v[0:deep, :] = jnp.minimum(head[0:deep] * scale + head[deep : 2 * deep], slots - 1.0).astype(I32)
    bits_v[deep : deep + 1, :] = (head[2 * deep : 2 * deep + 1] * scale + head[2 * deep + 1 : 2 * deep + 2]).astype(I32)
    buf[0] = jnp.zeros(buf.shape[1:], buf.dtype)


def copy_in(src, dst, sem):
    copy = pltpu.make_async_copy(src, dst, sem)
    copy.start()
    copy.wait()


def expand(buf, bits, first, count, blocks, store):
    lanes = buf.shape[2]
    batch = math.gcd(2, count)

    def some(i, _):
        tiles = []
        for j in range(batch):
            base = (first + i * batch + j) * blocks
            row, col = lax.div(base, lanes), lax.rem(base, lanes)
            tiles += [buf[bits[row, col + b]] for b in range(blocks)]
        for j in range(batch):
            for b in range(blocks):
                store(i * batch + j, b, tiles[j * blocks + b])
        return 0

    lax.fori_loop(0, count // batch, some, 0)


def into(dense, times, lanes, offset):
    def store(i, b, tile):
        dense[aligned(i * times, times), offset + b * lanes : offset + (b + 1) * lanes] = tile

    return store


def read_info(buf, blocks, row_v, turned):
    times, lanes = buf.shape[1:]
    for b in range(blocks):
        tile = buf[1 + b].astype(F32)[0:INFO]
        sigma = tile[2:3] + tile[3:4] + tile[4:5]
        tile = jnp.where(lax.broadcasted_iota(I32, tile.shape, 0) == 2, sigma, tile)
        at = slice(b * lanes, (b + 1) * lanes)
        if row_v is not None:
            row_v[:, at] = tile
        if turned is not None:
            turned[at, :] = tile.T


def fill_covariance(dst, dst_first, src_first, rows, turned, own):
    x, y, s = own[0:1, :], own[1:2, :], own[2:3, :]
    step = min(32, rows)
    for i in range(rows // step):
        at = aligned(src_first + i * step, step)
        dx = turned[at, 0:1] - x
        dy = turned[at, 1:2] - y
        square = dx * dx + dy * dy + 1.0
        decay = jnp.exp(square * lax.rsqrt(square) * (-1.0 / LENGTH))
        dst[aligned(dst_first + i * step, step), :] = (decay * (turned[at, 2:3] * s)).astype(BF16)


def own_kernel(chunks, *refs):
    own_msg, mate_msg = refs[:chunks], refs[chunks]
    out_ref, next_ref, info_ref, flag_ref = refs[chunks + 1 : chunks + 5]
    buf, mate_buf, bits_v, bits_s, dense, cov, turned, sem = refs[chunks + 5 :]
    slots, times, lanes = buf.shape
    cells = cov.shape[1]
    blocks = cells // lanes
    rows = dense.shape[0] // times
    tall = min(256, rows * times)
    part = cells * tall // (rows * times)
    copies = fetch(own_msg, buf, sem)
    mate = pltpu.make_async_copy(mate_msg.at[pl.ds(0, 1 + blocks)], mate_buf, sem.at[chunks])
    mate.start()
    for copy in copies:
        copy.wait()
    mate.wait()
    read_info(buf, blocks, info_ref, turned.at[0])
    read_info(mate_buf, blocks, None, turned.at[1])
    read_head(buf, rows, blocks, bits_v)
    copy_in(bits_v, bits_s, sem.at[chunks + 1])
    deep = -(-rows * blocks // lanes)
    flag_ref[0] = (bits_s[deep, rows - 1] > slots - 1).astype(I32)

    expand(buf, bits_s, 0, rows, blocks, into(dense, times, lanes, 0))

    piece = min(128, cells)

    @pl.loop(0, cells // piece)
    def _(i):
        fill_covariance(cov, i * piece, i * piece, piece, turned.at[0], info_ref)

    @pl.loop(0, rows * times // tall)
    def _(u):
        here = aligned(u * tall, tall)
        fill_covariance(next_ref, u * part, u * part, part, turned.at[1], info_ref)
        out_ref[here, :] = jnp.dot(dense[here, :], cov[...], preferred_element_type=F32)


def own_call(own_msg, mate_first, rows, cells):
    times, lanes = mate_first.shape[1:]
    slots = sum(chunk.shape[0] for chunk in own_msg)
    blocks = cells // lanes
    chunks = len(own_msg)
    return pl.pallas_call(
        functools.partial(own_kernel, chunks),
        out_shape=(
            shape_of((rows * times, cells), F32),
            shape_of((cells, cells), BF16),
            shape_of((INFO, cells), F32),
            shape_of((1,), I32),
        ),
        in_specs=[ANY] * (chunks + 1),
        out_specs=(VMEM, VMEM, VMEM, SMEM),
        scratch_shapes=[
            pltpu.VMEM((slots, times, lanes), BF16),
            pltpu.VMEM((1 + blocks, times, lanes), BF16),
            pltpu.VMEM((8, lanes), I32),
            pltpu.SMEM((8, lanes), I32),
            pltpu.VMEM((rows * times, cells), BF16),
            pltpu.VMEM((cells, cells), BF16),
            pltpu.VMEM((2, cells, INFO), F32),
            pltpu.SemaphoreType.DMA((chunks + 2,)),
        ],
        compiler_params=params(20),
        cost_estimate=cost(10),
        name="own_product",
    )(*own_msg, mate_first)


def mate_kernel(chunks, count, *refs):
    mate_msg, firsts = refs[:chunks], refs[chunks : chunks + count]
    near_ref, cov_ref, info_ref = refs[chunks + count : chunks + count + 3]
    out_ref, far_ref, flag_ref = refs[chunks + count + 3 : chunks + count + 6]
    buf, info_buf, bits_v, bits_s, dense, turned, sem = refs[chunks + count + 6 :]
    slots, times, lanes = buf.shape
    cells = cov_ref.shape[1]
    blocks = cells // lanes
    rows = dense.shape[0] // times
    tall = min(256, rows * times)
    part = count * cells * tall // (rows * times)
    copies = fetch(mate_msg, buf, sem)
    for k in range(count):
        copies.append(pltpu.make_async_copy(firsts[k].at[pl.ds(0, 1 + blocks)], info_buf.at[k], sem.at[chunks + k]))
        copies[-1].start()
    for copy in copies:
        copy.wait()
    for k in range(count):
        read_info(info_buf.at[k], blocks, None, turned.at[pl.ds(k * cells, cells)])
    read_head(buf, rows, blocks, bits_v)
    copy_in(bits_v, bits_s, sem.at[chunks + count])
    deep = -(-rows * blocks // lanes)
    flag_ref[0] = (bits_s[deep, rows - 1] > slots - 1).astype(I32)

    expand(buf, bits_s, 0, rows, blocks, into(dense, times, lanes, 0))

    @pl.loop(0, rows * times // tall)
    def _(u):
        here = aligned(u * tall, tall)
        fill_covariance(far_ref, u * part, u * part, part, turned, info_ref)
        out_ref[here, :] = near_ref[here, :] + jnp.dot(dense[here, :], cov_ref[...], preferred_element_type=F32)


def mate_call(mate_msg, firsts, near, cov, info, rows):
    times, lanes = firsts[0].shape[1:]
    cells = cov.shape[1]
    slots = sum(chunk.shape[0] for chunk in mate_msg)
    blocks = cells // lanes
    chunks, count = len(mate_msg), len(firsts)
    return pl.pallas_call(
        functools.partial(mate_kernel, chunks, count),
        out_shape=(
            shape_of((rows * times, cells), F32),
            shape_of((count * cells, cells), BF16),
            shape_of((1,), I32),
        ),
        in_specs=[ANY] * (chunks + count) + [VMEM] * 3,
        out_specs=(VMEM, VMEM, SMEM),
        scratch_shapes=[
            pltpu.VMEM((slots, times, lanes), BF16),
            pltpu.VMEM((count, 1 + blocks, times, lanes), BF16),
            pltpu.VMEM((8, lanes), I32),
            pltpu.SMEM((8, lanes), I32),
            pltpu.VMEM((rows * times, cells), BF16),
            pltpu.VMEM((count * cells, INFO), F32),
            pltpu.SemaphoreType.DMA((chunks + count + 1,)),
        ],
        input_output_aliases={chunks + count: 0},
        compiler_params=params(28),
        cost_estimate=cost(9),
        name="mate_product",
    )(*mate_msg, *firsts, near, cov, info)


def rows_kernel(count, chunks, last, unit, limit, *refs):
    msgs = [refs[k * chunks : (k + 1) * chunks] for k in range(count)]
    refs = refs[count * chunks :]
    start_ref, flags_ref, cov_ref, near_ref, mix_ref = refs[:5]
    out_ref, turn_ref, next_ref, flag_ref = refs[-12:-8]
    bufs, bits_v, bits_s, dense, stage, turn_stage, sem, out_sem = refs[-8:]
    times, lanes = bufs.shape[2:]
    cells = near_ref.shape[1]
    blocks = cells // lanes
    rows = stage.shape[0]
    deep = -(-rows * blocks // lanes)
    copies = []
    for k in range(count):
        copies += fetch(msgs[k], bufs.at[k], sem.at[k])
    for copy in copies:
        copy.wait()
    for k in range(count):
        read_head(bufs.at[k], rows, blocks, bits_v.at[k])
    copy_in(bits_v, bits_s, sem.at[count, 0])
    first = start_ref[0]
    if last:
        ready = jnp.int32(rows // unit)
    else:
        ready = jnp.int32(0)
        for u in range(rows // unit):
            whole = jnp.int32(1)
            for k in range(count):
                whole = whole * (bits_s[k, deep, (u + 1) * unit - 1] <= limit).astype(I32)
            ready = ready + whole
    over = flags_ref[0] + flags_ref[1]
    for k in range(count):
        over = over + (bits_s[k, deep, rows - 1] > bufs.shape[1] - 1).astype(I32)
    flag_ref[0] = over
    next_ref[0] = ready

    def outgoing(u):
        at = aligned(u * unit, unit)
        return (
            pltpu.make_async_copy(stage.at[at], out_ref.at[at], out_sem.at[0, u]),
            pltpu.make_async_copy(turn_stage.at[:, at], turn_ref.at[:, at], out_sem.at[1, u]),
        )

    def step(u, _):
        for k in range(count):
            expand(bufs.at[k], bits_s.at[k], u * unit, unit, blocks, into(dense, times, lanes, k * cells))
        here = aligned(u * unit * times, unit * times)
        value = near_ref[here, :] + jnp.dot(dense[...], cov_ref[...], preferred_element_type=F32)
        high = value.astype(BF16)
        low = (value - high.astype(F32)).astype(BF16)
        mixed = jnp.dot(
            mix_ref[...], jnp.concatenate([high, low, high], axis=0), preferred_element_type=F32
        ).astype(BF16)
        at = aligned(u * unit, unit)
        stage[at] = mixed[: unit * times].reshape(unit, times, cells)
        turn_stage[:, at, :] = mixed[unit * times :].reshape(times, unit, cells)
        for copy in outgoing(u):
            copy.start()
        return 0

    lax.fori_loop(first, ready, step, 0)

    def settle(u, _):
        for copy in outgoing(u):
            copy.wait()
        return 0

    lax.fori_loop(first, ready, settle, 0)


def rows_call(msgs, start, flags, cov, near, mix, rows, unit, slots, carried):
    times, lanes = msgs[0][0].shape[1:]
    cells = near.shape[1]
    count, chunks = len(msgs), len(msgs[0])
    last = carried is not None
    limit = sum(chunk.shape[0] for chunk in msgs[0])
    flat = [chunk for msg in msgs for chunk in msg]
    base = len(flat) + 5
    return pl.pallas_call(
        functools.partial(rows_kernel, count, chunks, last, unit, limit),
        out_shape=(
            shape_of((rows, times, cells), BF16),
            shape_of((times, rows, cells), BF16),
            shape_of((1,), I32),
            shape_of((1,), I32),
        ),
        in_specs=[ANY] * len(flat) + [SMEM, SMEM] + [VMEM] * 3 + ([ANY, ANY] if last else []),
        out_specs=(ANY, ANY, SMEM, SMEM),
        scratch_shapes=[
            pltpu.VMEM((count, slots, times, lanes), BF16),
            pltpu.VMEM((count, 8, lanes), I32),
            pltpu.SMEM((count, 8, lanes), I32),
            pltpu.VMEM((unit * times, count * cells), BF16),
            pltpu.VMEM((rows, times, cells), BF16),
            pltpu.VMEM((times, rows, cells), BF16),
            pltpu.SemaphoreType.DMA((count + 1, chunks)),
            pltpu.SemaphoreType.DMA((2, rows // unit)),
        ],
        input_output_aliases={base: 0, base + 1: 1} if last else {},
        compiler_params=params(28),
        cost_estimate=cost(5),
        name="last_rows" if last else "first_rows",
    )(*flat, start, flags, cov, near, mix, *(carried or ()))


def mix_kernel(unit, time_ref, out_ref):
    times = time_ref.shape[0]
    size = unit * times
    value = time_ref[...]
    high = value.astype(BF16)
    low = (value - high.astype(F32)).astype(BF16)

    def pick(shape, index, dim):
        return (index == lax.broadcasted_iota(I32, shape, dim)).astype(F32).astype(BF16)

    tall = lax.broadcasted_iota(I32, (size, times), 0)
    wide = lax.broadcasted_iota(I32, (times, size), 1)
    row = lax.broadcasted_iota(I32, (size, size), 0)
    col = lax.broadcasted_iota(I32, (size, size), 1)
    right = pick((times, size), wide % times, 0)
    for k in range(2):
        left = pick((size, times), tall % times if k == 0 else tall // unit, 1)
        same = (row // times if k == 0 else row % unit) == col // times
        for j, part in enumerate((high, high, low)):
            spread = jnp.dot(left, part, preferred_element_type=F32).astype(BF16)
            spread = jnp.dot(spread, right, preferred_element_type=F32)
            out_ref[k * size : (k + 1) * size, j * size : (j + 1) * size] = jnp.where(same, spread, 0.0).astype(BF16)


def mixing(time_cov, unit):
    size = unit * time_cov.shape[0]
    return pl.pallas_call(
        functools.partial(mix_kernel, unit),
        out_shape=shape_of((2 * size, 3 * size), BF16),
        in_specs=[VMEM],
        out_specs=VMEM,
        compiler_params=params(8),
        cost_estimate=cost(1),
        name="mixing",
    )(time_cov)


def panel_kernel(count, panel_each, *refs):
    msgs = refs[:count]
    out_ref, flag_ref, bufs, bits_v, bits_s, dense, sem = refs[count:]
    slots, times, lanes = bufs.shape[1:]
    cells = out_ref.shape[2]
    blocks = cells // lanes
    deep = -(-panel_each * blocks // lanes)
    size = panel_each * times
    row = lax.broadcasted_iota(I32, (size, size), 0)
    swap = (lax.broadcasted_iota(I32, (size, size), 1) == row % panel_each * times + row // panel_each)
    swap = swap.astype(F32).astype(BF16)
    copies = [pltpu.make_async_copy(msg, bufs.at[k], sem.at[k]) for k, msg in enumerate(msgs)]
    for copy in copies:
        copy.start()
    for k, copy in enumerate(copies):
        copy.wait()
        read_head(bufs.at[k], panel_each, blocks, bits_v.at[k])
    copy_in(bits_v, bits_s, sem.at[count])
    over = jnp.int32(0)
    for k in range(count):
        over = over + (bits_s[k, deep, panel_each - 1] > slots - 1).astype(I32)
        expand(bufs.at[k], bits_s.at[k], 0, panel_each, blocks, into(dense, times, lanes, 0))
        turned = jnp.dot(swap, dense[...], preferred_element_type=F32).astype(BF16)
        out_ref[:, k * panel_each : (k + 1) * panel_each, :] = turned.reshape(times, panel_each, cells)
    flag_ref[0] = over


def panel_rows_of(msgs, panel_each, cells):
    slots, times, lanes = msgs[0].shape
    count = len(msgs)
    return pl.pallas_call(
        functools.partial(panel_kernel, count, panel_each),
        out_shape=(shape_of((times, count * panel_each, cells), BF16), shape_of((1,), I32)),
        in_specs=[ANY] * count,
        out_specs=(VMEM, SMEM),
        scratch_shapes=[
            pltpu.VMEM((count, slots, times, lanes), BF16),
            pltpu.VMEM((count, 8, lanes), I32),
            pltpu.SMEM((count, 8, lanes), I32),
            pltpu.VMEM((panel_each * times, cells), BF16),
            pltpu.SemaphoreType.DMA((count + 1,)),
        ],
        compiler_params=params(12),
        cost_estimate=cost(4),
        name="panel_rows",
    )(*msgs)


def product_kernel(sources_ref, turn_ref, *refs):
    panels, out_ref = refs[:-1], refs[-1]
    times, rows = turn_ref.shape[:2]
    pieces = []
    for panel_ref in panels:
        total = None
        for t in range(times):
            part = lax.dot_general(
                turn_ref[t], panel_ref[t], (((1,), (1,)), ((), ())), preferred_element_type=F32
            )
            total = part if total is None else total + part
        pieces.append(total)
    value = jnp.concatenate(pieces, axis=1) if len(pieces) > 1 else pieces[0]
    width = value.shape[1]
    count = sources_ref.shape[0]
    each = width // count
    row = lax.broadcasted_iota(I32, (width, width), 0)
    col = lax.broadcasted_iota(I32, (width, width), 1)
    target = jnp.zeros((width, width), I32)
    for k in range(count):
        target = jnp.where(row // each == k, sources_ref[k] * each + row % each, target)
    select = (col == target).astype(F32).astype(BF16)
    total = jnp.zeros(value.shape, F32)
    for _ in range(3):
        part = value.astype(BF16)
        total = total + jnp.dot(part, select, preferred_element_type=F32)
        value = value - part.astype(F32)
    out_ref[...] = total


def panel_product(sources, turned, panels):
    times, rows, cells = turned.shape
    width = sum(panel.shape[1] for panel in panels)
    return pl.pallas_call(
        product_kernel,
        out_shape=shape_of((rows, width), F32),
        in_specs=[SMEM] + [VMEM] * (1 + len(panels)),
        out_specs=VMEM,
        compiler_params=params(12),
        cost_estimate=cost(2),
        name="panel_product",
    )(sources, turned, *panels)


def partner(value, axis, count):
    return lax.ppermute(value, axis, [(i, i ^ 1) for i in range(count)])


def shifted(value, axis, count, shift, flip=0):
    return lax.ppermute(value, axis, [(i, ((i + 2 * shift) % count) ^ flip) for i in range(count)])


def dense_rows(cells, footprints, info, time_cov):
    obs_rows, time_count, cell_local = footprints.shape
    own = info

    def add(carry, _):
        total, feet, info = carry
        dx = info[0][:, None] - own[0][None, :]
        dy = info[1][:, None] - own[1][None, :]
        decay = jnp.exp(-jnp.sqrt(dx * dx + dy * dy + 1.0) / LENGTH)
        cov = (decay * (info[2][:, None] * own[2][None, :])).astype(BF16)
        total = total + jnp.dot(feet.reshape(-1, cell_local), cov, preferred_element_type=F32)
        ring = [(i, (i + 1) % cells) for i in range(cells)]
        return (total, lax.ppermute(feet, "cell", ring), lax.ppermute(info, "cell", ring)), None

    zero = jnp.zeros((obs_rows * time_count, cell_local), F32)
    (total, _, _), _ = lax.scan(add, (zero, footprints, info), None, length=cells)
    mixed = jnp.einsum(
        "ts,ksc->ktc", time_cov, total.reshape(obs_rows, time_count, cell_local), precision=lax.Precision.HIGHEST
    ).astype(BF16)
    return mixed, mixed.transpose(1, 0, 2)


def dense_panel(observers, own_rows):
    def meet(held, _):
        both = jnp.concatenate([held, partner(held, "obs", observers)], axis=0)
        return shifted(held, "obs", observers, 1), both.transpose(1, 0, 2)

    _, pieces = lax.scan(meet, own_rows, None, length=observers // 2)
    return pieces.transpose(1, 0, 2, 3).reshape(pieces.shape[1], -1, pieces.shape[3])


def body(cells, observers, footprint, block_mask, cell_coords, cell_sigma, time_cov, error_var, panel_index):
    obs_rows, times, cell_local = footprint.shape
    blocks = block_mask.shape[1]
    lanes = cell_local // blocks
    group = lax.axis_index("obs")
    panel_each = panel_index.shape[0] // observers
    half = observers // 2
    unit = math.gcd(16, obs_rows)
    slots = slot_count(obs_rows * blocks, 1 + blocks)
    chunks = (slots - slots // 2, slots // 2)

    own_panel = pack_panel(
        block_mask, panel_index, group, footprint, panel_each, slot_count(panel_each * blocks, 1)
    )
    own_msg = pack_feet(block_mask, cell_coords, cell_sigma[None, :], footprint, chunks)
    far_msgs = [[shifted(c, "cell", cells, shift) for c in own_msg] for shift in range(1, cells // 2)]
    mate_msg = [partner(c, "cell", cells) for c in own_msg]
    ring = [own_panel]
    for _ in range(1, half):
        ring.append(shifted(ring[-1], "obs", observers, 1))
    messages = []
    for held in ring:
        messages += [held, partner(held, "obs", observers)]
    far_msgs += [[partner(c, "cell", cells) for c in msg] for msg in far_msgs]

    near, mate_cov, info, own_flag = own_call(own_msg, mate_msg[0], obs_rows, cell_local)
    near, far_cov, mate_flag = mate_call(mate_msg, [msg[0] for msg in far_msgs], near, mate_cov, info, obs_rows)
    mix = mixing(time_cov, unit)
    flags = jnp.concatenate([own_flag, mate_flag])
    zero = jnp.zeros((1,), I32)
    cov_product, turned, start, _ = rows_call(
        [msg[:1] for msg in far_msgs], zero, flags, far_cov, near, mix, obs_rows, unit, slots, None
    )
    cov_product, turned, _, full = rows_call(
        far_msgs, start, flags, far_cov, near, mix, obs_rows, unit, slots, (cov_product, turned)
    )
    cut = len(messages) // 2
    first_panel, first_full = panel_rows_of(messages[:cut], panel_each, cell_local)
    last_panel, last_full = panel_rows_of(messages[cut:], panel_each, cell_local)

    def kept_footprints():
        keep = block_mask.astype(BF16)[:, None, :, None]
        return (footprint.reshape(obs_rows, times, blocks, lanes) * keep).reshape(footprint.shape)

    def rows_again(carry):
        return (jnp.bool_(False),) + dense_rows(cells, kept_footprints(), info, time_cov)

    _, cov_product, turned = lax.while_loop(lambda c: c[0], rows_again, (full[0] > 0, cov_product, turned))

    def panel_again(carry):
        mine = lax.dynamic_slice_in_dim(panel_index, group * panel_each, panel_each) - group * obs_rows
        panel = dense_panel(observers, jnp.take(kept_footprints(), mine, axis=0))
        split = cut * panel_each
        return jnp.bool_(False), panel[:, :split], panel[:, split:]

    _, first_panel, last_panel = lax.while_loop(
        lambda c: c[0], panel_again, ((first_full[0] + last_full[0]) > 0, first_panel, last_panel)
    )

    hi, lo = group // 2, group % 2
    order = jnp.arange(observers, dtype=I32)
    sources = (hi - order // 2) % half * 2 + (lo ^ (order % 2))
    part = panel_product(sources, turned, (first_panel, last_panel))
    total = part
    for shift in range(cells // 2):
        for flip in range(2):
            if shift or flip:
                total = total + shifted(part, "cell", cells, shift, flip)
    positions = jnp.arange(obs_rows, dtype=I32)
    on_diagonal = ((group * obs_rows + positions)[:, None] == panel_index[None, :]).astype(F32)
    return cov_product, total + error_var[:, None] * on_diagonal


def solution(mesh):
    in_specs = (
        P("obs", None, "cell"),
        P("obs", "cell"),
        P(None, "cell"),
        P("cell"),
        P(),
        P("obs"),
        P(),
    )
    out_specs = (P("obs", None, "cell"), P("obs", None))
    cells, observers = mesh.shape["cell"], mesh.shape["obs"]

    def per_device(*args):
        return body(cells, observers, *args)

    return jax.shard_map(
        per_device, mesh=mesh, in_specs=in_specs, out_specs=out_specs, check_vma=False
    )
```

```python
import functools
import math

import jax
import jax.numpy as jnp
from jax import lax
from jax.experimental import pallas as pl
from jax.experimental.pallas import tpu as pltpu
from jax.sharding import PartitionSpec as P

GRID = 64
LENGTH = GRID / 16.0
F32, BF16, I32 = jnp.float32, jnp.bfloat16, jnp.int32
SHIFT = 4
INFO = 8


VMEM = pl.BlockSpec(memory_space=pltpu.VMEM)
SMEM = pl.BlockSpec(memory_space=pltpu.SMEM)
ANY = pl.BlockSpec(memory_space=pl.ANY)


def shape_of(shape, dtype):
    return jax.ShapeDtypeStruct(shape, dtype)


def params(mib):
    return pltpu.CompilerParams(vmem_limit_bytes=mib * 2**20)


def cost(micros):
    return pl.CostEstimate(flops=int(micros * 9e8), bytes_accessed=1_000_000, transcendentals=0)


def aligned(start, size):
    return pl.ds(pl.multiple_of(start, size), size)


def slot_count(tiles, extra):
    room = tiles / 2 + 4.1 * math.sqrt(tiles / 4)
    return extra + min(tiles + 1, 2 * math.ceil(room / 2) + 1)


def pack_rows(mask_at, feet_at, begin, end, blocks, buf, carry):
    slots, times, lanes = buf.shape
    row_of = lax.broadcasted_iota(I32, (8, lanes), 0)
    lane_of = lax.broadcasted_iota(I32, (8, lanes), 1)
    flat = row_of * lanes + lane_of
    batch = math.gcd(2, end - begin)

    def some(i, carry):
        pos, head, ends = carry
        first = begin + i * batch
        tiles = [[feet_at(first + j, b) for b in range(blocks)] for j in range(batch)]
        kept = [[mask_at(first + j, b) for b in range(blocks)] for j in range(batch)]
        for j in range(batch):
            for b in range(blocks):
                buf[jnp.minimum(pos, slots - 1)] = tiles[j][b]
                head = jnp.where(flat == (first + j) * blocks + b, kept[j][b] * pos, head)
                pos = pos + kept[j][b]
            ends = jnp.where(lane_of == first + j, pos, ends)
        return pos, head, ends

    return lax.fori_loop(0, (end - begin) // batch, some, carry)


def no_rows(first, lanes):
    zeros = jnp.zeros((8, lanes), I32)
    return jnp.int32(first), zeros, zeros


def write_head(carry, rows, blocks, buf, head_v, flag=None):
    lanes = buf.shape[2]
    deep = -(-rows * blocks // lanes)
    _, head, ends = carry
    low = (1 << SHIFT) - 1
    head_v[...] = jnp.zeros_like(head_v)
    head_v[0:deep, :] = (head >> SHIFT)[0:deep].astype(F32)
    head_v[deep : 2 * deep, :] = (head & low)[0:deep].astype(F32)
    head_v[2 * deep : 2 * deep + 1, :] = (ends >> SHIFT)[0:1].astype(F32)
    head_v[2 * deep + 1 : 2 * deep + 2, :] = (ends & low)[0:1].astype(F32)
    if flag is not None:
        head_v[2 * deep + 2 : 2 * deep + 3, :] = jnp.broadcast_to(flag, (1, lanes)).astype(F32)
    buf[0] = head_v[...].astype(BF16)


def pack_feet_kernel(chunks, mask_ref, coords_ref, sigma_ref, feet_ref, *rest):
    outs, (flag_ref, feet, buf, head_v, in_sem, sem) = rest[: len(chunks)], rest[len(chunks) :]
    blocks, rows = mask_ref.shape
    times, lanes = buf.shape[1:]
    groups = in_sem.shape[0]
    each = rows // groups
    loads = [
        pltpu.make_async_copy(feet_ref.at[pl.ds(g * each, each)], feet.at[pl.ds(g * each, each)], in_sem.at[g])
        for g in range(groups)
    ]
    for load in loads:
        load.start()
    sigma = sigma_ref[...]
    high = sigma.astype(BF16).astype(F32)
    middle = (sigma - high).astype(BF16).astype(F32)
    lowest = sigma - high - middle
    at = lax.broadcasted_iota(I32, (times, sigma.shape[1]), 0)
    info = jnp.zeros(at.shape, F32)
    for k, row in enumerate((coords_ref[0:1, :].astype(F32), coords_ref[1:2, :].astype(F32), high, middle, lowest)):
        info = jnp.where(at == k, row, info)
    info = info.astype(BF16)
    for b in range(blocks):
        buf[1 + b] = info[:, b * lanes : (b + 1) * lanes]
    carry = no_rows(1 + blocks, lanes)
    for g in range(groups):
        loads[g].wait()
        carry = pack_rows(
            lambda o, b: mask_ref[b, o],
            lambda o, b: feet[o, :, b * lanes : (b + 1) * lanes],
            g * each,
            (g + 1) * each,
            blocks,
            buf,
            carry,
        )
    write_head(carry, rows, blocks, buf, head_v)
    flag_ref[0] = (carry[0] > buf.shape[0] - 1).astype(I32)
    copies, first = [], 0
    for k, size in enumerate(chunks):
        copies.append(pltpu.make_async_copy(buf.at[pl.ds(first, size)], outs[k], sem.at[k]))
        first += size
    for copy in copies:
        copy.start()
    for copy in copies:
        copy.wait()


def pack_feet(mask, coords, sigma, feet, chunks):
    rows, times, cells = feet.shape
    lanes = cells // mask.shape[0]
    groups = math.gcd(4, rows)
    return pl.pallas_call(
        functools.partial(pack_feet_kernel, chunks),
        out_shape=tuple(shape_of((size, times, lanes), BF16) for size in chunks) + (shape_of((1,), I32),),
        in_specs=[SMEM, VMEM, VMEM, ANY],
        out_specs=(ANY,) * len(chunks) + (SMEM,),
        scratch_shapes=[
            pltpu.VMEM((rows, times, cells), BF16),
            pltpu.VMEM((sum(chunks), times, lanes), BF16),
            pltpu.VMEM((times, lanes), F32),
            pltpu.SemaphoreType.DMA((groups,)),
            pltpu.SemaphoreType.DMA((len(chunks),)),
        ],
        compiler_params=params(12),
        cost_estimate=cost(3),
        name="pack_feet",
    )(mask, coords, sigma, feet)


def pack_panel_kernel(mask_ref, index_ref, group_ref, flag_ref, feet_ref, out_ref, rows_buf, head_v, sem):
    count = rows_buf.shape[0]
    blocks, obs = mask_ref.shape
    lanes = out_ref.shape[2]
    base = group_ref[0]
    rows = [jnp.clip(index_ref[base * count + j] - base * obs, 0, obs - 1) for j in range(count)]
    copies = [pltpu.make_async_copy(feet_ref.at[rows[j]], rows_buf.at[j], sem.at[j]) for j in range(count)]
    for copy in copies:
        copy.start()
    for copy in copies:
        copy.wait()

    def mask_at(o, b):
        return mask_ref[b, jnp.clip(index_ref[base * count + o] - base * obs, 0, obs - 1)]

    carry = pack_rows(
        mask_at, lambda o, b: rows_buf[o, :, b * lanes : (b + 1) * lanes], 0, count, blocks, out_ref, no_rows(1, lanes)
    )
    write_head(carry, count, blocks, out_ref, head_v, flag_ref[0])


def pack_panel(mask, panel_index, group, flag, feet, count, slots):
    rows, times, cells = feet.shape
    lanes = cells // mask.shape[0]
    return pl.pallas_call(
        pack_panel_kernel,
        out_shape=shape_of((slots, times, lanes), BF16),
        in_specs=[SMEM, SMEM, SMEM, SMEM, ANY],
        out_specs=VMEM,
        scratch_shapes=[
            pltpu.VMEM((count, times, cells), BF16),
            pltpu.VMEM((times, lanes), F32),
            pltpu.SemaphoreType.DMA((count,)),
        ],
        compiler_params=params(8),
        cost_estimate=cost(2),
        name="pack_panel",
    )(mask, panel_index, group[None], flag, feet)


def fetch(chunks, buf, sem):
    copies, first = [], 0
    for k, chunk in enumerate(chunks):
        copies.append(pltpu.make_async_copy(chunk, buf.at[pl.ds(first, chunk.shape[0])], sem.at[k]))
        copies[-1].start()
        first += chunk.shape[0]
    return copies


def read_head(buf, rows, blocks, bits_v, flagged=False):
    slots, times, lanes = buf.shape
    deep = -(-rows * blocks // lanes)
    head = buf[0].astype(F32)
    scale = float(1 << SHIFT)
    bits_v[0:deep, :] = jnp.minimum(head[0:deep] * scale + head[deep : 2 * deep], slots - 1.0).astype(I32)
    bits_v[deep : deep + 1, :] = (head[2 * deep : 2 * deep + 1] * scale + head[2 * deep + 1 : 2 * deep + 2]).astype(I32)
    if flagged:
        bits_v[deep + 1 : deep + 2, :] = head[2 * deep + 2 : 2 * deep + 3].astype(I32)
    buf[0] = jnp.zeros(buf.shape[1:], buf.dtype)


def copy_in(src, dst, sem):
    copy = pltpu.make_async_copy(src, dst, sem)
    copy.start()
    copy.wait()


def expand(buf, bits, first, count, blocks, store, unrolled=False):
    lanes = buf.shape[2]
    batch = math.gcd(2, count)

    def some(i, _):
        tiles = []
        for j in range(batch):
            base = (first + i * batch + j) * blocks
            row, col = lax.div(base, lanes), lax.rem(base, lanes)
            tiles += [buf[bits[row, col + b]] for b in range(blocks)]
        for j in range(batch):
            for b in range(blocks):
                store(i * batch + j, b, tiles[j * blocks + b])
        return 0

    if unrolled:
        for i in range(count // batch):
            some(i, 0)
    else:
        lax.fori_loop(0, count // batch, some, 0)


def into(dense, times, lanes, offset, first=0):
    def store(i, b, tile):
        at = aligned((first + i) * times, times)
        dense[at, offset + b * lanes : offset + (b + 1) * lanes] = tile.astype(dense.dtype)

    return store


def read_info(buf, blocks, row_v, turned):
    times, lanes = buf.shape[1:]
    for b in range(blocks):
        tile = buf[1 + b].astype(F32)[0:INFO]
        sigma = tile[2:3] + tile[3:4] + tile[4:5]
        tile = jnp.where(lax.broadcasted_iota(I32, tile.shape, 0) == 2, sigma, tile)
        at = slice(b * lanes, (b + 1) * lanes)
        if row_v is not None:
            row_v[:, at] = tile
        if turned is not None:
            turned[at, :] = tile.T


def fill_covariance(dst, dst_first, src_first, rows, turned, own):
    x, y, s = own[0:1, :], own[1:2, :], own[2:3, :]
    step = min(32, rows)
    for i in range(rows // step):
        at = aligned(src_first + i * step, step)
        dx = turned[at, 0:1] - x
        dy = turned[at, 1:2] - y
        square = dx * dx + dy * dy + 1.0
        decay = jnp.exp(square * lax.rsqrt(square) * (-1.0 / LENGTH))
        dst[aligned(dst_first + i * step, step), :] = (decay * (turned[at, 2:3] * s)).astype(BF16)


def own_kernel(chunks, *refs):
    msgs = refs[:chunks], refs[chunks : 2 * chunks]
    out_ref, mate_dense, next_ref, info_ref = refs[2 * chunks : 2 * chunks + 4]
    bufs, bits_v, bits_s, dense, cov, turned, sem = refs[2 * chunks + 4 :]
    times, lanes = bufs.shape[2:]
    cells = cov.shape[1]
    blocks = cells // lanes
    rows = dense.shape[0] // times
    tall = min(256, rows * times)
    steps = rows * times // tall
    part = cells // steps
    copies = [fetch(msg, bufs.at[k], sem.at[k]) for k, msg in enumerate(msgs)]
    for k in range(2):
        for copy in copies[k]:
            copy.wait()
        read_info(bufs.at[k], blocks, None if k else info_ref, turned.at[k])
        read_head(bufs.at[k], rows, blocks, bits_v.at[k])
    copy_in(bits_v, bits_s, sem.at[2, 0])
    fine = math.gcd(8, rows // 2)
    piece = cells // fine

    @pl.loop(0, fine)
    def _(i):
        fill_covariance(cov, i * piece, i * piece, piece, turned.at[0], info_ref)
        some = rows // fine
        expand(bufs.at[0], bits_s.at[0], i * some, some, blocks, into(dense, times, lanes, 0, i * some), unrolled=True)

    @pl.loop(0, steps)
    def _(u):
        here = aligned(u * tall, tall)
        fill_covariance(next_ref, u * part, u * part, part, turned.at[1], info_ref)
        out_ref[here, :] = jnp.dot(dense[here, :], cov[...], preferred_element_type=F32)
        some = rows // steps
        expand(bufs.at[1], bits_s.at[1], u * some, some, blocks, into(mate_dense, times, lanes, 0, u * some))


def own_call(own_msg, mate_msg, rows, cells):
    times, lanes = own_msg[0].shape[1:]
    slots = sum(chunk.shape[0] for chunk in own_msg)
    chunks = len(own_msg)
    return pl.pallas_call(
        functools.partial(own_kernel, chunks),
        out_shape=(
            shape_of((rows * times, cells), F32),
            shape_of((rows * times, cells), BF16),
            shape_of((cells, cells), BF16),
            shape_of((INFO, cells), F32),
        ),
        in_specs=[ANY] * (2 * chunks),
        out_specs=(VMEM,) * 4,
        scratch_shapes=[
            pltpu.VMEM((2, slots, times, lanes), BF16),
            pltpu.VMEM((2, 8, lanes), I32),
            pltpu.SMEM((2, 8, lanes), I32),
            pltpu.VMEM((rows * times, cells), BF16),
            pltpu.VMEM((cells, cells), BF16),
            pltpu.VMEM((2, cells, INFO), F32),
            pltpu.SemaphoreType.DMA((3, chunks)),
        ],
        compiler_params=params(24),
        cost_estimate=cost(9),
        name="own_product",
    )(*own_msg, *mate_msg)


def mate_kernel(count, *refs):
    firsts = refs[:count]
    near_ref, dense, cov_ref, info_ref, out_ref, far_ref, info_buf, turned, sem = refs[count:]
    times, lanes = info_buf.shape[2:]
    cells = cov_ref.shape[1]
    blocks = cells // lanes
    tall = min(256, dense.shape[0])
    steps = dense.shape[0] // tall
    part = count * cells // steps
    copies = []
    for k in range(count):
        copies.append(pltpu.make_async_copy(firsts[k].at[pl.ds(0, 1 + blocks)], info_buf.at[k], sem.at[k]))
        copies[-1].start()
    for k in range(count):
        copies[k].wait()
        read_info(info_buf.at[k], blocks, None, turned.at[pl.ds(k * cells, cells)])

    @pl.loop(0, steps)
    def _(u):
        here = aligned(u * tall, tall)
        fill_covariance(far_ref, u * part, u * part, part, turned, info_ref)
        out_ref[here, :] = near_ref[here, :] + jnp.dot(dense[here, :], cov_ref[...], preferred_element_type=F32)


def mate_call(firsts, near, mate_dense, cov, info):
    times, lanes = firsts[0].shape[1:]
    cells = cov.shape[1]
    blocks = cells // lanes
    count = len(firsts)
    return pl.pallas_call(
        functools.partial(mate_kernel, count),
        out_shape=(shape_of(near.shape, F32), shape_of((count * cells, cells), BF16)),
        in_specs=[ANY] * count + [VMEM] * 4,
        out_specs=(VMEM, VMEM),
        scratch_shapes=[
            pltpu.VMEM((count, 1 + blocks, times, lanes), BF16),
            pltpu.VMEM((count * cells, INFO), F32),
            pltpu.SemaphoreType.DMA((count,)),
        ],
        input_output_aliases={count: 0},
        compiler_params=params(24),
        cost_estimate=cost(8),
        name="mate_product",
    )(*firsts, near, mate_dense, cov, info)


def mixed_unit(mix_ref, value):
    high = value.astype(BF16)
    low = (value - high.astype(F32)).astype(BF16)
    stacked = jnp.concatenate([high, low, high], axis=0)
    return jnp.dot(mix_ref[...], stacked, preferred_element_type=F32).astype(BF16)


def first_kernel(count, chunks, unit, *refs):
    msgs = [refs[k * chunks : (k + 1) * chunks] for k in range(count)]
    cov_ref, near_ref, mix_ref, out_ref, next_ref, bufs, bits_v, bits_s, dense, sem = refs[count * chunks :]
    times, lanes = bufs.shape[2:]
    cells = near_ref.shape[1]
    blocks = cells // lanes
    rows = out_ref.shape[0]
    deep = -(-rows * blocks // lanes)
    limit = sum(chunk.shape[0] for chunk in msgs[0])
    copies = [fetch(msgs[k], bufs.at[k], sem.at[k]) for k in range(count)]
    for k in range(count):
        for copy in copies[k]:
            copy.wait()
        read_head(bufs.at[k], rows, blocks, bits_v.at[k])
    copy_in(bits_v, bits_s, sem.at[count, 0])
    ready = jnp.int32(0)
    for u in range(rows // unit):
        whole = jnp.int32(1)
        for k in range(count):
            whole = whole * (bits_s[k, deep, (u + 1) * unit - 1] <= limit).astype(I32)
        ready = ready + whole
    next_ref[0] = ready

    def step(u, _):
        for k in range(count):
            expand(bufs.at[k], bits_s.at[k], u * unit, unit, blocks, into(dense, times, lanes, k * cells))
        here = aligned(u * unit * times, unit * times)
        value = near_ref[here, :] + jnp.dot(dense[...], cov_ref[...], preferred_element_type=F32)
        out_ref[aligned(u * unit, unit)] = mixed_unit(mix_ref, value).reshape(unit, times, cells)
        return 0

    lax.fori_loop(0, ready, step, 0)


def first_rows(msgs, cov, near, mix, rows, unit, slots):
    times, lanes = msgs[0][0].shape[1:]
    cells = near.shape[1]
    count, chunks = len(msgs), len(msgs[0])
    flat = [chunk for msg in msgs for chunk in msg]
    return pl.pallas_call(
        functools.partial(first_kernel, count, chunks, unit),
        out_shape=(shape_of((rows, times, cells), BF16), shape_of((1,), I32)),
        in_specs=[ANY] * len(flat) + [VMEM] * 3,
        out_specs=(VMEM, SMEM),
        scratch_shapes=[
            pltpu.VMEM((count, slots, times, lanes), BF16),
            pltpu.VMEM((count, 8, lanes), I32),
            pltpu.SMEM((count, 8, lanes), I32),
            pltpu.VMEM((unit * times, count * cells), BF16),
            pltpu.SemaphoreType.DMA((count + 1, chunks)),
        ],
        compiler_params=params(20),
        cost_estimate=cost(6),
        name="first_rows",
    )(*flat, cov, near, mix)


def last_kernel(count, chunks, pieces, unit, each, *refs):
    msgs = [refs[k * chunks : (k + 1) * chunks] for k in range(count)]
    panel_msgs = refs[count * chunks : count * chunks + pieces]
    refs = refs[count * chunks + pieces :]
    start_ref, sources_ref, cov_ref, near_ref, mix_ref, _, out_ref, part_ref = refs[:8]
    bufs, panel_bufs, bits_v, bits_s, dense, wide, panel, sem, panel_sem = refs[8:]
    times, lanes = bufs.shape[2:]
    cells = near_ref.shape[1]
    blocks = cells // lanes
    rows = out_ref.shape[0]
    copies = [fetch(msgs[k], bufs.at[k], sem.at[k]) for k in range(count)]
    panel_copies = [
        pltpu.make_async_copy(panel_msgs[k], panel_bufs.at[k], panel_sem.at[k]) for k in range(pieces)
    ]
    for copy in panel_copies:
        copy.start()
    for k in range(count):
        for copy in copies[k]:
            copy.wait()
        read_head(bufs.at[k], rows, blocks, bits_v.at[k])
    for k in range(pieces):
        panel_copies[k].wait()
        read_head(panel_bufs.at[k], each, blocks, bits_v.at[count + k], flagged=True)
    copy_in(bits_v, bits_s, sem.at[count, 0])
    first = start_ref[0]

    def step(u, _):
        for k in range(count):
            expand(bufs.at[k], bits_s.at[k], u * unit, unit, blocks, into(dense, times, lanes, k * cells))
        here = aligned(u * unit * times, unit * times)
        value = near_ref[here, :] + jnp.dot(dense[...], cov_ref[...], preferred_element_type=F32)
        mixed = mixed_unit(mix_ref, value)
        out_ref[aligned(u * unit, unit)] = mixed.reshape(unit, times, cells)
        for b in range(blocks):
            wide[b, here, :] = mixed[:, b * lanes : (b + 1) * lanes].astype(F32)
        return 0

    lax.fori_loop(first, rows // unit, step, 0)

    def widen(i, _):
        tile = out_ref[aligned(i * 2, 2)].reshape(2 * times, cells)
        for b in range(blocks):
            wide[b, aligned(i * 2 * times, 2 * times), :] = tile[:, b * lanes : (b + 1) * lanes].astype(F32)
        return 0

    lax.fori_loop(0, first * unit // 2, widen, 0)

    deep = -(-each * blocks // lanes)
    over = jnp.int32(0)
    for k in range(pieces):
        over = over + (bits_s[count + k, deep, each - 1] > panel_bufs.shape[1] - 1).astype(I32)
        over = over + bits_s[count + k, deep + 1, 0]

    @pl.loop(0, pieces)
    def _(k):
        place = sources_ref[k] * each

        def store(i, b, tile):
            panel[b, aligned((place + i) * times, times), :] = tile.astype(F32)

        expand(panel_bufs.at[k], bits_s.at[count + k], 0, each, blocks, store)

    def at_time(values, t, size):
        picked = [values[b, pl.ds(t, size, stride=times), :] for b in range(blocks)]
        return jnp.concatenate(picked, axis=1).astype(BF16)

    def product(t, total):
        left = at_time(wide, t, rows)
        right = at_time(panel, t, pieces * each)
        return total + lax.dot_general(left, right, (((1,), (1,)), ((), ())), preferred_element_type=F32)

    part_ref[0:rows, :] = lax.fori_loop(0, times, product, jnp.zeros((rows, pieces * each), F32))
    part_ref[rows:, :] = jnp.broadcast_to(over, (8, pieces * each)).astype(F32)


def last_rows(msgs, panel_msgs, start, sources, cov, near, mix, done, unit, each):
    times, lanes = panel_msgs[0].shape[1:]
    rows, _, cells = done.shape
    count, chunks, pieces = len(msgs), len(msgs[0]), len(panel_msgs)
    slots = sum(chunk.shape[0] for chunk in msgs[0])
    flat = [chunk for msg in msgs for chunk in msg] + list(panel_msgs)
    return pl.pallas_call(
        functools.partial(last_kernel, count, chunks, pieces, unit, each),
        out_shape=(shape_of(done.shape, BF16), shape_of((rows + 8, pieces * each), F32)),
        in_specs=[ANY] * len(flat) + [SMEM, SMEM] + [VMEM] * 4,
        out_specs=(VMEM, VMEM),
        scratch_shapes=[
            pltpu.VMEM((count, slots, times, lanes), BF16),
            pltpu.VMEM((pieces, panel_msgs[0].shape[0], times, lanes), BF16),
            pltpu.VMEM((count + pieces, 8, lanes), I32),
            pltpu.SMEM((count + pieces, 8, lanes), I32),
            pltpu.VMEM((unit * times, count * cells), BF16),
            pltpu.VMEM((cells // lanes, rows * times, lanes), F32),
            pltpu.VMEM((cells // lanes, pieces * each * times, lanes), F32),
            pltpu.SemaphoreType.DMA((count + 1, chunks)),
            pltpu.SemaphoreType.DMA((pieces,)),
        ],
        input_output_aliases={len(flat) + 5: 0},
        compiler_params=params(36),
        cost_estimate=cost(10),
        name="last_rows",
    )(*flat, start, sources, cov, near, mix, done)


def mix_kernel(unit, time_ref, out_ref):
    times = time_ref.shape[0]
    size = unit * times
    value = time_ref[...]
    high = value.astype(BF16)
    low = (value - high.astype(F32)).astype(BF16)

    def same(shape, dim):
        index = lax.broadcasted_iota(I32, shape, 1 - dim) % times
        return (index == lax.broadcasted_iota(I32, shape, dim)).astype(F32).astype(BF16)

    row = lax.broadcasted_iota(I32, (size, size), 0)
    col = lax.broadcasted_iota(I32, (size, size), 1)
    for j, part in enumerate((high, high, low)):
        spread = jnp.dot(same((size, times), 1), part, preferred_element_type=F32).astype(BF16)
        spread = jnp.dot(spread, same((times, size), 0), preferred_element_type=F32)
        out_ref[:, j * size : (j + 1) * size] = jnp.where(row // times == col // times, spread, 0.0).astype(BF16)


def mixing(time_cov, unit):
    size = unit * time_cov.shape[0]
    return pl.pallas_call(
        functools.partial(mix_kernel, unit),
        out_shape=shape_of((size, 3 * size), BF16),
        in_specs=[VMEM],
        out_specs=VMEM,
        compiler_params=params(8),
        cost_estimate=cost(1),
        name="mixing",
    )(time_cov)


def partner(value, axis, count):
    return lax.ppermute(value, axis, [(i, i ^ 1) for i in range(count)])


def shifted(value, axis, count, shift, flip=0):
    return lax.ppermute(value, axis, [(i, ((i + 2 * shift) % count) ^ flip) for i in range(count)])


def add_cells(part, cells):
    total = part
    for shift in range(cells // 2):
        for flip in range(2):
            if shift or flip:
                total = total + shifted(part, "cell", cells, shift, flip)
    return total


def dense_way(cells, observers, footprint, block_mask, own, time_cov, mine, sources):
    obs_rows, times, cell_local = footprint.shape
    blocks = block_mask.shape[1]
    keep = block_mask.astype(BF16)[:, None, :, None]
    feet = (footprint.reshape(obs_rows, times, blocks, cell_local // blocks) * keep).reshape(footprint.shape)

    def add(carry, _):
        total, feet, info = carry
        dx = info[0][:, None] - own[0][None, :]
        dy = info[1][:, None] - own[1][None, :]
        decay = jnp.exp(-jnp.sqrt(dx * dx + dy * dy + 1.0) / LENGTH)
        cov = (decay * (info[2][:, None] * own[2][None, :])).astype(BF16)
        total = total + jnp.dot(feet.reshape(-1, cell_local), cov, preferred_element_type=F32)
        ring = [(i, (i + 1) % cells) for i in range(cells)]
        return (total, lax.ppermute(feet, "cell", ring), lax.ppermute(info, "cell", ring)), None

    zero = jnp.zeros((obs_rows * times, cell_local), F32)
    (total, _, _), _ = lax.scan(add, (zero, feet, own), None, length=cells)
    cov_product = jnp.einsum(
        "ts,ksc->ktc", time_cov, total.reshape(obs_rows, times, cell_local), precision=lax.Precision.HIGHEST
    ).astype(BF16)
    flat = cov_product.reshape(obs_rows, times * cell_local)

    def meet(held, _):
        both = jnp.concatenate([held, partner(held, "obs", observers)], axis=0)
        part = lax.dot_general(
            flat, both.reshape(both.shape[0], -1), (((1,), (1,)), ((), ())), preferred_element_type=F32
        )
        return shifted(held, "obs", observers, 1), part

    _, parts = lax.scan(meet, jnp.take(feet, mine, axis=0), None, length=observers // 2)
    parts = parts.transpose(1, 0, 2).reshape(obs_rows, observers, -1)
    ordered = jnp.zeros_like(parts).at[:, sources].set(parts)
    return cov_product, add_cells(ordered.reshape(obs_rows, -1), cells)


def body(cells, observers, footprint, block_mask, cell_coords, cell_sigma, time_cov, error_var, panel_index):
    obs_rows, times, cell_local = footprint.shape
    blocks = block_mask.shape[1]
    group = lax.axis_index("obs")
    each = panel_index.shape[0] // observers
    half = observers // 2
    unit = math.gcd(16, obs_rows)
    slots = slot_count(obs_rows * blocks, 1 + blocks)
    chunks = (slots - slots // 2, slots // 2)
    mask = block_mask.T
    order = jnp.arange(observers, dtype=I32)
    sources = (group // 2 - order // 2) % half * 2 + (group % 2 ^ (order % 2))

    *own_msg, flag = pack_feet(mask, cell_coords, cell_sigma[None, :], footprint, chunks)
    far_msgs = [[shifted(c, "cell", cells, shift) for c in own_msg] for shift in range(1, cells // 2)]
    mate_msg = [partner(c, "cell", cells) for c in own_msg]
    own_panel = pack_panel(mask, panel_index, group, flag, footprint, each, slot_count(each * blocks, 1))
    ring = [own_panel]
    for _ in range(1, half):
        ring.append(shifted(ring[-1], "obs", observers, 1))
    messages = []
    for held in ring:
        messages += [held, partner(held, "obs", observers)]
    far_msgs += [[partner(c, "cell", cells) for c in msg] for msg in far_msgs]

    near, mate_dense, mate_cov, info = own_call(own_msg, mate_msg, obs_rows, cell_local)
    near, far_cov = mate_call([msg[0] for msg in far_msgs], near, mate_dense, mate_cov, info)
    mix = mixing(time_cov, unit)
    cov_product, start = first_rows([msg[:1] for msg in far_msgs], far_cov, near, mix, obs_rows, unit, slots)
    cov_product, part = last_rows(
        far_msgs, messages, start, sources, far_cov, near, mix, cov_product, unit, each
    )
    total = add_cells(part, cells)

    def again(carry):
        mine = lax.dynamic_slice_in_dim(panel_index, group * each, each) - group * obs_rows
        return (jnp.bool_(False),) + dense_way(
            cells, observers, footprint, block_mask, info, time_cov, mine, sources
        )

    _, cov_product, total = lax.while_loop(
        lambda carry: carry[0], again, (total[obs_rows, 0] > 0, cov_product, total[:obs_rows])
    )
    positions = jnp.arange(obs_rows, dtype=I32)
    on_diagonal = ((group * obs_rows + positions)[:, None] == panel_index[None, :]).astype(F32)
    return cov_product, total + error_var[:, None] * on_diagonal


def solution(mesh):
    in_specs = (
        P("obs", None, "cell"),
        P("obs", "cell"),
        P(None, "cell"),
        P("cell"),
        P(),
        P("obs"),
        P(),
    )
    out_specs = (P("obs", None, "cell"), P("obs", None))
    cells, observers = mesh.shape["cell"], mesh.shape["obs"]

    def per_device(*args):
        return body(cells, observers, *args)

    return jax.shard_map(
        per_device, mesh=mesh, in_specs=in_specs, out_specs=out_specs, check_vma=False
    )
```

```python
import functools
import math

import jax
import jax.numpy as jnp
from jax import lax
from jax.experimental import pallas as pl
from jax.experimental.pallas import tpu as pltpu
from jax.sharding import PartitionSpec as P


GRID = 64
LENGTH = GRID / 16.0
F32, BF16, I32 = jnp.float32, jnp.bfloat16, jnp.int32
SHIFT = 4
INFO = 8


VMEM = pl.BlockSpec(memory_space=pltpu.VMEM)
SMEM = pl.BlockSpec(memory_space=pltpu.SMEM)
ANY = pl.BlockSpec(memory_space=pl.ANY)
HBM = pl.BlockSpec(memory_space=pltpu.HBM)


def shape_of(shape, dtype):
    return jax.ShapeDtypeStruct(shape, dtype)


def params(mib):
    return pltpu.CompilerParams(vmem_limit_bytes=mib * 2**20)


def cost(micros):
    return pl.CostEstimate(flops=int(micros * 9e8), bytes_accessed=1_000_000, transcendentals=0)


def aligned(start, size):
    return pl.ds(pl.multiple_of(start, size), size)


def slot_count(tiles, extra):
    room = tiles / 2 + 4.1 * math.sqrt(tiles / 4)
    return extra + min(tiles + 1, 2 * math.ceil(room / 2) + 1)


def pack_rows(mask_at, feet_at, begin, end, blocks, buf, carry):
    slots, _, lanes = buf.shape
    row_of = lax.broadcasted_iota(I32, (8, lanes), 0)
    lane_of = lax.broadcasted_iota(I32, (8, lanes), 1)
    flat = row_of * lanes + lane_of
    batch = math.gcd(2, end - begin)

    def some(i, carry):
        pos, head, ends = carry
        first = begin + i * batch
        tiles = [[feet_at(first + j, b) for b in range(blocks)] for j in range(batch)]
        kept = [[mask_at(first + j, b) for b in range(blocks)] for j in range(batch)]
        for j in range(batch):
            for b in range(blocks):
                buf[jnp.minimum(pos, slots - 1)] = tiles[j][b]
                head = jnp.where(flat == (first + j) * blocks + b, kept[j][b] * pos, head)
                pos = pos + kept[j][b]
            ends = jnp.where(lane_of == first + j, pos, ends)
        return pos, head, ends

    return lax.fori_loop(0, (end - begin) // batch, some, carry)


def no_rows(first, lanes):
    zeros = jnp.zeros((8, lanes), I32)
    return jnp.int32(first), zeros, zeros


def write_head(carry, rows, blocks, buf, head_v, flag=None):
    lanes = buf.shape[2]
    deep = -(-rows * blocks // lanes)
    _, head, ends = carry
    low = (1 << SHIFT) - 1
    head_v[...] = jnp.zeros_like(head_v)
    head_v[0:deep, :] = (head >> SHIFT)[0:deep].astype(F32)
    head_v[deep : 2 * deep, :] = (head & low)[0:deep].astype(F32)
    head_v[2 * deep : 2 * deep + 1, :] = (ends >> SHIFT)[0:1].astype(F32)
    head_v[2 * deep + 1 : 2 * deep + 2, :] = (ends & low)[0:1].astype(F32)
    if flag is not None:
        head_v[2 * deep + 2 : 2 * deep + 3, :] = jnp.broadcast_to(flag, (1, lanes)).astype(F32)
    buf[0] = head_v[...].astype(BF16)


def pack_feet_kernel(chunks, mask_ref, coords_hbm, sigma_hbm, feet_ref, *rest):
    outs, (coords_ref, sigma_ref, feet, buf, head_v, small_sem, in_sem, sem) = (
        rest[: len(chunks)],
        rest[len(chunks) :],
    )
    blocks, rows = mask_ref.shape
    small = [
        pltpu.make_async_copy(src, dst, small_sem.at[k])
        for k, (src, dst) in enumerate(((coords_hbm, coords_ref), (sigma_hbm, sigma_ref)))
    ]
    for copy in small:
        copy.start()
    times, lanes = buf.shape[1:]
    groups = in_sem.shape[0]
    each = rows // groups
    loads = [
        pltpu.make_async_copy(feet_ref.at[pl.ds(g * each, each)], feet.at[pl.ds(g * each, each)], in_sem.at[g])
        for g in range(groups)
    ]
    for load in loads:
        load.start()
    for copy in small:
        copy.wait()
    sigma = sigma_ref[...]
    high = sigma.astype(BF16).astype(F32)
    middle = (sigma - high).astype(BF16).astype(F32)
    lowest = sigma - high - middle
    at = lax.broadcasted_iota(I32, (times, sigma.shape[1]), 0)
    info = jnp.zeros(at.shape, F32)
    for k, row in enumerate((coords_ref[0:1, :].astype(F32), coords_ref[1:2, :].astype(F32), high, middle, lowest)):
        info = jnp.where(at == k, row, info)
    info = info.astype(BF16)
    for b in range(blocks):
        buf[1 + b] = info[:, b * lanes : (b + 1) * lanes]
    carry = no_rows(1 + blocks, lanes)
    for g in range(groups):
        loads[g].wait()
        carry = pack_rows(
            lambda o, b: mask_ref[b, o],
            lambda o, b: feet[o, :, b * lanes : (b + 1) * lanes],
            g * each,
            (g + 1) * each,
            blocks,
            buf,
            carry,
        )
    write_head(carry, rows, blocks, buf, head_v)
    copies, first = [], 0
    for k, size in enumerate(chunks):
        copies.append(pltpu.make_async_copy(buf.at[pl.ds(first, size)], outs[k], sem.at[k]))
        first += size
    for copy in copies:
        copy.start()
    for copy in copies:
        copy.wait()


def pack_feet(mask, coords, sigma, feet, chunks):
    rows, times, cells = feet.shape
    lanes = cells // mask.shape[0]
    groups = math.gcd(4, rows)
    return pl.pallas_call(
        functools.partial(pack_feet_kernel, chunks),
        out_shape=tuple(shape_of((size, times, lanes), BF16) for size in chunks),
        in_specs=[SMEM, HBM, HBM, HBM],
        out_specs=(ANY,) * len(chunks),
        scratch_shapes=[
            pltpu.VMEM(coords.shape, I32),
            pltpu.VMEM(sigma.shape, F32),
            pltpu.VMEM((rows, times, cells), BF16),
            pltpu.VMEM((sum(chunks), times, lanes), BF16),
            pltpu.VMEM((times, lanes), F32),
            pltpu.SemaphoreType.DMA((2,)),
            pltpu.SemaphoreType.DMA((groups,)),
            pltpu.SemaphoreType.DMA((len(chunks),)),
        ],
        compiler_params=params(12),
        cost_estimate=cost(3),
        name="pack_feet",
    )(mask, coords, sigma, feet)


def pack_panel_kernel(room, mask_ref, mask_hbm, index_hbm, group_ref, feet_ref, out_ref, mask_v, index_ref, rows_buf, head_v, small_sem, sem):
    count = rows_buf.shape[0]
    blocks, obs = mask_ref.shape
    lanes = out_ref.shape[2]
    small = [
        pltpu.make_async_copy(src, dst, small_sem.at[k])
        for k, (src, dst) in enumerate(((index_hbm, index_ref), (mask_hbm, mask_v)))
    ]
    for copy in small:
        copy.start()
    base = group_ref[0]
    small[0].wait()
    rows = [jnp.clip(index_ref[base * count + j] - base * obs, 0, obs - 1) for j in range(count)]
    copies = [pltpu.make_async_copy(feet_ref.at[rows[j]], rows_buf.at[j], sem.at[j]) for j in range(count)]
    for copy in copies:
        copy.start()
    for copy in small[1:]:
        copy.wait()
    flag = (jnp.sum(mask_v[...].astype(F32), axis=(0, 1), keepdims=True) > room).astype(I32)
    for copy in copies:
        copy.wait()

    def mask_at(o, b):
        return mask_ref[b, jnp.clip(index_ref[base * count + o] - base * obs, 0, obs - 1)]

    carry = pack_rows(
        mask_at, lambda o, b: rows_buf[o, :, b * lanes : (b + 1) * lanes], 0, count, blocks, out_ref, no_rows(1, lanes)
    )
    write_head(carry, count, blocks, out_ref, head_v, flag)


def pack_panel(mask, panel_index, group, feet, count, slots, room):
    _, times, cells = feet.shape
    lanes = cells // mask.shape[0]
    return pl.pallas_call(
        functools.partial(pack_panel_kernel, room),
        out_shape=shape_of((slots, times, lanes), BF16),
        in_specs=[SMEM, HBM, HBM, SMEM, HBM],
        out_specs=VMEM,
        scratch_shapes=[
            pltpu.VMEM(mask.shape, I32),
            pltpu.SMEM(panel_index.shape, I32),
            pltpu.VMEM((count, times, cells), BF16),
            pltpu.VMEM((times, lanes), F32),
            pltpu.SemaphoreType.DMA((2,)),
            pltpu.SemaphoreType.DMA((count,)),
        ],
        compiler_params=params(8),
        cost_estimate=cost(2),
        name="pack_panel",
    )(mask, mask, panel_index, group[None], feet)


def fetch(chunks, buf, sem):
    copies, first = [], 0
    for k, chunk in enumerate(chunks):
        copies.append(pltpu.make_async_copy(chunk, buf.at[pl.ds(first, chunk.shape[0])], sem.at[k]))
        copies[-1].start()
        first += chunk.shape[0]
    return copies


def read_head(buf, rows, blocks, bits_v, flagged=False):
    slots, _, lanes = buf.shape
    deep = -(-rows * blocks // lanes)
    head = buf[0].astype(F32)
    scale = float(1 << SHIFT)
    bits_v[0:deep, :] = jnp.minimum(head[0:deep] * scale + head[deep : 2 * deep], slots - 1.0).astype(I32)
    bits_v[deep : deep + 1, :] = (head[2 * deep : 2 * deep + 1] * scale + head[2 * deep + 1 : 2 * deep + 2]).astype(I32)
    if flagged:
        bits_v[deep + 1 : deep + 2, :] = head[2 * deep + 2 : 2 * deep + 3].astype(I32)
    buf[0] = jnp.zeros(buf.shape[1:], buf.dtype)


def copy_in(src, dst, sem):
    copy = pltpu.make_async_copy(src, dst, sem)
    copy.start()
    copy.wait()


def expand(buf, bits, first, count, blocks, store, unrolled=False):
    lanes = buf.shape[2]
    batch = math.gcd(2, count)

    def some(i, _):
        tiles = []
        for j in range(batch):
            base = (first + i * batch + j) * blocks
            row, col = lax.div(base, lanes), lax.rem(base, lanes)
            tiles += [buf[bits[row, col + b]] for b in range(blocks)]
        for j in range(batch):
            for b in range(blocks):
                store(i * batch + j, b, tiles[j * blocks + b])
        return 0

    if unrolled:
        for i in range(count // batch):
            some(i, 0)
    else:
        lax.fori_loop(0, count // batch, some, 0)


def into(dense, times, lanes, offset, first=0):
    def store(i, b, tile):
        at = aligned((first + i) * times, times)
        dense[at, offset + b * lanes : offset + (b + 1) * lanes] = tile.astype(dense.dtype)

    return store


def read_info(buf, blocks, row_v, turned):
    _, lanes = buf.shape[1:]
    for b in range(blocks):
        tile = buf[1 + b].astype(F32)[0:INFO]
        sigma = tile[2:3] + tile[3:4] + tile[4:5]
        tile = jnp.where(lax.broadcasted_iota(I32, tile.shape, 0) == 2, sigma, tile)
        at = slice(b * lanes, (b + 1) * lanes)
        if row_v is not None:
            row_v[:, at] = tile
        if turned is not None:
            turned[at, :] = tile.T


def fill_covariance(dst, dst_first, src_first, rows, turned, own):
    x, y, s = own[0:1, :], own[1:2, :], own[2:3, :]
    step = min(32, rows)
    for i in range(rows // step):
        at = aligned(src_first + i * step, step)
        dx = turned[at, 0:1] - x
        dy = turned[at, 1:2] - y
        square = dx * dx + dy * dy + 1.0
        decay = jnp.exp(square * lax.rsqrt(square) * (-1.0 / LENGTH))
        dst[aligned(dst_first + i * step, step), :] = (decay * (turned[at, 2:3] * s)).astype(BF16)


def own_kernel(chunks, *refs):
    msgs = refs[:chunks], refs[chunks : 2 * chunks]
    out_ref, mate_dense, next_ref, info_ref = refs[2 * chunks : 2 * chunks + 4]
    bufs, bits_v, bits_s, dense, cov, turned, sem = refs[2 * chunks + 4 :]
    times, lanes = bufs.shape[2:]
    cells = cov.shape[1]
    blocks = cells // lanes
    rows = dense.shape[0] // times
    tall = min(256, rows * times)
    steps = rows * times // tall
    part = cells // steps
    copies = [fetch(msg, bufs.at[k], sem.at[k]) for k, msg in enumerate(msgs)]
    for k in range(2):
        for copy in copies[k]:
            copy.wait()
        read_info(bufs.at[k], blocks, None if k else info_ref, turned.at[k])
        read_head(bufs.at[k], rows, blocks, bits_v.at[k])
    copy_in(bits_v, bits_s, sem.at[2, 0])
    fine = math.gcd(8, rows // 2)
    piece = cells // fine

    @pl.loop(0, fine)
    def _(i):
        fill_covariance(cov, i * piece, i * piece, piece, turned.at[0], info_ref)
        some = rows // fine
        expand(bufs.at[0], bits_s.at[0], i * some, some, blocks, into(dense, times, lanes, 0, i * some), unrolled=True)

    @pl.loop(0, steps)
    def _(u):
        here = aligned(u * tall, tall)
        fill_covariance(next_ref, u * part, u * part, part, turned.at[1], info_ref)
        out_ref[here, :] = jnp.dot(dense[here, :], cov[...], preferred_element_type=F32)
        some = rows // steps
        expand(bufs.at[1], bits_s.at[1], u * some, some, blocks, into(mate_dense, times, lanes, 0, u * some), unrolled=True)


def own_call(own_msg, mate_msg, rows, cells):
    times, lanes = own_msg[0].shape[1:]
    slots = sum(chunk.shape[0] for chunk in own_msg)
    chunks = len(own_msg)
    return pl.pallas_call(
        functools.partial(own_kernel, chunks),
        out_shape=(
            shape_of((rows * times, cells), F32),
            shape_of((rows * times, cells), BF16),
            shape_of((cells, cells), BF16),
            shape_of((INFO, cells), F32),
        ),
        in_specs=[ANY] * (2 * chunks),
        out_specs=(VMEM,) * 4,
        scratch_shapes=[
            pltpu.VMEM((2, slots, times, lanes), BF16),
            pltpu.VMEM((2, 8, lanes), I32),
            pltpu.SMEM((2, 8, lanes), I32),
            pltpu.VMEM((rows * times, cells), BF16),
            pltpu.VMEM((cells, cells), BF16),
            pltpu.VMEM((2, cells, INFO), F32),
            pltpu.SemaphoreType.DMA((3, chunks)),
        ],
        compiler_params=params(24),
        cost_estimate=cost(9),
        name="own_product",
    )(*own_msg, *mate_msg)


def mate_kernel(count, *refs):
    firsts = refs[:count]
    near_ref, dense, cov_ref, info_ref, out_ref, far_ref, info_buf, turned, sem = refs[count:]
    _, lanes = info_buf.shape[2:]
    cells = cov_ref.shape[1]
    blocks = cells // lanes
    tall = min(256, dense.shape[0])
    steps = dense.shape[0] // tall
    part = count * cells // steps
    copies = []
    for k in range(count):
        copies.append(pltpu.make_async_copy(firsts[k].at[pl.ds(0, 1 + blocks)], info_buf.at[k], sem.at[k]))
        copies[-1].start()
    for k in range(count):
        copies[k].wait()
        read_info(info_buf.at[k], blocks, None, turned.at[pl.ds(k * cells, cells)])

    @pl.loop(0, steps)
    def _(u):
        here = aligned(u * tall, tall)
        fill_covariance(far_ref, u * part, u * part, part, turned, info_ref)
        out_ref[here, :] = near_ref[here, :] + jnp.dot(dense[here, :], cov_ref[...], preferred_element_type=F32)


def mate_call(firsts, near, mate_dense, cov, info):
    times, lanes = firsts[0].shape[1:]
    cells = cov.shape[1]
    blocks = cells // lanes
    count = len(firsts)
    return pl.pallas_call(
        functools.partial(mate_kernel, count),
        out_shape=(shape_of(near.shape, F32), shape_of((count * cells, cells), BF16)),
        in_specs=[ANY] * count + [VMEM] * 4,
        out_specs=(VMEM, VMEM),
        scratch_shapes=[
            pltpu.VMEM((count, 1 + blocks, times, lanes), BF16),
            pltpu.VMEM((count * cells, INFO), F32),
            pltpu.SemaphoreType.DMA((count,)),
        ],
        input_output_aliases={count: 0},
        compiler_params=params(24),
        cost_estimate=cost(8),
        name="mate_product",
    )(*firsts, near, mate_dense, cov, info)


def mixed_unit(mix_ref, value):
    high = value.astype(BF16)
    low = (value - high.astype(F32)).astype(BF16)
    stacked = jnp.concatenate([high, low, high], axis=0)
    return jnp.dot(mix_ref[...], stacked, preferred_element_type=F32).astype(BF16)


def turn(value, rows, times):
    return jnp.swapaxes(value.reshape(rows, times, value.shape[1]), 0, 1)


def first_kernel(count, chunks, unit, *refs):
    msgs = [refs[k * chunks : (k + 1) * chunks] for k in range(count)]
    cov_ref, near_ref, mix_ref, out_ref, next_ref, bufs, bits_v, bits_s, dense, sem = refs[count * chunks :]
    times, lanes = bufs.shape[2:]
    cells = near_ref.shape[1]
    blocks = cells // lanes
    rows = out_ref.shape[0]
    deep = -(-rows * blocks // lanes)
    limit = sum(chunk.shape[0] for chunk in msgs[0])
    copies = [fetch(msgs[k], bufs.at[k], sem.at[k]) for k in range(count)]
    for k in range(count):
        for copy in copies[k]:
            copy.wait()
        read_head(bufs.at[k], rows, blocks, bits_v.at[k])
    copy_in(bits_v, bits_s, sem.at[count, 0])
    ready = jnp.int32(0)
    for u in range(rows // unit):
        whole = jnp.int32(1)
        for k in range(count):
            whole = whole * (bits_s[k, deep, (u + 1) * unit - 1] <= limit).astype(I32)
        ready = ready + whole
    next_ref[0] = ready

    def step(u, _):
        for k in range(count):
            expand(bufs.at[k], bits_s.at[k], u * unit, unit, blocks, into(dense, times, lanes, k * cells))
        here = aligned(u * unit * times, unit * times)
        value = near_ref[here, :] + jnp.dot(dense[...], cov_ref[...], preferred_element_type=F32)
        out_ref[aligned(u * unit, unit)] = mixed_unit(mix_ref, value).reshape(unit, times, cells)
        return 0

    lax.fori_loop(0, ready, step, 0)


def first_rows(msgs, cov, near, mix, rows, unit, slots):
    times, lanes = msgs[0][0].shape[1:]
    cells = near.shape[1]
    count, chunks = len(msgs), len(msgs[0])
    flat = [chunk for msg in msgs for chunk in msg]
    return pl.pallas_call(
        functools.partial(first_kernel, count, chunks, unit),
        out_shape=(shape_of((rows, times, cells), BF16), shape_of((1,), I32)),
        in_specs=[ANY] * len(flat) + [VMEM] * 3,
        out_specs=(VMEM, SMEM),
        scratch_shapes=[
            pltpu.VMEM((count, slots, times, lanes), BF16),
            pltpu.VMEM((count, 8, lanes), I32),
            pltpu.SMEM((count, 8, lanes), I32),
            pltpu.VMEM((unit * times, count * cells), BF16),
            pltpu.SemaphoreType.DMA((count + 1, chunks)),
        ],
        compiler_params=params(20),
        cost_estimate=cost(6),
        name="first_rows",
    )(*flat, cov, near, mix)


def last_kernel(count, chunks, pieces, unit, each, *refs):
    msgs = [refs[k * chunks : (k + 1) * chunks] for k in range(count)]
    panel_msgs = refs[count * chunks : count * chunks + pieces]
    refs = refs[count * chunks + pieces :]
    start_ref, sources_ref, cov_ref, near_ref, mix_ref, done_ref, out_ref, part_ref = refs[:8]
    bufs, panel_bufs, bits_v, bits_s, dense, turned, panel, sem, panel_sem = refs[8:]
    times, lanes = bufs.shape[2:]
    cells = near_ref.shape[1]
    blocks = cells // lanes
    rows = out_ref.shape[0]
    copies = [fetch(msgs[k], bufs.at[k], sem.at[k]) for k in range(count)]
    panel_copies = [
        pltpu.make_async_copy(panel_msgs[k], panel_bufs.at[k], panel_sem.at[k]) for k in range(pieces)
    ]
    for copy in panel_copies:
        copy.start()
    for k in range(count):
        for copy in copies[k]:
            copy.wait()
        read_head(bufs.at[k], rows, blocks, bits_v.at[k])
    for k in range(pieces):
        panel_copies[k].wait()
        read_head(panel_bufs.at[k], each, blocks, bits_v.at[count + k], flagged=True)
    copy_in(bits_v, bits_s, sem.at[count, 0])
    first = start_ref[0]

    def step(u, _):
        for k in range(count):
            expand(bufs.at[k], bits_s.at[k], u * unit, unit, blocks, into(dense, times, lanes, k * cells))
        here = aligned(u * unit * times, unit * times)
        value = near_ref[here, :] + jnp.dot(dense[...], cov_ref[...], preferred_element_type=F32)
        mixed = mixed_unit(mix_ref, value)
        out_ref[aligned(u * unit, unit)] = mixed.reshape(unit, times, cells)
        turned[:, aligned(u * unit, unit), :] = turn(mixed, unit, times)
        return 0

    lax.fori_loop(first, rows // unit, step, 0)

    def earlier(u, _):
        at = aligned(u * unit, unit)
        value = done_ref[at]
        out_ref[at] = value
        value = value.reshape(unit * times, cells)
        turned[:, aligned(u * unit, unit), :] = turn(value, unit, times)
        return 0

    lax.fori_loop(0, first, earlier, 0)

    deep = -(-each * blocks // lanes)
    over = jnp.int32(0)
    for k in range(pieces):
        over = over + (bits_s[count + k, deep, each - 1] > panel_bufs.shape[1] - 1).astype(I32)
        over = over + bits_s[count + k, deep + 1, 0]

    group = max(1, 16 // each)
    placed = each % 16 == 0

    @pl.loop(0, pieces // group)
    def _(g):
        at = pl.multiple_of((sources_ref[g] if placed else g) * each * group, 16)
        for b in range(blocks):
            tiles = []
            for i in range(group * each):
                k, place = g * group + i // each, i % each * blocks + b
                tiles.append(panel_bufs[k, bits_s[count + k, place // lanes, place % lanes]])
            value = turn(jnp.concatenate(tiles, axis=0), group * each, times)
            panel[:, pl.ds(at, group * each), b * lanes : (b + 1) * lanes] = value

    total = None
    for t in range(times):
        value = lax.dot_general(
            turned[t], panel[t], (((1,), (1,)), ((), ())), preferred_element_type=F32
        )
        total = value if total is None else total + value
    if not placed:
        size = pieces * each
        row = lax.broadcasted_iota(I32, (size, size), 0)
        target = row
        for k in range(pieces):
            target = jnp.where(row // each == k, sources_ref[k] * each + row % each, target)
        select = (lax.broadcasted_iota(I32, (size, size), 1) == target).astype(F32).astype(BF16)
        value, total = total, jnp.zeros(total.shape, F32)
        for _ in range(3):
            high = value.astype(BF16)
            total = total + jnp.dot(high, select, preferred_element_type=F32)
            value = value - high.astype(F32)
    part_ref[0:rows, :] = total
    part_ref[rows:, :] = jnp.broadcast_to(over, (8, pieces * each)).astype(F32)


def last_rows(msgs, panel_msgs, start, sources, cov, near, mix, done, unit, each):
    times, lanes = panel_msgs[0].shape[1:]
    rows, _, cells = done.shape
    count, chunks, pieces = len(msgs), len(msgs[0]), len(panel_msgs)
    slots = sum(chunk.shape[0] for chunk in msgs[0])
    flat = [chunk for msg in msgs for chunk in msg] + list(panel_msgs)
    return pl.pallas_call(
        functools.partial(last_kernel, count, chunks, pieces, unit, each),
        out_shape=(shape_of(done.shape, BF16), shape_of((rows + 8, pieces * each), F32)),
        in_specs=[ANY] * len(flat) + [SMEM, SMEM] + [VMEM] * 4,
        out_specs=(VMEM, VMEM),
        scratch_shapes=[
            pltpu.VMEM((count, slots, times, lanes), BF16),
            pltpu.VMEM((pieces, panel_msgs[0].shape[0], times, lanes), BF16),
            pltpu.VMEM((count + pieces, 8, lanes), I32),
            pltpu.SMEM((count + pieces, 8, lanes), I32),
            pltpu.VMEM((unit * times, count * cells), BF16),
            pltpu.VMEM((times, rows, cells), BF16),
            pltpu.VMEM((times, pieces * each, cells), BF16),
            pltpu.SemaphoreType.DMA((count + 1, chunks)),
            pltpu.SemaphoreType.DMA((pieces,)),
        ],
        compiler_params=params(36),
        cost_estimate=cost(10),
        name="last_rows",
    )(*flat, start, sources, cov, near, mix, done)


def mix_kernel(unit, time_ref, out_ref):
    times = time_ref.shape[0]
    size = unit * times
    value = time_ref[...]
    high = value.astype(BF16)
    low = (value - high.astype(F32)).astype(BF16)

    def same(shape, dim):
        index = lax.broadcasted_iota(I32, shape, 1 - dim) % times
        return (index == lax.broadcasted_iota(I32, shape, dim)).astype(F32).astype(BF16)

    row = lax.broadcasted_iota(I32, (size, size), 0)
    col = lax.broadcasted_iota(I32, (size, size), 1)
    for j, part in enumerate((high, high, low)):
        spread = jnp.dot(same((size, times), 1), part, preferred_element_type=F32).astype(BF16)
        spread = jnp.dot(spread, same((times, size), 0), preferred_element_type=F32)
        out_ref[:, j * size : (j + 1) * size] = jnp.where(row // times == col // times, spread, 0.0).astype(BF16)


def mixing(time_cov, unit):
    size = unit * time_cov.shape[0]
    return pl.pallas_call(
        functools.partial(mix_kernel, unit),
        out_shape=shape_of((size, 3 * size), BF16),
        in_specs=[VMEM],
        out_specs=VMEM,
        compiler_params=params(8),
        cost_estimate=cost(1),
        name="mixing",
    )(time_cov)


def partner(value, axis, count):
    return lax.ppermute(value, axis, [(i, i ^ 1) for i in range(count)])


def shifted(value, axis, count, shift, flip=0):
    return lax.ppermute(value, axis, [(i, ((i + 2 * shift) % count) ^ flip) for i in range(count)])


def add_cells(part, cells):
    total = part
    for shift in range(cells // 2):
        for flip in range(2):
            if shift or flip:
                total = total + shifted(part, "cell", cells, shift, flip)
    return total


def dense_way(cells, observers, footprint, block_mask, own, time_cov, mine, sources):
    obs_rows, times, cell_local = footprint.shape
    blocks = block_mask.shape[1]
    keep = block_mask.astype(BF16)[:, None, :, None]
    feet = (footprint.reshape(obs_rows, times, blocks, cell_local // blocks) * keep).reshape(footprint.shape)

    def add(carry, _):
        total, feet, info = carry
        dx = info[0][:, None] - own[0][None, :]
        dy = info[1][:, None] - own[1][None, :]
        decay = jnp.exp(-jnp.sqrt(dx * dx + dy * dy + 1.0) / LENGTH)
        cov = (decay * (info[2][:, None] * own[2][None, :])).astype(BF16)
        total = total + jnp.dot(feet.reshape(-1, cell_local), cov, preferred_element_type=F32)
        ring = [(i, (i + 1) % cells) for i in range(cells)]
        return (total, lax.ppermute(feet, "cell", ring), lax.ppermute(info, "cell", ring)), None

    zero = jnp.zeros((obs_rows * times, cell_local), F32)
    (total, _, _), _ = lax.scan(add, (zero, feet, own), None, length=cells)
    cov_product = jnp.einsum(
        "ts,ksc->ktc", time_cov, total.reshape(obs_rows, times, cell_local), precision=lax.Precision.HIGHEST
    ).astype(BF16)
    flat = cov_product.reshape(obs_rows, times * cell_local)

    def meet(held, _):
        both = jnp.concatenate([held, partner(held, "obs", observers)], axis=0)
        part = lax.dot_general(
            flat, both.reshape(both.shape[0], -1), (((1,), (1,)), ((), ())), preferred_element_type=F32
        )
        return shifted(held, "obs", observers, 1), part

    _, parts = lax.scan(meet, jnp.take(feet, mine, axis=0), None, length=observers // 2)
    parts = parts.transpose(1, 0, 2).reshape(obs_rows, observers, -1)
    ordered = jnp.zeros_like(parts).at[:, sources].set(parts)
    return cov_product, add_cells(ordered.reshape(obs_rows, -1), cells)


def body(cells, observers, footprint, block_mask, cell_coords, cell_sigma, time_cov, error_var, panel_index):
    obs_rows, _, cell_local = footprint.shape
    blocks = block_mask.shape[1]
    group = lax.axis_index("obs")
    each = panel_index.shape[0] // observers
    half = observers // 2
    unit = math.gcd(16, obs_rows)
    slots = slot_count(obs_rows * blocks, 1 + blocks)
    chunks = (slots - slots // 2, slots // 2)
    mask = block_mask.T
    order = jnp.arange(observers, dtype=I32)
    sources = (group // 2 - order // 2) % half * 2 + (group % 2 ^ (order % 2))

    room = slots - 2 - blocks - 1
    own_panel = pack_panel(mask, panel_index, group, footprint, each, slot_count(each * blocks, 1), room)
    ring = [own_panel]
    for _ in range(1, half):
        ring.append(shifted(ring[-1], "obs", observers, 1))
    messages = []
    for held in ring:
        messages += [held, partner(held, "obs", observers)]
    own_msg = pack_feet(mask, cell_coords, cell_sigma[None, :], footprint, chunks)
    far_msgs = []
    for shift in range(1, cells // 2):
        far_msgs.append([shifted(c, "cell", cells, shift) for c in own_msg])
    mate_msg = [partner(c, "cell", cells) for c in own_msg]
    for shift in range(1, cells // 2):
        far_msgs.append([partner(c, "cell", cells) for c in far_msgs[shift - 1]])

    near, mate_dense, mate_cov, info = own_call(own_msg, mate_msg, obs_rows, cell_local)
    near, far_cov = mate_call([msg[0] for msg in far_msgs], near, mate_dense, mate_cov, info)
    mix = mixing(time_cov, unit)
    cov_product, start = first_rows([msg[:1] for msg in far_msgs], far_cov, near, mix, obs_rows, unit, slots)
    cov_product, part = last_rows(far_msgs, messages, start, sources, far_cov, near, mix, cov_product, unit, each)
    total = add_cells(part, cells)

    def again(carry):
        wanted = carry[1][obs_rows, 0] > 0
        mask, cell_info, place, from_group = (
            jnp.where(wanted, value, 0) for value in (block_mask, info, group, sources)
        )
        mine = lax.dynamic_slice_in_dim(panel_index, place * each, each) - place * obs_rows
        cov_product, total = dense_way(
            cells, observers, footprint, mask, cell_info, time_cov, mine, from_group
        )
        return cov_product, jnp.pad(total, ((0, 8), (0, 0)))

    cov_product, total = lax.while_loop(lambda carry: carry[1][obs_rows, 0] > 0, again, (cov_product, total))
    total = total[:obs_rows]
    positions = jnp.arange(obs_rows, dtype=I32)
    on_diagonal = ((group * obs_rows + positions)[:, None] == panel_index[None, :]).astype(F32)
    return cov_product, total + error_var[:, None] * on_diagonal


def solution(mesh):
    in_specs = (
        P("obs", None, "cell"),
        P("obs", "cell"),
        P(None, "cell"),
        P("cell"),
        P(),
        P("obs"),
        P(),
    )
    out_specs = (P("obs", None, "cell"), P("obs", None))
    cells, observers = mesh.shape["cell"], mesh.shape["obs"]

    def per_device(*args):
        return body(cells, observers, *args)

    return jax.shard_map(per_device, mesh=mesh, in_specs=in_specs, out_specs=out_specs, check_vma=False)
```

```python
import functools
import math

import jax
import jax.numpy as jnp
from jax import lax
from jax.experimental import pallas as pl
from jax.experimental.pallas import tpu as pltpu
from jax.sharding import PartitionSpec as P


GRID = 64
LENGTH = GRID / 16.0
F32, BF16, I32 = jnp.float32, jnp.bfloat16, jnp.int32
SHIFT = 4
INFO = 8


VMEM = pl.BlockSpec(memory_space=pltpu.VMEM)
SMEM = pl.BlockSpec(memory_space=pltpu.SMEM)
ANY = pl.BlockSpec(memory_space=pl.ANY)
HBM = pl.BlockSpec(memory_space=pltpu.HBM)


def shape_of(shape, dtype):
    return jax.ShapeDtypeStruct(shape, dtype)


def params(mib):
    return pltpu.CompilerParams(vmem_limit_bytes=mib * 2**20)


def cost(micros):
    return pl.CostEstimate(flops=int(micros * 9e8), bytes_accessed=1_000_000, transcendentals=0)


def aligned(start, size):
    return pl.ds(pl.multiple_of(start, size), size)


def slot_count(tiles, extra):
    room = tiles / 2 + 4.1 * math.sqrt(tiles / 4)
    return extra + min(tiles + 1, 2 * math.ceil(room / 2) + 1)


def pack_rows(mask_at, feet_at, begin, end, blocks, buf, carry):
    slots, _, lanes = buf.shape
    row_of = lax.broadcasted_iota(I32, (8, lanes), 0)
    lane_of = lax.broadcasted_iota(I32, (8, lanes), 1)
    flat = row_of * lanes + lane_of
    batch = math.gcd(2, end - begin)

    def some(i, carry):
        pos, head, ends = carry
        first = begin + i * batch
        tiles = [[feet_at(first + j, b) for b in range(blocks)] for j in range(batch)]
        kept = [[mask_at(first + j, b) for b in range(blocks)] for j in range(batch)]
        for j in range(batch):
            for b in range(blocks):
                buf[jnp.minimum(pos, slots - 1)] = tiles[j][b]
                head = jnp.where(flat == (first + j) * blocks + b, kept[j][b] * pos, head)
                pos = pos + kept[j][b]
            ends = jnp.where(lane_of == first + j, pos, ends)
        return pos, head, ends

    return lax.fori_loop(0, (end - begin) // batch, some, carry)


def no_rows(first, lanes):
    zeros = jnp.zeros((8, lanes), I32)
    return jnp.int32(first), zeros, zeros


def write_head(carry, rows, blocks, buf, head_v, flag=None):
    lanes = buf.shape[2]
    deep = -(-rows * blocks // lanes)
    _, head, ends = carry
    low = (1 << SHIFT) - 1
    head_v[...] = jnp.zeros_like(head_v)
    head_v[0:deep, :] = (head >> SHIFT)[0:deep].astype(F32)
    head_v[deep : 2 * deep, :] = (head & low)[0:deep].astype(F32)
    head_v[2 * deep : 2 * deep + 1, :] = (ends >> SHIFT)[0:1].astype(F32)
    head_v[2 * deep + 1 : 2 * deep + 2, :] = (ends & low)[0:1].astype(F32)
    if flag is not None:
        head_v[2 * deep + 2 : 2 * deep + 3, :] = jnp.broadcast_to(flag, (1, lanes)).astype(F32)
    buf[0] = head_v[...].astype(BF16)


def pack_feet_kernel(chunks, mask_ref, coords_hbm, sigma_hbm, feet_ref, *rest):
    outs, (coords_ref, sigma_ref, feet, buf, head_v, small_sem, in_sem, sem) = (
        rest[: len(chunks)],
        rest[len(chunks) :],
    )
    blocks, rows = mask_ref.shape
    small = [
        pltpu.make_async_copy(src, dst, small_sem.at[k])
        for k, (src, dst) in enumerate(((coords_hbm, coords_ref), (sigma_hbm, sigma_ref)))
    ]
    for copy in small:
        copy.start()
    times, lanes = buf.shape[1:]
    groups = in_sem.shape[0]
    each = rows // groups
    loads = [
        pltpu.make_async_copy(feet_ref.at[pl.ds(g * each, each)], feet.at[pl.ds(g * each, each)], in_sem.at[g])
        for g in range(groups)
    ]
    for load in loads:
        load.start()
    for copy in small:
        copy.wait()
    sigma = sigma_ref[...]
    high = sigma.astype(BF16).astype(F32)
    middle = (sigma - high).astype(BF16).astype(F32)
    lowest = sigma - high - middle
    at = lax.broadcasted_iota(I32, (times, sigma.shape[1]), 0)
    info = jnp.zeros(at.shape, F32)
    for k, row in enumerate((coords_ref[0:1, :].astype(F32), coords_ref[1:2, :].astype(F32), high, middle, lowest)):
        info = jnp.where(at == k, row, info)
    info = info.astype(BF16)
    for b in range(blocks):
        buf[1 + b] = info[:, b * lanes : (b + 1) * lanes]
    carry = no_rows(1 + blocks, lanes)
    for g in range(groups):
        loads[g].wait()
        carry = pack_rows(
            lambda o, b: mask_ref[b, o],
            lambda o, b: feet[o, :, b * lanes : (b + 1) * lanes],
            g * each,
            (g + 1) * each,
            blocks,
            buf,
            carry,
        )
    write_head(carry, rows, blocks, buf, head_v)
    copies, first = [], 0
    for k, size in enumerate(chunks):
        copies.append(pltpu.make_async_copy(buf.at[pl.ds(first, size)], outs[k], sem.at[k]))
        first += size
    for copy in copies:
        copy.start()
    for copy in copies:
        copy.wait()


def pack_feet(mask, coords, sigma, feet, chunks):
    rows, times, cells = feet.shape
    lanes = cells // mask.shape[0]
    groups = math.gcd(4, rows)
    return pl.pallas_call(
        functools.partial(pack_feet_kernel, chunks),
        out_shape=tuple(shape_of((size, times, lanes), BF16) for size in chunks),
        in_specs=[SMEM, HBM, HBM, HBM],
        out_specs=(ANY,) * len(chunks),
        scratch_shapes=[
            pltpu.VMEM(coords.shape, I32),
            pltpu.VMEM(sigma.shape, F32),
            pltpu.VMEM((rows, times, cells), BF16),
            pltpu.VMEM((sum(chunks), times, lanes), BF16),
            pltpu.VMEM((times, lanes), F32),
            pltpu.SemaphoreType.DMA((2,)),
            pltpu.SemaphoreType.DMA((groups,)),
            pltpu.SemaphoreType.DMA((len(chunks),)),
        ],
        compiler_params=params(12),
        cost_estimate=cost(3),
        name="pack_feet",
    )(mask, coords, sigma, feet)


def pack_panel_kernel(room, mask_ref, mask_hbm, index_ref, group_ref, feet_ref, out_ref, mask_v, rows_buf, head_v, small_sem, sem):
    count = rows_buf.shape[0]
    blocks, obs = mask_ref.shape
    lanes = out_ref.shape[2]
    mask_copy = pltpu.make_async_copy(mask_hbm, mask_v, small_sem.at[0])
    mask_copy.start()
    base = group_ref[0]
    rows = [jnp.clip(index_ref[base * count + j] - base * obs, 0, obs - 1) for j in range(count)]
    copies = [pltpu.make_async_copy(feet_ref.at[rows[j]], rows_buf.at[j], sem.at[j]) for j in range(count)]
    for copy in copies:
        copy.start()
    mask_copy.wait()
    flag = (jnp.sum(mask_v[...].astype(F32), axis=(0, 1), keepdims=True) > room).astype(I32)
    for copy in copies:
        copy.wait()

    def mask_at(o, b):
        return mask_ref[b, jnp.clip(index_ref[base * count + o] - base * obs, 0, obs - 1)]

    carry = pack_rows(
        mask_at, lambda o, b: rows_buf[o, :, b * lanes : (b + 1) * lanes], 0, count, blocks, out_ref, no_rows(1, lanes)
    )
    write_head(carry, count, blocks, out_ref, head_v, flag)


def pack_panel(mask, panel_index, group, feet, count, slots, room):
    _, times, cells = feet.shape
    lanes = cells // mask.shape[0]
    return pl.pallas_call(
        functools.partial(pack_panel_kernel, room),
        out_shape=shape_of((slots, times, lanes), BF16),
        in_specs=[SMEM, HBM, SMEM, SMEM, HBM],
        out_specs=VMEM,
        scratch_shapes=[
            pltpu.VMEM(mask.shape, I32),
            pltpu.VMEM((count, times, cells), BF16),
            pltpu.VMEM((times, lanes), F32),
            pltpu.SemaphoreType.DMA((1,)),
            pltpu.SemaphoreType.DMA((count,)),
        ],
        compiler_params=params(8),
        cost_estimate=cost(2),
        name="pack_panel",
    )(mask, mask, panel_index, group[None], feet)


def fetch(chunks, buf, sem):
    copies, first = [], 0
    for k, chunk in enumerate(chunks):
        copies.append(pltpu.make_async_copy(chunk, buf.at[pl.ds(first, chunk.shape[0])], sem.at[k]))
        copies[-1].start()
        first += chunk.shape[0]
    return copies


def read_head(buf, rows, blocks, bits_v, flagged=False):
    slots, _, lanes = buf.shape
    deep = -(-rows * blocks // lanes)
    head = buf[0].astype(F32)
    scale = float(1 << SHIFT)
    bits_v[0:deep, :] = jnp.minimum(head[0:deep] * scale + head[deep : 2 * deep], slots - 1.0).astype(I32)
    bits_v[deep : deep + 1, :] = (head[2 * deep : 2 * deep + 1] * scale + head[2 * deep + 1 : 2 * deep + 2]).astype(I32)
    if flagged:
        bits_v[deep + 1 : deep + 2, :] = head[2 * deep + 2 : 2 * deep + 3].astype(I32)
    buf[0] = jnp.zeros(buf.shape[1:], buf.dtype)


def copy_in(src, dst, sem):
    copy = pltpu.make_async_copy(src, dst, sem)
    copy.start()
    copy.wait()


def expand(buf, bits, first, count, blocks, store, unrolled=False):
    lanes = buf.shape[2]
    batch = math.gcd(2, count)

    def some(i, _):
        tiles = []
        for j in range(batch):
            base = (first + i * batch + j) * blocks
            row, col = lax.div(base, lanes), lax.rem(base, lanes)
            tiles += [buf[bits[row, col + b]] for b in range(blocks)]
        for j in range(batch):
            for b in range(blocks):
                store(i * batch + j, b, tiles[j * blocks + b])
        return 0

    if unrolled:
        for i in range(count // batch):
            some(i, 0)
    else:
        lax.fori_loop(0, count // batch, some, 0)


def into(dense, times, lanes, offset, first=0):
    def store(i, b, tile):
        at = aligned((first + i) * times, times)
        dense[at, offset + b * lanes : offset + (b + 1) * lanes] = tile.astype(dense.dtype)

    return store


def read_info(buf, blocks, row_v, turned):
    _, lanes = buf.shape[1:]
    for b in range(blocks):
        tile = buf[1 + b].astype(F32)[0:INFO]
        sigma = tile[2:3] + tile[3:4] + tile[4:5]
        tile = jnp.where(lax.broadcasted_iota(I32, tile.shape, 0) == 2, sigma, tile)
        at = slice(b * lanes, (b + 1) * lanes)
        if row_v is not None:
            row_v[:, at] = tile
        if turned is not None:
            turned[at, :] = tile.T


def fill_covariance(dst, dst_first, src_first, rows, turned, own):
    x, y, s = own[0:1, :], own[1:2, :], own[2:3, :]
    step = min(32, rows)
    for i in range(rows // step):
        at = aligned(src_first + i * step, step)
        dx = turned[at, 0:1] - x
        dy = turned[at, 1:2] - y
        square = dx * dx + dy * dy + 1.0
        decay = jnp.exp(square * lax.rsqrt(square) * (-1.0 / LENGTH))
        dst[aligned(dst_first + i * step, step), :] = (decay * (turned[at, 2:3] * s)).astype(BF16)


def own_kernel(chunks, *refs):
    msgs = refs[:chunks], refs[chunks : 2 * chunks]
    out_ref, mate_dense, next_ref, info_ref = refs[2 * chunks : 2 * chunks + 4]
    bufs, bits_v, bits_s, dense, cov, turned, sem = refs[2 * chunks + 4 :]
    times, lanes = bufs.shape[2:]
    cells = cov.shape[1]
    blocks = cells // lanes
    rows = dense.shape[0] // times
    tall = min(256, rows * times)
    steps = rows * times // tall
    part = cells // steps
    copies = [fetch(msg, bufs.at[k], sem.at[k]) for k, msg in enumerate(msgs)]
    for k in range(2):
        for copy in copies[k]:
            copy.wait()
        read_info(bufs.at[k], blocks, None if k else info_ref, turned.at[k])
        read_head(bufs.at[k], rows, blocks, bits_v.at[k])
    copy_in(bits_v, bits_s, sem.at[2, 0])
    fine = math.gcd(8, rows // 2)
    piece = cells // fine

    @pl.loop(0, fine)
    def _(i):
        fill_covariance(cov, i * piece, i * piece, piece, turned.at[0], info_ref)
        some = rows // fine
        expand(bufs.at[0], bits_s.at[0], i * some, some, blocks, into(dense, times, lanes, 0, i * some), unrolled=True)

    @pl.loop(0, steps)
    def _(u):
        here = aligned(u * tall, tall)
        fill_covariance(next_ref, u * part, u * part, part, turned.at[1], info_ref)
        out_ref[here, :] = jnp.dot(dense[here, :], cov[...], preferred_element_type=F32)
        some = rows // steps
        expand(bufs.at[1], bits_s.at[1], u * some, some, blocks, into(mate_dense, times, lanes, 0, u * some), unrolled=True)


def own_call(own_msg, mate_msg, rows, cells):
    times, lanes = own_msg[0].shape[1:]
    slots = sum(chunk.shape[0] for chunk in own_msg)
    chunks = len(own_msg)
    return pl.pallas_call(
        functools.partial(own_kernel, chunks),
        out_shape=(
            shape_of((rows * times, cells), F32),
            shape_of((rows * times, cells), BF16),
            shape_of((cells, cells), BF16),
            shape_of((INFO, cells), F32),
        ),
        in_specs=[ANY] * (2 * chunks),
        out_specs=(VMEM,) * 4,
        scratch_shapes=[
            pltpu.VMEM((2, slots, times, lanes), BF16),
            pltpu.VMEM((2, 8, lanes), I32),
            pltpu.SMEM((2, 8, lanes), I32),
            pltpu.VMEM((rows * times, cells), BF16),
            pltpu.VMEM((cells, cells), BF16),
            pltpu.VMEM((2, cells, INFO), F32),
            pltpu.SemaphoreType.DMA((3, chunks)),
        ],
        compiler_params=params(16),
        cost_estimate=cost(9),
        name="own_product",
    )(*own_msg, *mate_msg)


def mate_kernel(count, *refs):
    firsts = refs[:count]
    near_ref, dense, cov_ref, info_ref, out_ref, far_ref, info_buf, turned, sem = refs[count:]
    _, lanes = info_buf.shape[2:]
    cells = cov_ref.shape[1]
    blocks = cells // lanes
    tall = min(256, dense.shape[0])
    steps = dense.shape[0] // tall
    part = count * cells // steps
    copies = []
    for k in range(count):
        copies.append(pltpu.make_async_copy(firsts[k].at[pl.ds(0, 1 + blocks)], info_buf.at[k], sem.at[k]))
        copies[-1].start()
    for k in range(count):
        copies[k].wait()
        read_info(info_buf.at[k], blocks, None, turned.at[pl.ds(k * cells, cells)])

    @pl.loop(0, steps)
    def _(u):
        here = aligned(u * tall, tall)
        fill_covariance(far_ref, u * part, u * part, part, turned, info_ref)
        out_ref[here, :] = near_ref[here, :] + jnp.dot(dense[here, :], cov_ref[...], preferred_element_type=F32)


def mate_call(firsts, near, mate_dense, cov, info):
    times, lanes = firsts[0].shape[1:]
    cells = cov.shape[1]
    blocks = cells // lanes
    count = len(firsts)
    return pl.pallas_call(
        functools.partial(mate_kernel, count),
        out_shape=(shape_of(near.shape, F32), shape_of((count * cells, cells), BF16)),
        in_specs=[ANY] * count + [VMEM] * 4,
        out_specs=(VMEM, VMEM),
        scratch_shapes=[
            pltpu.VMEM((count, 1 + blocks, times, lanes), BF16),
            pltpu.VMEM((count * cells, INFO), F32),
            pltpu.SemaphoreType.DMA((count,)),
        ],
        input_output_aliases={count: 0},
        compiler_params=params(16),
        cost_estimate=cost(8),
        name="mate_product",
    )(*firsts, near, mate_dense, cov, info)


def mixed_unit(mix_ref, value):
    high = value.astype(BF16)
    low = (value - high.astype(F32)).astype(BF16)
    stacked = jnp.concatenate([high, low, high], axis=0)
    return jnp.dot(mix_ref[...], stacked, preferred_element_type=F32).astype(BF16)


def turn(value, rows, times):
    return jnp.swapaxes(value.reshape(rows, times, value.shape[1]), 0, 1)


def rows_kernel(count, chunks, unit, late, *refs):
    msgs = [refs[k * chunks : (k + 1) * chunks] for k in range(count)]
    refs = refs[count * chunks :]
    cov_ref, near_ref, mix_ref = refs[:3]
    if late:
        start_ref, done_ref, out_ref, turned_ref = refs[3:7]
    else:
        out_ref, next_ref = refs[3:5]
    bufs, bits_v, bits_s, dense, sem = refs[-5:]
    times, lanes = bufs.shape[2:]
    cells = near_ref.shape[1]
    blocks = cells // lanes
    rows = out_ref.shape[0]
    deep = -(-rows * blocks // lanes)
    copies = [fetch(msgs[k], bufs.at[k], sem.at[k]) for k in range(count)]
    for k in range(count):
        for copy in copies[k]:
            copy.wait()
        read_head(bufs.at[k], rows, blocks, bits_v.at[k])
    copy = pltpu.make_async_copy(bits_v, bits_s, sem.at[count, 0])
    copy.start()

    def step(u, _):
        for k in range(count):
            expand(bufs.at[k], bits_s.at[k], u * unit, unit, blocks, into(dense, times, lanes, k * cells))
        here = aligned(u * unit * times, unit * times)
        value = near_ref[here, :] + jnp.dot(dense[...], cov_ref[...], preferred_element_type=F32)
        mixed = mixed_unit(mix_ref, value)
        at = aligned(u * unit, unit)
        out_ref[at] = mixed.reshape(unit, times, cells)
        if late:
            turned_ref[:, at, :] = turn(mixed, unit, times)
        return 0

    def carry_over(u, _):
        at = aligned(u * unit, unit)
        value = done_ref[at]
        out_ref[at] = value
        turned_ref[:, at, :] = turn(value.reshape(unit * times, cells), unit, times)
        return 0

    if late:
        first = start_ref[0]
        lax.fori_loop(0, first, carry_over, 0)
        copy.wait()
        lax.fori_loop(first, rows // unit, step, 0)
    else:
        copy.wait()
        limit = sum(chunk.shape[0] for chunk in msgs[0])
        ready = jnp.int32(0)
        for u in range(rows // unit):
            whole = jnp.int32(1)
            for k in range(count):
                whole = whole * (bits_s[k, deep, (u + 1) * unit - 1] <= limit).astype(I32)
            ready = ready + whole
        next_ref[0] = ready
        lax.fori_loop(0, ready, step, 0)


def some_rows(msgs, cov, near, mix, rows, unit, slots, carried=None):
    times, lanes = msgs[0][0].shape[1:]
    cells = near.shape[1]
    count, chunks = len(msgs), len(msgs[0])
    late = carried is not None
    flat = [chunk for msg in msgs for chunk in msg]
    out = shape_of((rows, times, cells), BF16)
    return pl.pallas_call(
        functools.partial(rows_kernel, count, chunks, unit, late),
        out_shape=(out, shape_of((times, rows, cells), BF16) if late else shape_of((1,), I32)),
        in_specs=[ANY] * len(flat) + [VMEM] * 3 + ([SMEM, VMEM] if late else []),
        out_specs=(VMEM, VMEM if late else SMEM),
        scratch_shapes=[
            pltpu.VMEM((count, slots, times, lanes), BF16),
            pltpu.VMEM((count, 8, lanes), I32),
            pltpu.SMEM((count, 8, lanes), I32),
            pltpu.VMEM((unit * times, count * cells), BF16),
            pltpu.SemaphoreType.DMA((count + 1, chunks)),
        ],
        compiler_params=params(16),
        cost_estimate=cost(6),
        name="late_rows" if late else "first_rows",
    )(*flat, cov, near, mix, *(carried or ()))


def mix_kernel(unit, time_ref, out_ref):
    times = time_ref.shape[0]
    size = unit * times
    value = time_ref[...]
    high = value.astype(BF16)
    low = (value - high.astype(F32)).astype(BF16)

    def same(shape, dim):
        index = lax.broadcasted_iota(I32, shape, 1 - dim) % times
        return (index == lax.broadcasted_iota(I32, shape, dim)).astype(F32).astype(BF16)

    row = lax.broadcasted_iota(I32, (size, size), 0)
    col = lax.broadcasted_iota(I32, (size, size), 1)
    for j, part in enumerate((high, high, low)):
        spread = jnp.dot(same((size, times), 1), part, preferred_element_type=F32).astype(BF16)
        spread = jnp.dot(spread, same((times, size), 0), preferred_element_type=F32)
        out_ref[:, j * size : (j + 1) * size] = jnp.where(row // times == col // times, spread, 0.0).astype(BF16)


def mixing(time_cov, unit):
    size = unit * time_cov.shape[0]
    return pl.pallas_call(
        functools.partial(mix_kernel, unit),
        out_shape=shape_of((size, 3 * size), BF16),
        in_specs=[VMEM],
        out_specs=VMEM,
        compiler_params=params(8),
        cost_estimate=cost(1),
        name="mixing",
    )(time_cov)


def panel_kernel(pieces, each, final, *refs):
    msgs = refs[:pieces]
    refs = refs[pieces:]
    if final:
        sources_ref, turned, before_ref, over_ref, out_ref = refs[:5]
    else:
        turned, out_ref, over_ref = refs[:3]
    bufs, bits_v, bits_s, panel, sem = refs[-5:]
    slots, times, lanes = bufs.shape[1:]
    rows, cells = turned.shape[1:]
    blocks = cells // lanes
    deep = -(-each * blocks // lanes)
    copies = [pltpu.make_async_copy(msg, bufs.at[k], sem.at[k]) for k, msg in enumerate(msgs)]
    for copy in copies:
        copy.start()
    for k, copy in enumerate(copies):
        copy.wait()
        read_head(bufs.at[k], each, blocks, bits_v.at[k], flagged=True)
    copy_in(bits_v, bits_s, sem.at[pieces])
    over = over_ref[0] if final else jnp.int32(0)
    for k in range(pieces):
        over = over + (bits_s[k, deep, each - 1] > slots - 1).astype(I32) + bits_s[k, deep + 1, 0]
    group = max(1, 16 // each)

    @pl.loop(0, pieces // group)
    def _(g):
        for b in range(blocks):
            tiles = []
            for i in range(group * each):
                k, place = g * group + i // each, i % each * blocks + b
                tiles.append(bufs[k, bits_s[k, place // lanes, place % lanes]])
            value = turn(jnp.concatenate(tiles, axis=0), group * each, times)
            panel[:, aligned(g * group * each, group * each), b * lanes : (b + 1) * lanes] = value

    total = None
    for t in range(times):
        value = lax.dot_general(turned[t], panel[t], (((1,), (1,)), ((), ())), preferred_element_type=F32)
        total = value if total is None else total + value
    if not final:
        out_ref[...] = total
        over_ref[0] = over
        return
    value = jnp.concatenate([before_ref[...], total], axis=1)
    size = value.shape[1]
    row = lax.broadcasted_iota(I32, (size, size), 0)
    target = row
    for k in range(size // each):
        target = jnp.where(row // each == k, sources_ref[k] * each + row % each, target)
    select = (lax.broadcasted_iota(I32, (size, size), 1) == target).astype(F32).astype(BF16)
    total = jnp.zeros(value.shape, F32)
    for _ in range(3):
        high = value.astype(BF16)
        total = total + jnp.dot(high, select, preferred_element_type=F32)
        value = value - high.astype(F32)
    out_ref[0:rows, :] = total
    out_ref[rows:, :] = jnp.broadcast_to(over, (8, size)).astype(F32)


def panel_part(msgs, turned, each, final=None):
    slots, times, lanes = msgs[0].shape
    rows, cells = turned.shape[1:]
    pieces = len(msgs)
    width = pieces * each
    if final:
        sources, before, over = final
        operands, in_specs = (sources, turned, before, over), [SMEM, VMEM, VMEM, SMEM]
        out_shape = shape_of((rows + 8, before.shape[1] + width), F32)
        out_specs = VMEM
    else:
        operands, in_specs = (turned,), [VMEM]
        out_shape, out_specs = (shape_of((rows, width), F32), shape_of((1,), I32)), (VMEM, SMEM)
    return pl.pallas_call(
        functools.partial(panel_kernel, pieces, each, bool(final)),
        out_shape=out_shape,
        in_specs=[ANY] * pieces + in_specs,
        out_specs=out_specs,
        scratch_shapes=[
            pltpu.VMEM((pieces, slots, times, lanes), BF16),
            pltpu.VMEM((pieces, 8, lanes), I32),
            pltpu.SMEM((pieces, 8, lanes), I32),
            pltpu.VMEM((times, width, cells), BF16),
            pltpu.SemaphoreType.DMA((pieces + 1,)),
        ],
        compiler_params=params(14),
        cost_estimate=cost(3 if final else 5),
        name="panel_last" if final else "panel_first",
    )(*msgs, *operands)


def partner(value, axis, count):
    return lax.ppermute(value, axis, [(i, i ^ 1) for i in range(count)])


def shifted(value, axis, count, shift, flip=0):
    return lax.ppermute(value, axis, [(i, ((i + 2 * shift) % count) ^ flip) for i in range(count)])


def add_cells(part, cells):
    total = part
    for shift in range(cells // 2):
        for flip in range(2):
            if shift or flip:
                total = total + shifted(part, "cell", cells, shift, flip)
    return total


def dense_way(cells, observers, footprint, block_mask, own, time_cov, mine, sources):
    obs_rows, times, cell_local = footprint.shape
    blocks = block_mask.shape[1]
    keep = block_mask.astype(BF16)[:, None, :, None]
    feet = (footprint.reshape(obs_rows, times, blocks, cell_local // blocks) * keep).reshape(footprint.shape)

    def add(carry, _):
        total, feet, info = carry
        dx = info[0][:, None] - own[0][None, :]
        dy = info[1][:, None] - own[1][None, :]
        decay = jnp.exp(-jnp.sqrt(dx * dx + dy * dy + 1.0) / LENGTH)
        cov = (decay * (info[2][:, None] * own[2][None, :])).astype(BF16)
        total = total + jnp.dot(feet.reshape(-1, cell_local), cov, preferred_element_type=F32)
        ring = [(i, (i + 1) % cells) for i in range(cells)]
        return (total, lax.ppermute(feet, "cell", ring), lax.ppermute(info, "cell", ring)), None

    zero = jnp.zeros((obs_rows * times, cell_local), F32)
    (total, _, _), _ = lax.scan(add, (zero, feet, own), None, length=cells)
    cov_product = jnp.einsum(
        "ts,ksc->ktc", time_cov, total.reshape(obs_rows, times, cell_local), precision=lax.Precision.HIGHEST
    ).astype(BF16)
    flat = cov_product.reshape(obs_rows, times * cell_local)

    def meet(held, _):
        both = jnp.concatenate([held, partner(held, "obs", observers)], axis=0)
        part = lax.dot_general(
            flat, both.reshape(both.shape[0], -1), (((1,), (1,)), ((), ())), preferred_element_type=F32
        )
        return shifted(held, "obs", observers, 1), part

    _, parts = lax.scan(meet, jnp.take(feet, mine, axis=0), None, length=observers // 2)
    parts = parts.transpose(1, 0, 2).reshape(obs_rows, observers, -1)
    ordered = jnp.zeros_like(parts).at[:, sources].set(parts)
    return cov_product, add_cells(ordered.reshape(obs_rows, -1), cells)


def body(cells, observers, footprint, block_mask, cell_coords, cell_sigma, time_cov, error_var, panel_index):
    obs_rows, _, cell_local = footprint.shape
    blocks = block_mask.shape[1]
    group = lax.axis_index("obs")
    each = panel_index.shape[0] // observers
    half = observers // 2
    unit = math.gcd(16, obs_rows)
    slots = slot_count(obs_rows * blocks, 1 + blocks)
    chunks = (slots - slots // 2, slots // 2)
    mask = block_mask.T
    order = jnp.arange(observers, dtype=I32)
    sources = (group // 2 - order // 2) % half * 2 + (group % 2 ^ (order % 2))

    room = slots - 2 - blocks - 1
    own_panel = pack_panel(mask, panel_index, group, footprint, each, slot_count(each * blocks, 1), room)
    ring = [own_panel]
    for _ in range(1, half):
        ring.append(shifted(ring[-1], "obs", observers, 1))
    messages = []
    for held in ring:
        messages += [held, partner(held, "obs", observers)]
    own_msg = pack_feet(mask, cell_coords, cell_sigma[None, :], footprint, chunks)
    far_msgs = []
    for shift in range(1, cells // 2):
        far_msgs.append([shifted(c, "cell", cells, shift) for c in own_msg])
    mate_msg = [partner(c, "cell", cells) for c in own_msg]
    for shift in range(1, cells // 2):
        far_msgs.append([partner(c, "cell", cells) for c in far_msgs[shift - 1]])

    near, mate_dense, mate_cov, info = own_call(own_msg, mate_msg, obs_rows, cell_local)
    near, far_cov = mate_call([msg[0] for msg in far_msgs], near, mate_dense, mate_cov, info)
    mix = mixing(time_cov, unit)
    first_cov, start = some_rows([msg[:1] for msg in far_msgs], far_cov, near, mix, obs_rows, unit, slots)
    cov_product, turned = some_rows(far_msgs, far_cov, near, mix, obs_rows, unit, slots, (start, first_cov))
    cut = len(messages) * 3 // 4
    before, over = panel_part(messages[:cut], turned, each)
    part = panel_part(messages[cut:], turned, each, (sources, before, over))

    def innovation_of(total):
        positions = jnp.arange(obs_rows, dtype=I32)
        on_diagonal = ((group * obs_rows + positions)[:, None] == panel_index[None, :]).astype(F32)
        return total + error_var[:, None] * on_diagonal

    total = add_cells(part, cells)

    def again(carry):
        wanted = carry[0]
        mask, cell_info, place, from_group = (
            jnp.where(wanted, value, 0) for value in (block_mask, info, group, sources)
        )
        mine = lax.dynamic_slice_in_dim(panel_index, place * each, each) - place * obs_rows
        cov_product, total = dense_way(
            cells, observers, footprint, mask, cell_info, time_cov, mine, from_group
        )
        return jnp.bool_(False), cov_product, innovation_of(total)

    carry = (total[obs_rows, 0] > 0, cov_product, innovation_of(total[:obs_rows]))
    return lax.while_loop(lambda carry: carry[0], again, carry)[1:]


def solution(mesh):
    in_specs = (
        P("obs", None, "cell"),
        P("obs", "cell"),
        P(None, "cell"),
        P("cell"),
        P(),
        P("obs"),
        P(),
    )
    out_specs = (P("obs", None, "cell"), P("obs", None))
    cells, observers = mesh.shape["cell"], mesh.shape["obs"]

    def per_device(*args):
        return body(cells, observers, *args)

    return jax.shard_map(per_device, mesh=mesh, in_specs=in_specs, out_specs=out_specs, check_vma=False)
```

```python
import functools
import math

import jax
import jax.numpy as jnp
from jax import lax
from jax.experimental import pallas as pl
from jax.experimental.pallas import tpu as pltpu
from jax.experimental.layout import Layout, with_layout_constraint
from jax.sharding import PartitionSpec as P


GRID = 64
LENGTH = GRID / 16.0
F32, BF16, I32 = jnp.float32, jnp.bfloat16, jnp.int32
SHIFT = 4
INFO = 8


VMEM = pl.BlockSpec(memory_space=pltpu.VMEM)
SMEM = pl.BlockSpec(memory_space=pltpu.SMEM)
ANY = pl.BlockSpec(memory_space=pl.ANY)
HBM = pl.BlockSpec(memory_space=pltpu.HBM)


def shape_of(shape, dtype):
    return jax.ShapeDtypeStruct(shape, dtype)


def params(mib):
    return pltpu.CompilerParams(vmem_limit_bytes=mib * 2**20)


def cost(micros):
    return pl.CostEstimate(flops=int(micros * 9e8), bytes_accessed=1_000_000, transcendentals=0)


def aligned(start, size):
    return pl.ds(pl.multiple_of(start, size), size)


def slot_count(tiles, extra):
    room = tiles / 2 + 4.1 * math.sqrt(tiles / 4)
    return extra + min(tiles + 1, 2 * math.ceil(room / 2) + 1)


def pack_rows(mask_at, feet_at, begin, end, blocks, buf, carry):
    slots, _, lanes = buf.shape
    row_of = lax.broadcasted_iota(I32, (8, lanes), 0)
    lane_of = lax.broadcasted_iota(I32, (8, lanes), 1)
    flat = row_of * lanes + lane_of
    batch = math.gcd(2, end - begin)

    def some(i, carry):
        pos, head, ends = carry
        first = begin + i * batch
        tiles = [[feet_at(first + j, b) for b in range(blocks)] for j in range(batch)]
        kept = [[mask_at(first + j, b) for b in range(blocks)] for j in range(batch)]
        for j in range(batch):
            for b in range(blocks):
                buf[jnp.minimum(pos, slots - 1)] = tiles[j][b]
                head = jnp.where(flat == (first + j) * blocks + b, kept[j][b] * pos, head)
                pos = pos + kept[j][b]
            ends = jnp.where(lane_of == first + j, pos, ends)
        return pos, head, ends

    return lax.fori_loop(0, (end - begin) // batch, some, carry)


def no_rows(first, lanes):
    zeros = jnp.zeros((8, lanes), I32)
    return jnp.int32(first), zeros, zeros


def write_head(carry, rows, blocks, buf, head_v, flag=None):
    lanes = buf.shape[2]
    deep = -(-rows * blocks // lanes)
    _, head, ends = carry
    low = (1 << SHIFT) - 1
    head_v[...] = jnp.zeros_like(head_v)
    head_v[0:deep, :] = (head >> SHIFT)[0:deep].astype(F32)
    head_v[deep : 2 * deep, :] = (head & low)[0:deep].astype(F32)
    head_v[2 * deep : 2 * deep + 1, :] = (ends >> SHIFT)[0:1].astype(F32)
    head_v[2 * deep + 1 : 2 * deep + 2, :] = (ends & low)[0:1].astype(F32)
    if flag is not None:
        head_v[2 * deep + 2 : 2 * deep + 3, :] = jnp.broadcast_to(flag, (1, lanes)).astype(F32)
    buf[0] = head_v[...].astype(BF16)


def pack_feet_kernel(chunks, mask_ref, coords_hbm, sigma_hbm, feet_ref, *rest):
    outs, (coords_ref, sigma_ref, feet, buf, head_v, small_sem, in_sem, sem) = (
        rest[: len(chunks)],
        rest[len(chunks) :],
    )
    blocks, rows = mask_ref.shape
    small = [
        pltpu.make_async_copy(src, dst, small_sem.at[k])
        for k, (src, dst) in enumerate(((coords_hbm, coords_ref), (sigma_hbm, sigma_ref)))
    ]
    for copy in small:
        copy.start()
    times, lanes = buf.shape[1:]
    groups = in_sem.shape[0]
    each = rows // groups
    loads = [
        pltpu.make_async_copy(feet_ref.at[pl.ds(g * each, each)], feet.at[pl.ds(g * each, each)], in_sem.at[g])
        for g in range(groups)
    ]
    for load in loads:
        load.start()
    for copy in small:
        copy.wait()
    sigma = sigma_ref[...]
    high = sigma.astype(BF16).astype(F32)
    middle = (sigma - high).astype(BF16).astype(F32)
    lowest = sigma - high - middle
    at = lax.broadcasted_iota(I32, (times, sigma.shape[1]), 0)
    info = jnp.zeros(at.shape, F32)
    for k, row in enumerate((coords_ref[0:1, :].astype(F32), coords_ref[1:2, :].astype(F32), high, middle, lowest)):
        info = jnp.where(at == k, row, info)
    info = info.astype(BF16)
    for b in range(blocks):
        buf[1 + b] = info[:, b * lanes : (b + 1) * lanes]
    carry = no_rows(1 + blocks, lanes)
    for g in range(groups):
        loads[g].wait()
        carry = pack_rows(
            lambda o, b: mask_ref[b, o],
            lambda o, b: feet[o, :, b * lanes : (b + 1) * lanes],
            g * each,
            (g + 1) * each,
            blocks,
            buf,
            carry,
        )
    write_head(carry, rows, blocks, buf, head_v)
    copies, first = [], 0
    for k, size in enumerate(chunks):
        copies.append(pltpu.make_async_copy(buf.at[pl.ds(first, size)], outs[k], sem.at[k]))
        first += size
    for copy in copies:
        copy.start()
    for copy in copies:
        copy.wait()


def pack_feet(mask, coords, sigma, feet, chunks):
    rows, times, cells = feet.shape
    lanes = cells // mask.shape[0]
    groups = math.gcd(4, rows)
    return pl.pallas_call(
        functools.partial(pack_feet_kernel, chunks),
        out_shape=tuple(shape_of((size, times, lanes), BF16) for size in chunks),
        in_specs=[SMEM, HBM, HBM, HBM],
        out_specs=(ANY,) * len(chunks),
        scratch_shapes=[
            pltpu.VMEM(coords.shape, I32),
            pltpu.VMEM(sigma.shape, F32),
            pltpu.VMEM((rows, times, cells), BF16),
            pltpu.VMEM((sum(chunks), times, lanes), BF16),
            pltpu.VMEM((times, lanes), F32),
            pltpu.SemaphoreType.DMA((2,)),
            pltpu.SemaphoreType.DMA((groups,)),
            pltpu.SemaphoreType.DMA((len(chunks),)),
        ],
        compiler_params=params(12),
        cost_estimate=cost(3),
        name="pack_feet",
    )(mask, coords, sigma, feet)


def pack_panel_kernel(room, mask_ref, mask_hbm, index_ref, group_ref, feet_ref, out_ref, mask_v, rows_buf, head_v, small_sem, sem):
    count = rows_buf.shape[0]
    blocks, obs = mask_ref.shape
    lanes = out_ref.shape[2]
    mask_copy = pltpu.make_async_copy(mask_hbm, mask_v, small_sem.at[0])
    mask_copy.start()
    base = group_ref[0]
    rows = [jnp.clip(index_ref[base * count + j] - base * obs, 0, obs - 1) for j in range(count)]
    copies = [pltpu.make_async_copy(feet_ref.at[rows[j]], rows_buf.at[j], sem.at[j]) for j in range(count)]
    for copy in copies:
        copy.start()
    mask_copy.wait()
    flag = (jnp.sum(mask_v[...].astype(F32), axis=(0, 1), keepdims=True) > room).astype(I32)
    for copy in copies:
        copy.wait()

    def mask_at(o, b):
        return mask_ref[b, jnp.clip(index_ref[base * count + o] - base * obs, 0, obs - 1)]

    carry = pack_rows(
        mask_at, lambda o, b: rows_buf[o, :, b * lanes : (b + 1) * lanes], 0, count, blocks, out_ref, no_rows(1, lanes)
    )
    write_head(carry, count, blocks, out_ref, head_v, flag)


def pack_panel(mask, panel_index, group, feet, count, slots, room):
    _, times, cells = feet.shape
    lanes = cells // mask.shape[0]
    return pl.pallas_call(
        functools.partial(pack_panel_kernel, room),
        out_shape=shape_of((slots, times, lanes), BF16),
        in_specs=[SMEM, HBM, SMEM, SMEM, HBM],
        out_specs=VMEM,
        scratch_shapes=[
            pltpu.VMEM(mask.shape, I32),
            pltpu.VMEM((count, times, cells), BF16),
            pltpu.VMEM((times, lanes), F32),
            pltpu.SemaphoreType.DMA((1,)),
            pltpu.SemaphoreType.DMA((count,)),
        ],
        compiler_params=params(8),
        cost_estimate=cost(2),
        name="pack_panel",
    )(mask, mask, panel_index, group[None], feet)


def fetch(chunks, buf, sem):
    copies, first = [], 0
    for k, chunk in enumerate(chunks):
        copies.append(pltpu.make_async_copy(chunk, buf.at[pl.ds(first, chunk.shape[0])], sem.at[k]))
        copies[-1].start()
        first += chunk.shape[0]
    return copies


def read_head(buf, rows, blocks, bits_v, flagged=False):
    slots, _, lanes = buf.shape
    deep = -(-rows * blocks // lanes)
    head = buf[0].astype(F32)
    scale = float(1 << SHIFT)
    bits_v[0:deep, :] = jnp.minimum(head[0:deep] * scale + head[deep : 2 * deep], slots - 1.0).astype(I32)
    bits_v[deep : deep + 1, :] = (head[2 * deep : 2 * deep + 1] * scale + head[2 * deep + 1 : 2 * deep + 2]).astype(I32)
    if flagged:
        bits_v[deep + 1 : deep + 2, :] = head[2 * deep + 2 : 2 * deep + 3].astype(I32)
    buf[0] = jnp.zeros(buf.shape[1:], buf.dtype)


def copy_in(src, dst, sem):
    copy = pltpu.make_async_copy(src, dst, sem)
    copy.start()
    copy.wait()


def split(number, size):
    if size & (size - 1):
        return lax.div(number, size), lax.rem(number, size)
    return lax.shift_right_logical(number, size.bit_length() - 1), lax.bitwise_and(number, size - 1)


def expand(buf, bits, first, count, blocks, store, unrolled=False):
    lanes = buf.shape[2]
    batch = math.gcd(2, count)

    def some(i, _):
        tiles = []
        for j in range(batch):
            row, col = split(jnp.int32((first + i * batch + j) * blocks), lanes)
            tiles += [buf[bits[row, col + b]] for b in range(blocks)]
        for j in range(batch):
            for b in range(blocks):
                store(i * batch + j, b, tiles[j * blocks + b])
        return 0

    if unrolled:
        for i in range(count // batch):
            some(i, 0)
    else:
        lax.fori_loop(0, count // batch, some, 0)


def into(dense, times, lanes, offset, first=0):
    def store(i, b, tile):
        at = aligned((first + i) * times, times)
        dense[at, offset + b * lanes : offset + (b + 1) * lanes] = tile.astype(dense.dtype)

    return store


def read_info(buf, blocks, row_v, turned):
    _, lanes = buf.shape[1:]
    for b in range(blocks):
        tile = buf[1 + b].astype(F32)[0:INFO]
        sigma = tile[2:3] + tile[3:4] + tile[4:5]
        tile = jnp.where(lax.broadcasted_iota(I32, tile.shape, 0) == 2, sigma, tile)
        at = slice(b * lanes, (b + 1) * lanes)
        if row_v is not None:
            row_v[:, at] = tile
        if turned is not None:
            turned[at, :] = tile.T


def fill_covariance(dst, dst_first, src_first, rows, turned, own):
    x, y, s = own[0:1, :], own[1:2, :], own[2:3, :]
    step = min(32, rows)
    for i in range(rows // step):
        at = aligned(src_first + i * step, step)
        dx = turned[at, 0:1] - x
        dy = turned[at, 1:2] - y
        square = dx * dx + dy * dy + 1.0
        decay = jnp.exp(square * lax.rsqrt(square) * (-1.0 / LENGTH))
        dst[aligned(dst_first + i * step, step), :] = (decay * (turned[at, 2:3] * s)).astype(BF16)


def start_kernel(chunks, *refs):
    msg = refs[:chunks]
    dense, cov, info_ref, buf, bits_v, bits_s, turned, sem = refs[chunks:]
    times, lanes = buf.shape[1:]
    cells = cov.shape[1]
    blocks = cells // lanes
    rows = dense.shape[0] // times
    copies = fetch(msg, buf, sem)
    for copy in copies:
        copy.wait()
    read_info(buf, blocks, info_ref, turned)
    read_head(buf, rows, blocks, bits_v)
    copy = pltpu.make_async_copy(bits_v, bits_s, sem.at[chunks])
    copy.start()
    half = cells // 2
    fine = math.gcd(4, rows // 2)

    @pl.loop(0, fine)
    def _(i):
        fill_covariance(cov, i * (half // fine), i * (half // fine), half // fine, turned, info_ref)

    copy.wait()

    @pl.loop(0, fine)
    def _(i):
        first = half + i * (half // fine)
        fill_covariance(cov, first, first, half // fine, turned, info_ref)
        some = rows // fine
        expand(buf, bits_s, i * some, some, blocks, into(dense, times, lanes, 0, i * some), unrolled=True)


def start_call(own_msg, rows, cells):
    times, lanes = own_msg[0].shape[1:]
    slots = sum(chunk.shape[0] for chunk in own_msg)
    chunks = len(own_msg)
    return pl.pallas_call(
        functools.partial(start_kernel, chunks),
        out_shape=(
            shape_of((rows * times, cells), BF16),
            shape_of((cells, cells), BF16),
            shape_of((INFO, cells), F32),
        ),
        in_specs=[ANY] * chunks,
        out_specs=(VMEM,) * 3,
        scratch_shapes=[
            pltpu.VMEM((slots, times, lanes), BF16),
            pltpu.VMEM((8, lanes), I32),
            pltpu.SMEM((8, lanes), I32),
            pltpu.VMEM((cells, INFO), F32),
            pltpu.SemaphoreType.DMA((chunks + 1,)),
        ],
        compiler_params=params(12),
        cost_estimate=cost(4),
        name="own_start",
    )(*own_msg)


def own_kernel(chunks, *refs):
    msg = refs[:chunks]
    dense, cov, info_ref, out_ref, mate_dense, next_ref, buf, bits_v, bits_s, turned, sem = refs[chunks:]
    times, lanes = buf.shape[1:]
    cells = cov.shape[1]
    blocks = cells // lanes
    rows = dense.shape[0] // times
    tall = min(256, rows * times)
    steps = rows * times // tall
    part = cells // steps
    for copy in fetch(msg, buf, sem):
        copy.wait()
    read_info(buf, blocks, None, turned)
    read_head(buf, rows, blocks, bits_v)
    copy_in(bits_v, bits_s, sem.at[chunks])

    @pl.loop(0, steps)
    def _(u):
        here = aligned(u * tall, tall)
        fill_covariance(next_ref, u * part, u * part, part, turned, info_ref)
        out_ref[here, :] = jnp.dot(dense[here, :], cov[...], preferred_element_type=F32)
        some = rows // steps
        expand(buf, bits_s, u * some, some, blocks, into(mate_dense, times, lanes, 0, u * some), unrolled=True)


def own_call(mate_msg, dense, cov, info):
    times, lanes = mate_msg[0].shape[1:]
    cells = cov.shape[1]
    slots = sum(chunk.shape[0] for chunk in mate_msg)
    chunks = len(mate_msg)
    return pl.pallas_call(
        functools.partial(own_kernel, chunks),
        out_shape=(shape_of(dense.shape, F32), shape_of(dense.shape, BF16), shape_of((cells, cells), BF16)),
        in_specs=[ANY] * chunks + [VMEM] * 3,
        out_specs=(VMEM,) * 3,
        scratch_shapes=[
            pltpu.VMEM((slots, times, lanes), BF16),
            pltpu.VMEM((8, lanes), I32),
            pltpu.SMEM((8, lanes), I32),
            pltpu.VMEM((cells, INFO), F32),
            pltpu.SemaphoreType.DMA((chunks + 1,)),
        ],
        compiler_params=params(16),
        cost_estimate=cost(6),
        name="own_product",
    )(*mate_msg, dense, cov, info)


def mate_kernel(count, *refs):
    firsts = refs[:count]
    near_ref, dense, cov_ref, info_ref, out_ref, far_ref, info_buf, turned, sem = refs[count:]
    _, lanes = info_buf.shape[2:]
    cells = cov_ref.shape[1]
    blocks = cells // lanes
    tall = min(256, dense.shape[0])
    steps = dense.shape[0] // tall
    part = count * cells // steps
    copies = []
    for k in range(count):
        copies.append(pltpu.make_async_copy(firsts[k].at[pl.ds(0, 1 + blocks)], info_buf.at[k], sem.at[k]))
        copies[-1].start()
    for k in range(count):
        copies[k].wait()
        read_info(info_buf.at[k], blocks, None, turned.at[pl.ds(k * cells, cells)])

    @pl.loop(0, steps)
    def _(u):
        here = aligned(u * tall, tall)
        fill_covariance(far_ref, u * part, u * part, part, turned, info_ref)
        out_ref[here, :] = near_ref[here, :] + jnp.dot(dense[here, :], cov_ref[...], preferred_element_type=F32)


def mate_call(firsts, near, mate_dense, cov, info):
    times, lanes = firsts[0].shape[1:]
    cells = cov.shape[1]
    blocks = cells // lanes
    count = len(firsts)
    return pl.pallas_call(
        functools.partial(mate_kernel, count),
        out_shape=(shape_of(near.shape, F32), shape_of((count * cells, cells), BF16)),
        in_specs=[ANY] * count + [VMEM] * 4,
        out_specs=(VMEM, VMEM),
        scratch_shapes=[
            pltpu.VMEM((count, 1 + blocks, times, lanes), BF16),
            pltpu.VMEM((count * cells, INFO), F32),
            pltpu.SemaphoreType.DMA((count,)),
        ],
        input_output_aliases={count: 0},
        compiler_params=params(16),
        cost_estimate=cost(8),
        name="mate_product",
    )(*firsts, near, mate_dense, cov, info)


def mixed_unit(mix_ref, value):
    high = value.astype(BF16)
    low = (value - high.astype(F32)).astype(BF16)
    stacked = jnp.concatenate([high, low, high], axis=0)
    return jnp.dot(mix_ref[...], stacked, preferred_element_type=F32).astype(BF16)


def turn(value, rows, times):
    return jnp.swapaxes(value.reshape(rows, times, value.shape[1]), 0, 1)


def rows_kernel(count, chunks, unit, late, *refs):
    msgs = [refs[k * chunks : (k + 1) * chunks] for k in range(count)]
    refs = refs[count * chunks :]
    cov_ref, near_ref, mix_ref = refs[:3]
    if late:
        start_ref, done_ref, out_ref, turned_ref = refs[3:7]
    else:
        out_ref, next_ref = refs[3:5]
    bufs, bits_v, bits_s, dense_a, dense_b, sem = refs[-6:]
    times, lanes = bufs.shape[2:]
    cells = near_ref.shape[1]
    blocks = cells // lanes
    rows = out_ref.shape[0]
    few = count // 2
    deep = -(-rows * blocks // lanes)
    copies = [fetch(msgs[k], bufs.at[k], sem.at[k]) for k in range(count)]
    for k in range(count):
        for copy in copies[k]:
            copy.wait()
        read_head(bufs.at[k], rows, blocks, bits_v.at[k])
    copy = pltpu.make_async_copy(bits_v, bits_s, sem.at[count, 0])
    copy.start()

    def place(u, begin, end, dense):
        for k in range(begin, end):
            store = into(dense, times, lanes, (k - begin) * cells)
            expand(bufs.at[k], bits_s.at[k], u * unit, unit, blocks, store, unrolled=count <= 4)

    def step(u, _):
        here = aligned(u * unit * times, unit * times)
        place(u, few, count, dense_b)
        value = near_ref[here, :] + jnp.dot(dense_a[...], cov_ref[: few * cells, :], preferred_element_type=F32)
        place(jnp.minimum(u + 1, rows // unit - 1), 0, few, dense_a)
        value = value + jnp.dot(dense_b[...], cov_ref[few * cells :, :], preferred_element_type=F32)
        mixed = mixed_unit(mix_ref, value)
        at = aligned(u * unit, unit)
        out_ref[at] = mixed.reshape(unit, times, cells)
        if late:
            turned_ref[:, at, :] = turn(mixed, unit, times)
        return 0

    def carry_over(u, _):
        at = aligned(u * unit, unit)
        value = done_ref[at]
        out_ref[at] = value
        turned_ref[:, at, :] = turn(value.reshape(unit * times, cells), unit, times)
        return 0

    if late:
        first = start_ref[0]
        lax.fori_loop(0, first, carry_over, 0)
        copy.wait()
        place(jnp.minimum(first, rows // unit - 1), 0, few, dense_a)
        lax.fori_loop(first, rows // unit, step, 0)
    else:
        copy.wait()
        limit = sum(chunk.shape[0] for chunk in msgs[0])
        ready = jnp.int32(0)
        for u in range(rows // unit):
            whole = jnp.int32(1)
            for k in range(count):
                whole = whole * (bits_s[k, deep, (u + 1) * unit - 1] <= limit).astype(I32)
            ready = ready + whole
        next_ref[0] = ready
        place(jnp.int32(0), 0, few, dense_a)
        lax.fori_loop(0, ready, step, 0)


def some_rows(msgs, cov, near, mix, rows, unit, slots, carried=None):
    times, lanes = msgs[0][0].shape[1:]
    cells = near.shape[1]
    count, chunks = len(msgs), len(msgs[0])
    late = carried is not None
    flat = [chunk for msg in msgs for chunk in msg]
    out = shape_of((rows, times, cells), BF16)
    return pl.pallas_call(
        functools.partial(rows_kernel, count, chunks, unit, late),
        out_shape=(out, shape_of((times, rows, cells), BF16) if late else shape_of((1,), I32)),
        in_specs=[ANY] * len(flat) + [VMEM] * 3 + ([SMEM, VMEM] if late else []),
        out_specs=(VMEM, VMEM if late else SMEM),
        scratch_shapes=[
            pltpu.VMEM((count, slots, times, lanes), BF16),
            pltpu.VMEM((count, 8, lanes), I32),
            pltpu.SMEM((count, 8, lanes), I32),
            pltpu.VMEM((unit * times, count // 2 * cells), BF16),
            pltpu.VMEM((unit * times, (count - count // 2) * cells), BF16),
            pltpu.SemaphoreType.DMA((count + 1, chunks)),
        ],
        compiler_params=params(16),
        cost_estimate=cost(6),
        name="late_rows" if late else "first_rows",
    )(*flat, cov, near, mix, *(carried or ()))


def mix_kernel(unit, time_ref, out_ref):
    times = time_ref.shape[0]
    size = unit * times
    value = time_ref[...]
    high = value.astype(BF16)
    low = (value - high.astype(F32)).astype(BF16)

    def same(shape, dim):
        index = lax.broadcasted_iota(I32, shape, 1 - dim) % times
        return (index == lax.broadcasted_iota(I32, shape, dim)).astype(F32).astype(BF16)

    row = lax.broadcasted_iota(I32, (size, size), 0)
    col = lax.broadcasted_iota(I32, (size, size), 1)
    for j, part in enumerate((high, high, low)):
        spread = jnp.dot(same((size, times), 1), part, preferred_element_type=F32).astype(BF16)
        spread = jnp.dot(spread, same((times, size), 0), preferred_element_type=F32)
        out_ref[:, j * size : (j + 1) * size] = jnp.where(row // times == col // times, spread, 0.0).astype(BF16)


def mixing(time_cov, unit):
    size = unit * time_cov.shape[0]
    return pl.pallas_call(
        functools.partial(mix_kernel, unit),
        out_shape=shape_of((size, 3 * size), BF16),
        in_specs=[VMEM],
        out_specs=VMEM,
        compiler_params=params(8),
        cost_estimate=cost(1),
        name="mixing",
    )(time_cov)


def panel_kernel(pieces, each, final, *refs):
    msgs = refs[:pieces]
    refs = refs[pieces:]
    if final:
        group_ref, turned, before_ref, over_ref, out_ref = refs[:5]
    else:
        turned, out_ref, over_ref = refs[:3]
    bufs, bits_v, bits_s, panel, sem = refs[-5:]
    slots, times, lanes = bufs.shape[1:]
    rows, cells = turned.shape[1:]
    blocks = cells // lanes
    deep = -(-each * blocks // lanes)
    copies = [pltpu.make_async_copy(msg, bufs.at[k], sem.at[k]) for k, msg in enumerate(msgs)]
    for copy in copies:
        copy.start()
    for k, copy in enumerate(copies):
        copy.wait()
        read_head(bufs.at[k], each, blocks, bits_v.at[k], flagged=True)
    copy_in(bits_v, bits_s, sem.at[pieces])
    over = over_ref[0] if final else jnp.int32(0)
    for k in range(pieces):
        over = over + (bits_s[k, deep, each - 1] > slots - 1).astype(I32) + bits_s[k, deep + 1, 0]
    group = max(1, 16 // each)

    @pl.loop(0, pieces // group)
    def _(g):
        for b in range(blocks):
            tiles = []
            for i in range(group * each):
                k, place = g * group + i // each, i % each * blocks + b
                tiles.append(bufs[k, bits_s[k, place // lanes, place % lanes]])
            value = turn(jnp.concatenate(tiles, axis=0), group * each, times)
            panel[:, aligned(g * group * each, group * each), b * lanes : (b + 1) * lanes] = value

    total = None
    for t in range(times):
        value = lax.dot_general(turned[t], panel[t], (((1,), (1,)), ((), ())), preferred_element_type=F32)
        total = value if total is None else total + value
    if not final:
        out_ref[...] = total
        over_ref[0] = over
        return
    value = jnp.concatenate([before_ref[...], total], axis=1)
    size = value.shape[1]
    row = lax.broadcasted_iota(I32, (size, size), 0)
    half = size // each // 2
    hi, lo = split(group_ref[0], 2)
    target = row
    for k in range(size // each):
        back = hi - k // 2
        source = jnp.where(back < 0, back + half, back) * 2 + lax.bitwise_xor(lo, k % 2)
        target = jnp.where((row >= k * each) & (row < (k + 1) * each), row + (source - k) * each, target)
    select = (lax.broadcasted_iota(I32, (size, size), 1) == target).astype(F32).astype(BF16)
    total = jnp.zeros(value.shape, F32)
    for _ in range(3):
        high = value.astype(BF16)
        total = total + jnp.dot(high, select, preferred_element_type=F32)
        value = value - high.astype(F32)
    out_ref[0:rows, :] = total
    out_ref[rows:, :] = jnp.broadcast_to(over, (8, size)).astype(F32)


def panel_part(msgs, turned, each, final=None):
    slots, times, lanes = msgs[0].shape
    rows, cells = turned.shape[1:]
    pieces = len(msgs)
    width = pieces * each
    if final:
        group, before, over = final
        operands, in_specs = (group[None], turned, before, over), [SMEM, VMEM, VMEM, SMEM]
        out_shape = shape_of((rows + 8, before.shape[1] + width), F32)
        out_specs = VMEM
    else:
        operands, in_specs = (turned,), [VMEM]
        out_shape, out_specs = (shape_of((rows, width), F32), shape_of((1,), I32)), (VMEM, SMEM)
    return pl.pallas_call(
        functools.partial(panel_kernel, pieces, each, bool(final)),
        out_shape=out_shape,
        in_specs=[ANY] * pieces + in_specs,
        out_specs=out_specs,
        scratch_shapes=[
            pltpu.VMEM((pieces, slots, times, lanes), BF16),
            pltpu.VMEM((pieces, 8, lanes), I32),
            pltpu.SMEM((pieces, 8, lanes), I32),
            pltpu.VMEM((times, width, cells), BF16),
            pltpu.SemaphoreType.DMA((pieces + 1,)),
        ],
        compiler_params=params(14),
        cost_estimate=cost(3 if final else 5),
        name="panel_last" if final else "panel_first",
    )(*msgs, *operands)


def partner(value, axis, count):
    return lax.ppermute(value, axis, [(i, i ^ 1) for i in range(count)])


def shifted(value, axis, count, shift, flip=0):
    return lax.ppermute(value, axis, [(i, ((i + 2 * shift) % count) ^ flip) for i in range(count)])


def row_major(value):
    return with_layout_constraint(value, Layout(tuple(range(value.ndim))))


def add_cells(part, cells):
    total = part
    for shift in range(cells // 2):
        for flip in range(2):
            if shift or flip:
                total = total + shifted(part, "cell", cells, shift, flip)
    return total


def dense_way(cells, observers, footprint, block_mask, own, time_cov, mine, sources):
    obs_rows, times, cell_local = footprint.shape
    blocks = block_mask.shape[1]
    keep = block_mask.astype(BF16)[:, None, :, None]
    feet = (footprint.reshape(obs_rows, times, blocks, cell_local // blocks) * keep).reshape(footprint.shape)

    def add(carry, _):
        total, feet, info = carry
        dx = info[0][:, None] - own[0][None, :]
        dy = info[1][:, None] - own[1][None, :]
        decay = jnp.exp(-jnp.sqrt(dx * dx + dy * dy + 1.0) / LENGTH)
        cov = (decay * (info[2][:, None] * own[2][None, :])).astype(BF16)
        total = total + jnp.dot(feet.reshape(-1, cell_local), cov, preferred_element_type=F32)
        ring = [(i, (i + 1) % cells) for i in range(cells)]
        return (total, lax.ppermute(feet, "cell", ring), lax.ppermute(info, "cell", ring)), None

    zero = jnp.zeros((obs_rows * times, cell_local), F32)
    (total, _, _), _ = lax.scan(add, (zero, feet, own), None, length=cells)
    cov_product = jnp.einsum(
        "ts,ksc->ktc", time_cov, total.reshape(obs_rows, times, cell_local), precision=lax.Precision.HIGHEST
    ).astype(BF16)
    flat = cov_product.reshape(obs_rows, times * cell_local)

    def meet(held, _):
        both = jnp.concatenate([held, partner(held, "obs", observers)], axis=0)
        part = lax.dot_general(
            flat, both.reshape(both.shape[0], -1), (((1,), (1,)), ((), ())), preferred_element_type=F32
        )
        return shifted(held, "obs", observers, 1), part

    _, parts = lax.scan(meet, jnp.take(feet, mine, axis=0), None, length=observers // 2)
    parts = parts.transpose(1, 0, 2).reshape(obs_rows, observers, -1)
    ordered = jnp.zeros_like(parts).at[:, sources].set(parts)
    return cov_product, add_cells(ordered.reshape(obs_rows, -1), cells)


def body(cells, observers, footprint, block_mask, cell_coords, cell_sigma, time_cov, error_var, panel_index):
    obs_rows, _, cell_local = footprint.shape
    blocks = block_mask.shape[1]
    group = lax.axis_index("obs")
    each = panel_index.shape[0] // observers
    half = observers // 2
    unit = math.gcd(16, obs_rows)
    slots = slot_count(obs_rows * blocks, 1 + blocks)
    chunks = (slots - slots // 2, slots // 2)
    mask = block_mask.T

    room = slots - 2 - blocks - 1
    own_panel = pack_panel(mask, panel_index, group, footprint, each, slot_count(each * blocks, 1), room)
    ring = [own_panel]
    for _ in range(1, half):
        ring.append(shifted(ring[-1], "obs", observers, 1))
    messages = []
    for held in ring:
        messages += [held, partner(held, "obs", observers)]
    own_msg = pack_feet(mask, cell_coords, cell_sigma[None, :], footprint, chunks)
    far_msgs = []
    for shift in range(1, cells // 2):
        far_msgs.append([shifted(c, "cell", cells, shift) for c in own_msg])
    mate_msg = [partner(c, "cell", cells) for c in own_msg]
    for shift in range(1, cells // 2):
        far_msgs.append([partner(c, "cell", cells) for c in far_msgs[shift - 1]])

    dense, own_cov, info = start_call(own_msg, obs_rows, cell_local)
    near, mate_dense, mate_cov = own_call(mate_msg, dense, own_cov, info)
    near, far_cov = mate_call([msg[0] for msg in far_msgs], near, mate_dense, mate_cov, info)
    mix = mixing(time_cov, unit)
    first_cov, start = some_rows([msg[:1] for msg in far_msgs], far_cov, near, mix, obs_rows, unit, slots)
    cov_product, turned = some_rows(far_msgs, far_cov, near, mix, obs_rows, unit, slots, (start, first_cov))
    cut = len(messages) * 3 // 4
    before, over = panel_part(messages[:cut], turned, each)
    part = panel_part(messages[cut:], turned, each, (group, before, over))

    def innovation_of(total, group):
        positions = jnp.arange(obs_rows, dtype=I32)
        on_diagonal = ((group * obs_rows + positions)[:, None] == panel_index[None, :]).astype(F32)
        return total + error_var[:, None] * on_diagonal

    part, late_group, late_mask = lax.optimization_barrier((part, group, mask))
    total = add_cells(part, cells)

    def again(carry):
        wanted = carry[0]
        kept, cell_info, place = (jnp.where(wanted, value, 0) for value in (late_mask, info, late_group))
        order = jnp.arange(observers, dtype=I32)
        from_group = (place // 2 - order // 2) % half * 2 + (place % 2 ^ (order % 2))
        mine = lax.dynamic_slice_in_dim(panel_index, place * each, each) - place * obs_rows
        cov_product, total = dense_way(
            cells, observers, footprint, kept.T, cell_info, time_cov, mine, from_group
        )
        return jnp.bool_(False), cov_product, row_major(innovation_of(total, place))

    carry = (total[obs_rows, 0] > 0, cov_product, row_major(innovation_of(total[:obs_rows], late_group)))
    return lax.while_loop(lambda carry: carry[0], again, carry)[1:]


def solution(mesh):
    in_specs = (
        P("obs", None, "cell"),
        P("obs", "cell"),
        P(None, "cell"),
        P("cell"),
        P(),
        P("obs"),
        P(),
    )
    out_specs = (P("obs", None, "cell"), P("obs", None))
    cells, observers = mesh.shape["cell"], mesh.shape["obs"]

    def per_device(*args):
        return body(cells, observers, *args)

    return jax.shard_map(per_device, mesh=mesh, in_specs=in_specs, out_specs=out_specs, check_vma=False)
```

```python
import functools
import math

import jax
import jax.numpy as jnp
from jax import lax
from jax.experimental import pallas as pl
from jax.experimental.pallas import tpu as pltpu
from jax.experimental.layout import Layout, with_layout_constraint
from jax.sharding import PartitionSpec as P


GRID = 64
LENGTH = GRID / 16.0
F32, BF16, I32 = jnp.float32, jnp.bfloat16, jnp.int32
SHIFT = 4
INFO = 8


VMEM = pl.BlockSpec(memory_space=pltpu.VMEM)
SMEM = pl.BlockSpec(memory_space=pltpu.SMEM)
ANY = pl.BlockSpec(memory_space=pl.ANY)
HBM = pl.BlockSpec(memory_space=pltpu.HBM)


def shape_of(shape, dtype):
    return jax.ShapeDtypeStruct(shape, dtype)


def params(mib):
    return pltpu.CompilerParams(vmem_limit_bytes=mib * 2**20)


def cost(micros):
    return pl.CostEstimate(flops=int(micros * 9e8), bytes_accessed=1_000_000, transcendentals=0)


def aligned(start, size):
    return pl.ds(pl.multiple_of(start, size), size)


def slot_count(tiles, extra):
    room = tiles / 2 + 4.1 * math.sqrt(tiles / 4)
    return extra + min(tiles + 1, 2 * math.ceil(room / 2) + 1)


def chunk_sizes(slots, tiles, extra):
    most = min(slots - 2, extra + math.ceil(tiles * 3 / 8 + 3.4 * math.sqrt(tiles * 3 / 16)))
    least = min(extra + tiles // 10, most - 1)
    return least, most - least, slots - most


def pack_rows(mask_at, feet_at, begin, end, blocks, buf, carry):
    slots, _, lanes = buf.shape
    row_of = lax.broadcasted_iota(I32, (8, lanes), 0)
    lane_of = lax.broadcasted_iota(I32, (8, lanes), 1)
    flat = row_of * lanes + lane_of
    batch = math.gcd(2, end - begin)

    def some(i, carry):
        pos, head, ends = carry
        first = begin + i * batch
        tiles = [[feet_at(first + j, b) for b in range(blocks)] for j in range(batch)]
        kept = [[mask_at(first + j, b) for b in range(blocks)] for j in range(batch)]
        for j in range(batch):
            for b in range(blocks):
                buf[jnp.minimum(pos, slots - 1)] = tiles[j][b]
                head = jnp.where(flat == (first + j) * blocks + b, kept[j][b] * pos, head)
                pos = pos + kept[j][b]
            ends = jnp.where(lane_of == first + j, pos, ends)
        return pos, head, ends

    return lax.fori_loop(0, (end - begin) // batch, some, carry)


def no_rows(first, lanes):
    zeros = jnp.zeros((8, lanes), I32)
    return jnp.int32(first), zeros, zeros


def write_head(carry, rows, blocks, buf, head_v, flag=None):
    lanes = buf.shape[2]
    deep = -(-rows * blocks // lanes)
    _, head, ends = carry
    low = (1 << SHIFT) - 1
    head_v[...] = jnp.zeros_like(head_v)
    head_v[0:deep, :] = (head >> SHIFT)[0:deep].astype(F32)
    head_v[deep : 2 * deep, :] = (head & low)[0:deep].astype(F32)
    head_v[2 * deep : 2 * deep + 1, :] = (ends >> SHIFT)[0:1].astype(F32)
    head_v[2 * deep + 1 : 2 * deep + 2, :] = (ends & low)[0:1].astype(F32)
    if flag is not None:
        head_v[2 * deep + 2 : 2 * deep + 3, :] = jnp.broadcast_to(flag, (1, lanes)).astype(F32)
    buf[0] = head_v[...].astype(BF16)


def pack_feet_kernel(chunks, mask_ref, coords_hbm, sigma_hbm, feet_ref, *rest):
    outs, (coords_ref, sigma_ref, feet, buf, head_v, small_sem, in_sem, sem) = (
        rest[: len(chunks)],
        rest[len(chunks) :],
    )
    blocks, rows = mask_ref.shape
    small = [
        pltpu.make_async_copy(src, dst, small_sem.at[k])
        for k, (src, dst) in enumerate(((coords_hbm, coords_ref), (sigma_hbm, sigma_ref)))
    ]
    for copy in small:
        copy.start()
    times, lanes = buf.shape[1:]
    groups = in_sem.shape[0]
    each = rows // groups
    loads = [
        pltpu.make_async_copy(feet_ref.at[pl.ds(g * each, each)], feet.at[pl.ds(g * each, each)], in_sem.at[g])
        for g in range(groups)
    ]
    for load in loads:
        load.start()
    for copy in small:
        copy.wait()
    sigma = sigma_ref[...]
    high = sigma.astype(BF16).astype(F32)
    middle = (sigma - high).astype(BF16).astype(F32)
    lowest = sigma - high - middle
    at = lax.broadcasted_iota(I32, (times, sigma.shape[1]), 0)
    info = jnp.zeros(at.shape, F32)
    for k, row in enumerate((coords_ref[0:1, :].astype(F32), coords_ref[1:2, :].astype(F32), high, middle, lowest)):
        info = jnp.where(at == k, row, info)
    info = info.astype(BF16)
    for b in range(blocks):
        buf[1 + b] = info[:, b * lanes : (b + 1) * lanes]
    carry = no_rows(1 + blocks, lanes)
    for g in range(groups):
        loads[g].wait()
        carry = pack_rows(
            lambda o, b: mask_ref[b, o],
            lambda o, b: feet[o, :, b * lanes : (b + 1) * lanes],
            g * each,
            (g + 1) * each,
            blocks,
            buf,
            carry,
        )
    write_head(carry, rows, blocks, buf, head_v)
    copies, first = [], 0
    for k, size in enumerate(chunks):
        copies.append(pltpu.make_async_copy(buf.at[pl.ds(first, size)], outs[k], sem.at[k]))
        first += size
    for copy in copies:
        copy.start()
    for copy in copies:
        copy.wait()


def pack_feet(mask, coords, sigma, feet, chunks):
    rows, times, cells = feet.shape
    lanes = cells // mask.shape[0]
    groups = math.gcd(4, rows)
    return pl.pallas_call(
        functools.partial(pack_feet_kernel, chunks),
        out_shape=tuple(shape_of((size, times, lanes), BF16) for size in chunks),
        in_specs=[SMEM, HBM, HBM, HBM],
        out_specs=(ANY,) * len(chunks),
        scratch_shapes=[
            pltpu.VMEM(coords.shape, I32),
            pltpu.VMEM(sigma.shape, F32),
            pltpu.VMEM((rows, times, cells), BF16),
            pltpu.VMEM((sum(chunks), times, lanes), BF16),
            pltpu.VMEM((times, lanes), F32),
            pltpu.SemaphoreType.DMA((2,)),
            pltpu.SemaphoreType.DMA((groups,)),
            pltpu.SemaphoreType.DMA((len(chunks),)),
        ],
        compiler_params=params(12),
        cost_estimate=cost(3),
        name="pack_feet",
    )(mask, coords, sigma, feet)


def pack_panel_kernel(room, mask_ref, mask_hbm, index_ref, group_ref, feet_ref, out_ref, mask_v, rows_buf, head_v, small_sem, sem):
    count = rows_buf.shape[0]
    blocks, obs = mask_ref.shape
    lanes = out_ref.shape[2]
    mask_copy = pltpu.make_async_copy(mask_hbm, mask_v, small_sem.at[0])
    mask_copy.start()
    base = group_ref[0]
    rows = [jnp.clip(index_ref[base * count + j] - base * obs, 0, obs - 1) for j in range(count)]
    copies = [pltpu.make_async_copy(feet_ref.at[rows[j]], rows_buf.at[j], sem.at[j]) for j in range(count)]
    for copy in copies:
        copy.start()
    mask_copy.wait()
    flag = (jnp.sum(mask_v[...].astype(F32), axis=(0, 1), keepdims=True) > room).astype(I32)
    for copy in copies:
        copy.wait()

    def mask_at(o, b):
        return mask_ref[b, jnp.clip(index_ref[base * count + o] - base * obs, 0, obs - 1)]

    carry = pack_rows(
        mask_at, lambda o, b: rows_buf[o, :, b * lanes : (b + 1) * lanes], 0, count, blocks, out_ref, no_rows(1, lanes)
    )
    write_head(carry, count, blocks, out_ref, head_v, flag)


def pack_panel(mask, panel_index, group, feet, count, slots, room):
    _, times, cells = feet.shape
    lanes = cells // mask.shape[0]
    return pl.pallas_call(
        functools.partial(pack_panel_kernel, room),
        out_shape=shape_of((slots, times, lanes), BF16),
        in_specs=[SMEM, HBM, SMEM, SMEM, HBM],
        out_specs=VMEM,
        scratch_shapes=[
            pltpu.VMEM(mask.shape, I32),
            pltpu.VMEM((count, times, cells), BF16),
            pltpu.VMEM((times, lanes), F32),
            pltpu.SemaphoreType.DMA((1,)),
            pltpu.SemaphoreType.DMA((count,)),
        ],
        compiler_params=params(8),
        cost_estimate=cost(2),
        name="pack_panel",
    )(mask, mask, panel_index, group[None], feet)


def fetch(chunks, buf, sem):
    copies, first = [], 0
    for k, chunk in enumerate(chunks):
        copies.append(pltpu.make_async_copy(chunk, buf.at[pl.ds(first, chunk.shape[0])], sem.at[k]))
        copies[-1].start()
        first += chunk.shape[0]
    return copies


def read_head(buf, rows, blocks, bits_v, flagged=False):
    slots, _, lanes = buf.shape
    deep = -(-rows * blocks // lanes)
    head = buf[0].astype(F32)
    scale = float(1 << SHIFT)
    bits_v[0:deep, :] = jnp.minimum(head[0:deep] * scale + head[deep : 2 * deep], slots - 1.0).astype(I32)
    bits_v[5:6, :] = (head[2 * deep : 2 * deep + 1] * scale + head[2 * deep + 1 : 2 * deep + 2]).astype(I32)
    if flagged:
        bits_v[6:7, :] = head[2 * deep + 2 : 2 * deep + 3].astype(I32)
    buf[0] = jnp.zeros(buf.shape[1:], buf.dtype)


def copy_in(src, dst, sem):
    copy = pltpu.make_async_copy(src, dst, sem)
    copy.start()
    copy.wait()


def split(number, size):
    if size & (size - 1):
        return lax.div(number, size), lax.rem(number, size)
    return lax.shift_right_logical(number, size.bit_length() - 1), lax.bitwise_and(number, size - 1)


def expand(buf, bits, first, count, blocks, store, unrolled=False):
    lanes = buf.shape[2]
    batch = math.gcd(2, count)

    def some(i, _):
        tiles = []
        for j in range(batch):
            row, col = split(jnp.int32((first + i * batch + j) * blocks), lanes)
            tiles += [buf[bits[row, col + b]] for b in range(blocks)]
        for j in range(batch):
            for b in range(blocks):
                store(i * batch + j, b, tiles[j * blocks + b])
        return 0

    if unrolled:
        for i in range(count // batch):
            some(i, 0)
    else:
        lax.fori_loop(0, count // batch, some, 0)


def into(dense, times, lanes, offset, first=0):
    def store(i, b, tile):
        at = aligned((first + i) * times, times)
        dense[at, offset + b * lanes : offset + (b + 1) * lanes] = tile.astype(dense.dtype)

    return store


def read_info(buf, blocks, row_v, turned):
    _, lanes = buf.shape[1:]
    for b in range(blocks):
        tile = buf[1 + b].astype(F32)[0:INFO]
        sigma = tile[2:3] + tile[3:4] + tile[4:5]
        tile = jnp.where(lax.broadcasted_iota(I32, tile.shape, 0) == 2, sigma, tile)
        at = slice(b * lanes, (b + 1) * lanes)
        if row_v is not None:
            row_v[:, at] = tile
        if turned is not None:
            turned[at, :] = tile.T


def fill_covariance(dst, dst_first, src_first, rows, turned, own):
    x, y, s = own[0:1, :], own[1:2, :], own[2:3, :]
    step = min(32, rows)
    for i in range(rows // step):
        at = aligned(src_first + i * step, step)
        dx = turned[at, 0:1] - x
        dy = turned[at, 1:2] - y
        square = dx * dx + dy * dy + 1.0
        decay = jnp.exp(square * lax.rsqrt(square) * (-1.0 / LENGTH))
        dst[aligned(dst_first + i * step, step), :] = (decay * (turned[at, 2:3] * s)).astype(BF16)


def start_kernel(chunks, *refs):
    msg = refs[:chunks]
    dense, cov, info_ref, buf, bits_v, bits_s, turned, sem = refs[chunks:]
    times, lanes = buf.shape[1:]
    cells = cov.shape[1]
    blocks = cells // lanes
    rows = dense.shape[0] // times
    copies = fetch(msg, buf, sem)
    for copy in copies:
        copy.wait()
    read_info(buf, blocks, info_ref, turned)
    read_head(buf, rows, blocks, bits_v)
    copy = pltpu.make_async_copy(bits_v, bits_s, sem.at[chunks])
    copy.start()
    half = cells // 2
    fine = math.gcd(4, rows // 2)

    @pl.loop(0, fine)
    def _(i):
        fill_covariance(cov, i * (half // fine), i * (half // fine), half // fine, turned, info_ref)

    copy.wait()

    @pl.loop(0, fine)
    def _(i):
        first = half + i * (half // fine)
        fill_covariance(cov, first, first, half // fine, turned, info_ref)
        some = rows // fine
        expand(buf, bits_s, i * some, some, blocks, into(dense, times, lanes, 0, i * some), unrolled=True)


def start_call(own_msg, rows, cells):
    times, lanes = own_msg[0].shape[1:]
    slots = sum(chunk.shape[0] for chunk in own_msg)
    chunks = len(own_msg)
    return pl.pallas_call(
        functools.partial(start_kernel, chunks),
        out_shape=(
            shape_of((rows * times, cells), BF16),
            shape_of((cells, cells), BF16),
            shape_of((INFO, cells), F32),
        ),
        in_specs=[ANY] * chunks,
        out_specs=(VMEM,) * 3,
        scratch_shapes=[
            pltpu.VMEM((slots, times, lanes), BF16),
            pltpu.VMEM((8, lanes), I32),
            pltpu.SMEM((8, lanes), I32),
            pltpu.VMEM((cells, INFO), F32),
            pltpu.SemaphoreType.DMA((chunks + 1,)),
        ],
        compiler_params=params(12),
        cost_estimate=cost(4),
        name="own_start",
    )(*own_msg)


def own_kernel(chunks, *refs):
    msg = refs[:chunks]
    dense, cov, info_ref, out_ref, mate_dense, next_ref, buf, bits_v, bits_s, turned, sem = refs[chunks:]
    times, lanes = buf.shape[1:]
    cells = cov.shape[1]
    blocks = cells // lanes
    rows = dense.shape[0] // times
    tall = min(256, rows * times)
    steps = rows * times // tall
    part = cells // steps
    for copy in fetch(msg, buf, sem):
        copy.wait()
    read_info(buf, blocks, None, turned)
    read_head(buf, rows, blocks, bits_v)
    copy_in(bits_v, bits_s, sem.at[chunks])

    @pl.loop(0, steps)
    def _(u):
        here = aligned(u * tall, tall)
        fill_covariance(next_ref, u * part, u * part, part, turned, info_ref)
        out_ref[here, :] = jnp.dot(dense[here, :], cov[...], preferred_element_type=F32)
        some = rows // steps
        expand(buf, bits_s, u * some, some, blocks, into(mate_dense, times, lanes, 0, u * some), unrolled=True)


def own_call(mate_msg, dense, cov, info):
    times, lanes = mate_msg[0].shape[1:]
    cells = cov.shape[1]
    slots = sum(chunk.shape[0] for chunk in mate_msg)
    chunks = len(mate_msg)
    return pl.pallas_call(
        functools.partial(own_kernel, chunks),
        out_shape=(shape_of(dense.shape, F32), shape_of(dense.shape, BF16), shape_of((cells, cells), BF16)),
        in_specs=[ANY] * chunks + [VMEM] * 3,
        out_specs=(VMEM,) * 3,
        scratch_shapes=[
            pltpu.VMEM((slots, times, lanes), BF16),
            pltpu.VMEM((8, lanes), I32),
            pltpu.SMEM((8, lanes), I32),
            pltpu.VMEM((cells, INFO), F32),
            pltpu.SemaphoreType.DMA((chunks + 1,)),
        ],
        compiler_params=params(16),
        cost_estimate=cost(6),
        name="own_product",
    )(*mate_msg, dense, cov, info)


def mate_kernel(count, *refs):
    firsts = refs[:count]
    near_ref, dense, cov_ref, info_ref, out_ref, far_ref, info_buf, turned, sem = refs[count:]
    _, lanes = info_buf.shape[2:]
    cells = cov_ref.shape[1]
    blocks = cells // lanes
    tall = min(256, dense.shape[0])
    steps = dense.shape[0] // tall
    part = count * cells // steps
    copies = []
    for k in range(count):
        copies.append(pltpu.make_async_copy(firsts[k].at[pl.ds(0, 1 + blocks)], info_buf.at[k], sem.at[k]))
        copies[-1].start()
    for k in range(count):
        copies[k].wait()
        read_info(info_buf.at[k], blocks, None, turned.at[pl.ds(k * cells, cells)])

    @pl.loop(0, steps)
    def _(u):
        here = aligned(u * tall, tall)
        fill_covariance(far_ref, u * part, u * part, part, turned, info_ref)
        out_ref[here, :] = near_ref[here, :] + jnp.dot(dense[here, :], cov_ref[...], preferred_element_type=F32)


def mate_call(firsts, near, mate_dense, cov, info):
    times, lanes = firsts[0].shape[1:]
    cells = cov.shape[1]
    blocks = cells // lanes
    count = len(firsts)
    return pl.pallas_call(
        functools.partial(mate_kernel, count),
        out_shape=(shape_of(near.shape, F32), shape_of((count * cells, cells), BF16)),
        in_specs=[ANY] * count + [VMEM] * 4,
        out_specs=(VMEM, VMEM),
        scratch_shapes=[
            pltpu.VMEM((count, 1 + blocks, times, lanes), BF16),
            pltpu.VMEM((count * cells, INFO), F32),
            pltpu.SemaphoreType.DMA((count,)),
        ],
        input_output_aliases={count: 0},
        compiler_params=params(16),
        cost_estimate=cost(8),
        name="mate_product",
    )(*firsts, near, mate_dense, cov, info)


def mixed_unit(mix_ref, value):
    high = value.astype(BF16)
    low = (value - high.astype(F32)).astype(BF16)
    stacked = jnp.concatenate([high, low, high], axis=0)
    return jnp.dot(mix_ref[...], stacked, preferred_element_type=F32).astype(BF16)


def turn(value, rows, times):
    return jnp.swapaxes(value.reshape(rows, times, value.shape[1]), 0, 1)


def unit_step(u, count, unit, bufs, bits_s, dense_a, dense_b, near_ref, cov_ref, mix_ref, rows):
    times, _ = bufs.shape[2:]
    cells = near_ref.shape[1]
    few = count // 2
    here = aligned(u * unit * times, unit * times)
    place(u, few, count, unit, bufs, bits_s, dense_b, cells)
    value = near_ref[here, :] + jnp.dot(dense_a[...], cov_ref[: few * cells, :], preferred_element_type=F32)
    place(jnp.minimum(u + 1, rows // unit - 1), 0, few, unit, bufs, bits_s, dense_a, cells)
    value = value + jnp.dot(dense_b[...], cov_ref[few * cells :, :], preferred_element_type=F32)
    return mixed_unit(mix_ref, value)


def place(u, begin, end, unit, bufs, bits_s, dense, cells):
    times, lanes = bufs.shape[2:]
    for k in range(begin, end):
        store = into(dense, times, lanes, (k - begin) * cells)
        expand(bufs.at[k], bits_s.at[k], u * unit, unit, cells // lanes, store, unrolled=bufs.shape[0] <= 4)


def first_kernel(count, chunks, unit, *refs):
    msgs = [refs[k * chunks : (k + 1) * chunks] for k in range(count)]
    cov_ref, near_ref, mix_ref, out_ref, next_ref, bufs, bits_v, bits_s, dense_a, dense_b, sem = refs[count * chunks :]
    times, lanes = bufs.shape[2:]
    cells = near_ref.shape[1]
    blocks = cells // lanes
    rows = out_ref.shape[0]
    limit = sum(chunk.shape[0] for chunk in msgs[0])
    copies = [fetch(msgs[k], bufs.at[k], sem.at[k]) for k in range(count)]
    for k in range(count):
        for copy in copies[k]:
            copy.wait()
        read_head(bufs.at[k], rows, blocks, bits_v.at[k])
    copy_in(bits_v, bits_s, sem.at[count, 0])
    ready = jnp.int32(0)
    for u in range(rows // unit):
        whole = jnp.int32(1)
        for k in range(count):
            whole = whole * (bits_s[k, 5, (u + 1) * unit - 1] <= limit).astype(I32)
        ready = ready + whole
    next_ref[0] = ready
    place(jnp.int32(0), 0, count // 2, unit, bufs, bits_s, dense_a, cells)

    def step(u, _):
        mixed = unit_step(u, count, unit, bufs, bits_s, dense_a, dense_b, near_ref, cov_ref, mix_ref, rows)
        out_ref[aligned(u * unit, unit)] = mixed.reshape(unit, times, cells)
        return 0

    lax.fori_loop(0, ready, step, 0)


def rows_scratch(count, chunks, slots, times, lanes, unit, cells, more):
    return [
        pltpu.VMEM((count, slots, times, lanes), BF16),
        pltpu.VMEM((count + more, 8, lanes), I32),
        pltpu.SMEM((count + more, 8, lanes), I32),
        pltpu.VMEM((unit * times, count // 2 * cells), BF16),
        pltpu.VMEM((unit * times, (count - count // 2) * cells), BF16),
        pltpu.SemaphoreType.DMA((count + 1, chunks)),
    ]


def first_rows(msgs, cov, near, mix, rows, unit, slots):
    times, lanes = msgs[0][0].shape[1:]
    cells = near.shape[1]
    count, chunks = len(msgs), len(msgs[0])
    flat = [chunk for msg in msgs for chunk in msg]
    return pl.pallas_call(
        functools.partial(first_kernel, count, chunks, unit),
        out_shape=(shape_of((rows, times, cells), BF16), shape_of((1,), I32)),
        in_specs=[ANY] * len(flat) + [VMEM] * 3,
        out_specs=(VMEM, SMEM),
        scratch_shapes=rows_scratch(count, chunks, slots, times, lanes, unit, cells, 0),
        compiler_params=params(16),
        cost_estimate=cost(7),
        name="first_rows",
    )(*flat, cov, near, mix)


def late_kernel(count, chunks, unit, pieces, each, *refs):
    msgs = [refs[k * chunks : (k + 1) * chunks] for k in range(count)]
    panel_msgs = refs[count * chunks : count * chunks + pieces]
    refs = refs[count * chunks + pieces :]
    cov_ref, near_ref, mix_ref, start_ref, done_ref, out_ref, turned_ref, part_ref, over_ref = refs[:9]
    bufs, bits_v, bits_s, dense_a, dense_b, sem, panel_bufs, stage, panel, panel_sem, out_sem = refs[9:]
    times, lanes = bufs.shape[2:]
    cells = near_ref.shape[1]
    blocks = cells // lanes
    rows = stage.shape[0]
    copies = [fetch(msgs[k], bufs.at[k], sem.at[k]) for k in range(count)]
    panel_copies = [pltpu.make_async_copy(msg, panel_bufs.at[k], panel_sem.at[k]) for k, msg in enumerate(panel_msgs)]
    for copy in panel_copies:
        copy.start()
    for k in range(count):
        for copy in copies[k]:
            copy.wait()
        read_head(bufs.at[k], rows, blocks, bits_v.at[k])
    for k, copy in enumerate(panel_copies):
        copy.wait()
        read_head(panel_bufs.at[k], each, blocks, bits_v.at[count + k], flagged=True)
    bits_copy = pltpu.make_async_copy(bits_v, bits_s, sem.at[count, 0])
    bits_copy.start()
    first = start_ref[0]

    def outgoing(u, src):
        at = aligned(u * unit, unit)
        return pltpu.make_async_copy(src.at[at], out_ref.at[at], out_sem.at[u])

    def carry_over(u, _):
        outgoing(u, done_ref).start()
        at = aligned(u * unit, unit)
        turned_ref[:, at, :] = turn(done_ref[at].reshape(unit * times, cells), unit, times)
        return 0

    lax.fori_loop(0, first, carry_over, 0)
    bits_copy.wait()
    place(jnp.minimum(first, rows // unit - 1), 0, count // 2, unit, bufs, bits_s, dense_a, cells)

    def step(u, _):
        mixed = unit_step(u, count, unit, bufs, bits_s, dense_a, dense_b, near_ref, cov_ref, mix_ref, rows)
        at = aligned(u * unit, unit)
        stage[at] = mixed.reshape(unit, times, cells)
        outgoing(u, stage).start()
        turned_ref[:, at, :] = turn(mixed, unit, times)
        return 0

    lax.fori_loop(first, rows // unit, step, 0)
    over_ref[0] = panel_over(panel_bufs, bits_s, count, pieces, each)
    part_ref[...] = panel_products(panel_bufs, bits_s, count, pieces, each, turned_ref, panel)

    def settle(u, _):
        outgoing(u, stage).wait()
        return 0

    lax.fori_loop(0, rows // unit, settle, 0)


def late_rows(msgs, panel_msgs, each, cov, near, mix, start, done, unit, slots):
    times, lanes = msgs[0][0].shape[1:]
    rows, _, cells = done.shape
    count, chunks, pieces = len(msgs), len(msgs[0]), len(panel_msgs)
    flat = [chunk for msg in msgs for chunk in msg] + list(panel_msgs)
    return pl.pallas_call(
        functools.partial(late_kernel, count, chunks, unit, pieces, each),
        out_shape=(
            shape_of(done.shape, BF16),
            shape_of((times, rows, cells), BF16),
            shape_of((rows, pieces * each), F32),
            shape_of((1,), I32),
        ),
        in_specs=[ANY] * len(flat) + [VMEM] * 3 + [SMEM, VMEM],
        out_specs=(HBM, VMEM, VMEM, SMEM),
        scratch_shapes=rows_scratch(count, chunks, slots, times, lanes, unit, cells, pieces)
        + [
            pltpu.VMEM((pieces, panel_msgs[0].shape[0], times, lanes), BF16),
            pltpu.VMEM((rows, times, cells), BF16),
            pltpu.VMEM((times, pieces * each, cells), BF16),
            pltpu.SemaphoreType.DMA((pieces,)),
            pltpu.SemaphoreType.DMA((rows // unit,)),
        ],
        compiler_params=params(20),
        cost_estimate=cost(9),
        name="late_rows",
    )(*flat, cov, near, mix, start, done)


def mix_kernel(unit, time_ref, out_ref):
    times = time_ref.shape[0]
    size = unit * times
    value = time_ref[...]
    high = value.astype(BF16)
    low = (value - high.astype(F32)).astype(BF16)

    def same(shape, dim):
        index = lax.broadcasted_iota(I32, shape, 1 - dim) % times
        return (index == lax.broadcasted_iota(I32, shape, dim)).astype(F32).astype(BF16)

    row = lax.broadcasted_iota(I32, (size, size), 0)
    col = lax.broadcasted_iota(I32, (size, size), 1)
    for j, part in enumerate((high, high, low)):
        spread = jnp.dot(same((size, times), 1), part, preferred_element_type=F32).astype(BF16)
        spread = jnp.dot(spread, same((times, size), 0), preferred_element_type=F32)
        out_ref[:, j * size : (j + 1) * size] = jnp.where(row // times == col // times, spread, 0.0).astype(BF16)


def mixing(time_cov, unit):
    size = unit * time_cov.shape[0]
    return pl.pallas_call(
        functools.partial(mix_kernel, unit),
        out_shape=shape_of((size, 3 * size), BF16),
        in_specs=[VMEM],
        out_specs=VMEM,
        compiler_params=params(8),
        cost_estimate=cost(1),
        name="mixing",
    )(time_cov)


def panel_over(bufs, bits_s, base, pieces, each):
    slots, _, _ = bufs.shape[1:]
    over = jnp.int32(0)
    for k in range(pieces):
        ends = bits_s.shape[1] - 3
        over = over + (bits_s[base + k, ends, each - 1] > slots - 1).astype(I32) + bits_s[base + k, ends + 1, 0]
    return over


def panel_products(bufs, bits_s, base, pieces, each, turned, panel):
    times, lanes = bufs.shape[2:]
    blocks = panel.shape[2] // lanes
    group = max(1, 16 // each)

    @pl.loop(0, pieces // group)
    def _(g):
        for b in range(blocks):
            tiles = []
            for i in range(group * each):
                k, place = g * group + i // each, i % each * blocks + b
                tiles.append(bufs[k, bits_s[base + k, place // lanes, place % lanes]])
            value = turn(jnp.concatenate(tiles, axis=0), group * each, times)
            panel[:, aligned(g * group * each, group * each), b * lanes : (b + 1) * lanes] = value

    total = None
    for t in range(times):
        value = lax.dot_general(turned[t], panel[t], (((1,), (1,)), ((), ())), preferred_element_type=F32)
        total = value if total is None else total + value
    return total


def last_kernel(pieces, each, *refs):
    msgs = refs[:pieces]
    group_ref, turned, before_ref, over_ref, out_ref, bufs, bits_v, bits_s, panel, sem = refs[pieces:]
    _, lanes = bufs.shape[2:]
    rows, cells = turned.shape[1:]
    copies = [pltpu.make_async_copy(msg, bufs.at[k], sem.at[k]) for k, msg in enumerate(msgs)]
    for copy in copies:
        copy.start()
    for k, copy in enumerate(copies):
        copy.wait()
        read_head(bufs.at[k], each, cells // lanes, bits_v.at[k], flagged=True)
    bits_copy = pltpu.make_async_copy(bits_v, bits_s, sem.at[pieces])
    bits_copy.start()
    size = out_ref.shape[1]
    row = lax.broadcasted_iota(I32, (size, size), 0)
    half = size // each // 2
    hi, lo = split(group_ref[0], 2)
    target = row
    for k in range(size // each):
        back = hi - k // 2
        source = jnp.where(back < 0, back + half, back) * 2 + lax.bitwise_xor(lo, k % 2)
        target = jnp.where((row >= k * each) & (row < (k + 1) * each), row + (source - k) * each, target)
    select = (lax.broadcasted_iota(I32, (size, size), 1) == target).astype(F32).astype(BF16)
    bits_copy.wait()
    over = over_ref[0] + panel_over(bufs, bits_s, 0, pieces, each)
    total = panel_products(bufs, bits_s, 0, pieces, each, turned, panel)
    value = jnp.concatenate([before_ref[...], total], axis=1)
    total = jnp.zeros(value.shape, F32)
    for _ in range(3):
        high = value.astype(BF16)
        total = total + jnp.dot(high, select, preferred_element_type=F32)
        value = value - high.astype(F32)
    out_ref[0:rows, :] = total
    out_ref[rows:, :] = jnp.broadcast_to(over, (8, size)).astype(F32)


def panel_last(msgs, turned, each, group, before, over):
    slots, times, lanes = msgs[0].shape
    rows, cells = turned.shape[1:]
    pieces = len(msgs)
    return pl.pallas_call(
        functools.partial(last_kernel, pieces, each),
        out_shape=shape_of((rows + 8, before.shape[1] + pieces * each), F32),
        in_specs=[ANY] * pieces + [SMEM, VMEM, VMEM, SMEM],
        out_specs=VMEM,
        scratch_shapes=[
            pltpu.VMEM((pieces, slots, times, lanes), BF16),
            pltpu.VMEM((pieces, 8, lanes), I32),
            pltpu.SMEM((pieces, 8, lanes), I32),
            pltpu.VMEM((times, pieces * each, cells), BF16),
            pltpu.SemaphoreType.DMA((pieces + 1,)),
        ],
        compiler_params=params(14),
        cost_estimate=cost(3),
        name="panel_last",
    )(*msgs, group[None], turned, before, over)


def partner(value, axis, count):
    return lax.ppermute(value, axis, [(i, i ^ 1) for i in range(count)])


def shifted(value, axis, count, shift, flip=0):
    return lax.ppermute(value, axis, [(i, ((i + 2 * shift) % count) ^ flip) for i in range(count)])


def row_major(value):
    return with_layout_constraint(value, Layout(tuple(range(value.ndim))))


def add_cells(part, cells):
    total = part
    for shift in range(cells // 2):
        for flip in range(2):
            if shift or flip:
                total = total + shifted(part, "cell", cells, shift, flip)
    return total


def dense_way(cells, observers, footprint, block_mask, own, time_cov, mine, sources):
    obs_rows, times, cell_local = footprint.shape
    blocks = block_mask.shape[1]
    keep = block_mask.astype(BF16)[:, None, :, None]
    feet = (footprint.reshape(obs_rows, times, blocks, cell_local // blocks) * keep).reshape(footprint.shape)

    def add(carry, _):
        total, feet, info = carry
        dx = info[0][:, None] - own[0][None, :]
        dy = info[1][:, None] - own[1][None, :]
        decay = jnp.exp(-jnp.sqrt(dx * dx + dy * dy + 1.0) / LENGTH)
        cov = (decay * (info[2][:, None] * own[2][None, :])).astype(BF16)
        total = total + jnp.dot(feet.reshape(-1, cell_local), cov, preferred_element_type=F32)
        ring = [(i, (i + 1) % cells) for i in range(cells)]
        return (total, lax.ppermute(feet, "cell", ring), lax.ppermute(info, "cell", ring)), None

    zero = jnp.zeros((obs_rows * times, cell_local), F32)
    (total, _, _), _ = lax.scan(add, (zero, feet, own), None, length=cells)
    cov_product = jnp.einsum(
        "ts,ksc->ktc", time_cov, total.reshape(obs_rows, times, cell_local), precision=lax.Precision.HIGHEST
    ).astype(BF16)
    flat = cov_product.reshape(obs_rows, times * cell_local)

    def meet(held, _):
        both = jnp.concatenate([held, partner(held, "obs", observers)], axis=0)
        part = lax.dot_general(
            flat, both.reshape(both.shape[0], -1), (((1,), (1,)), ((), ())), preferred_element_type=F32
        )
        return shifted(held, "obs", observers, 1), part

    _, parts = lax.scan(meet, jnp.take(feet, mine, axis=0), None, length=observers // 2)
    parts = parts.transpose(1, 0, 2).reshape(obs_rows, observers, -1)
    ordered = jnp.zeros_like(parts).at[:, sources].set(parts)
    return cov_product, add_cells(ordered.reshape(obs_rows, -1), cells)


def body(cells, observers, footprint, block_mask, cell_coords, cell_sigma, time_cov, error_var, panel_index):
    obs_rows, _, cell_local = footprint.shape
    blocks = block_mask.shape[1]
    group = lax.axis_index("obs")
    each = panel_index.shape[0] // observers
    half = observers // 2
    unit = math.gcd(16, obs_rows)
    slots = slot_count(obs_rows * blocks, 1 + blocks)
    chunks = chunk_sizes(slots, obs_rows * blocks, 1 + blocks)
    mask = block_mask.T

    room = slots - 2 - blocks - 1
    own_panel = pack_panel(mask, panel_index, group, footprint, each, slot_count(each * blocks, 1), room)
    ring = [own_panel]
    for _ in range(1, half):
        ring.append(shifted(ring[-1], "obs", observers, 1))
    messages = []
    for held in ring:
        messages += [held, partner(held, "obs", observers)]
    own_msg = pack_feet(mask, cell_coords, cell_sigma[None, :], footprint, chunks)
    far_msgs = []
    for shift in range(1, cells // 2):
        far_msgs.append([shifted(c, "cell", cells, shift) for c in own_msg])
    mate_msg = [partner(c, "cell", cells) for c in own_msg]
    for shift in range(1, cells // 2):
        far_msgs.append([partner(c, "cell", cells) for c in far_msgs[shift - 1]])

    dense, own_cov, info = start_call(own_msg, obs_rows, cell_local)
    near, mate_dense, mate_cov = own_call(mate_msg, dense, own_cov, info)
    near, far_cov = mate_call([msg[0] for msg in far_msgs], near, mate_dense, mate_cov, info)
    mix = mixing(time_cov, unit)
    first_cov, start = first_rows([msg[:-1] for msg in far_msgs], far_cov, near, mix, obs_rows, unit, slots)
    cut = len(messages) * 3 // 4
    cov_product, turned, before, over = late_rows(
        far_msgs, messages[:cut], each, far_cov, near, mix, start, first_cov, unit, slots
    )
    part = panel_last(messages[cut:], turned, each, group, before, over)

    def innovation_of(total, group):
        positions = jnp.arange(obs_rows, dtype=I32)
        on_diagonal = ((group * obs_rows + positions)[:, None] == panel_index[None, :]).astype(F32)
        return total + error_var[:, None] * on_diagonal

    part, late_group, late_mask = lax.optimization_barrier((part, group, mask))
    total = add_cells(part, cells)

    def again(carry):
        wanted = carry[0]
        kept, cell_info, place = (jnp.where(wanted, value, 0) for value in (late_mask, info, late_group))
        order = jnp.arange(observers, dtype=I32)
        from_group = (place // 2 - order // 2) % half * 2 + (place % 2 ^ (order % 2))
        mine = lax.dynamic_slice_in_dim(panel_index, place * each, each) - place * obs_rows
        cov_product, total = dense_way(
            cells, observers, footprint, kept.T, cell_info, time_cov, mine, from_group
        )
        return jnp.bool_(False), cov_product, row_major(innovation_of(total, place))

    carry = (total[obs_rows, 0] > 0, cov_product, row_major(innovation_of(total[:obs_rows], late_group)))
    return lax.while_loop(lambda carry: carry[0], again, carry)[1:]


def solution(mesh):
    in_specs = (
        P("obs", None, "cell"),
        P("obs", "cell"),
        P(None, "cell"),
        P("cell"),
        P(),
        P("obs"),
        P(),
    )
    out_specs = (P("obs", None, "cell"), P("obs", None))
    cells, observers = mesh.shape["cell"], mesh.shape["obs"]

    def per_device(*args):
        return body(cells, observers, *args)

    return jax.shard_map(per_device, mesh=mesh, in_specs=in_specs, out_specs=out_specs, check_vma=False)
```

```python
import functools
import math

import jax
import jax.numpy as jnp
from jax import lax
from jax.experimental import pallas as pl
from jax.experimental.pallas import tpu as pltpu
from jax.experimental.layout import Layout, with_layout_constraint
from jax.sharding import PartitionSpec as P


GRID = 64
LENGTH = GRID / 16.0
F32, BF16, I32 = jnp.float32, jnp.bfloat16, jnp.int32
SHIFT = 4
INFO = 8


VMEM = pl.BlockSpec(memory_space=pltpu.VMEM)
SMEM = pl.BlockSpec(memory_space=pltpu.SMEM)
ANY = pl.BlockSpec(memory_space=pl.ANY)
HBM = pl.BlockSpec(memory_space=pltpu.HBM)


def shape_of(shape, dtype):
    return jax.ShapeDtypeStruct(shape, dtype)


def params(mib):
    return pltpu.CompilerParams(vmem_limit_bytes=mib * 2**20)


def cost(micros):
    return pl.CostEstimate(flops=int(micros * 9e8), bytes_accessed=1_000_000, transcendentals=0)


def aligned(start, size):
    return pl.ds(pl.multiple_of(start, size), size)


def slot_count(tiles, extra):
    room = tiles / 2 + 4.1 * math.sqrt(tiles / 4)
    return extra + min(tiles + 1, 2 * math.ceil(room / 2) + 1)


def chunk_sizes(slots, tiles, extra):
    most = min(slots - 2, extra + math.ceil(tiles / 4 + 3 * math.sqrt(tiles / 8)))
    return most, slots - most


def pack_rows(mask_at, feet_at, begin, end, blocks, buf, carry):
    slots, _, lanes = buf.shape
    row_of = lax.broadcasted_iota(I32, (8, lanes), 0)
    lane_of = lax.broadcasted_iota(I32, (8, lanes), 1)
    flat = row_of * lanes + lane_of
    batch = math.gcd(2, end - begin)

    def some(i, carry):
        pos, head, ends = carry
        first = begin + i * batch
        tiles = [[feet_at(first + j, b) for b in range(blocks)] for j in range(batch)]
        kept = [[mask_at(first + j, b) for b in range(blocks)] for j in range(batch)]
        for j in range(batch):
            for b in range(blocks):
                buf[jnp.minimum(pos, slots - 1)] = tiles[j][b]
                head = jnp.where(flat == (first + j) * blocks + b, kept[j][b] * pos, head)
                pos = pos + kept[j][b]
            ends = jnp.where(lane_of == first + j, pos, ends)
        return pos, head, ends

    return lax.fori_loop(0, (end - begin) // batch, some, carry)


def no_rows(first, lanes):
    zeros = jnp.zeros((8, lanes), I32)
    return jnp.int32(first), zeros, zeros


def write_head(carry, rows, blocks, buf, head_v, flag=None):
    lanes = buf.shape[2]
    deep = -(-rows * blocks // lanes)
    _, head, ends = carry
    low = (1 << SHIFT) - 1
    head_v[...] = jnp.zeros_like(head_v)
    head_v[0:deep, :] = (head >> SHIFT)[0:deep].astype(F32)
    head_v[deep : 2 * deep, :] = (head & low)[0:deep].astype(F32)
    head_v[2 * deep : 2 * deep + 1, :] = (ends >> SHIFT)[0:1].astype(F32)
    head_v[2 * deep + 1 : 2 * deep + 2, :] = (ends & low)[0:1].astype(F32)
    if flag is not None:
        head_v[2 * deep + 2 : 2 * deep + 3, :] = jnp.broadcast_to(flag, (1, lanes)).astype(F32)
    buf[0] = head_v[...].astype(BF16)


def pack_feet_kernel(chunks, mask_ref, coords_hbm, sigma_hbm, feet_ref, *rest):
    outs, (coords_ref, sigma_ref, feet, buf, head_v, small_sem, in_sem, sem) = (
        rest[: len(chunks)],
        rest[len(chunks) :],
    )
    blocks, rows = mask_ref.shape
    small = [
        pltpu.make_async_copy(src, dst, small_sem.at[k])
        for k, (src, dst) in enumerate(((coords_hbm, coords_ref), (sigma_hbm, sigma_ref)))
    ]
    for copy in small:
        copy.start()
    times, lanes = buf.shape[1:]
    groups = in_sem.shape[0]
    each = rows // groups
    loads = [
        pltpu.make_async_copy(feet_ref.at[pl.ds(g * each, each)], feet.at[pl.ds(g * each, each)], in_sem.at[g])
        for g in range(groups)
    ]
    for load in loads:
        load.start()
    for copy in small:
        copy.wait()
    sigma = sigma_ref[...]
    high = sigma.astype(BF16).astype(F32)
    middle = (sigma - high).astype(BF16).astype(F32)
    lowest = sigma - high - middle
    at = lax.broadcasted_iota(I32, (times, sigma.shape[1]), 0)
    info = jnp.zeros(at.shape, F32)
    for k, row in enumerate((coords_ref[0:1, :].astype(F32), coords_ref[1:2, :].astype(F32), high, middle, lowest)):
        info = jnp.where(at == k, row, info)
    info = info.astype(BF16)
    for b in range(blocks):
        buf[1 + b] = info[:, b * lanes : (b + 1) * lanes]
    carry = no_rows(1 + blocks, lanes)
    for g in range(groups):
        loads[g].wait()
        carry = pack_rows(
            lambda o, b: mask_ref[b, o],
            lambda o, b: feet[o, :, b * lanes : (b + 1) * lanes],
            g * each,
            (g + 1) * each,
            blocks,
            buf,
            carry,
        )
    write_head(carry, rows, blocks, buf, head_v)
    copies, first = [], 0
    for k, size in enumerate(chunks):
        copies.append(pltpu.make_async_copy(buf.at[pl.ds(first, size)], outs[k], sem.at[k]))
        first += size
    for copy in copies:
        copy.start()
    for copy in copies:
        copy.wait()


def pack_feet(mask, coords, sigma, feet, chunks):
    rows, times, cells = feet.shape
    lanes = cells // mask.shape[0]
    groups = math.gcd(4, rows)
    return pl.pallas_call(
        functools.partial(pack_feet_kernel, chunks),
        out_shape=tuple(shape_of((size, times, lanes), BF16) for size in chunks),
        in_specs=[SMEM, HBM, HBM, HBM],
        out_specs=(ANY,) * len(chunks),
        scratch_shapes=[
            pltpu.VMEM(coords.shape, I32),
            pltpu.VMEM(sigma.shape, F32),
            pltpu.VMEM((rows, times, cells), BF16),
            pltpu.VMEM((sum(chunks), times, lanes), BF16),
            pltpu.VMEM((times, lanes), F32),
            pltpu.SemaphoreType.DMA((2,)),
            pltpu.SemaphoreType.DMA((groups,)),
            pltpu.SemaphoreType.DMA((len(chunks),)),
        ],
        compiler_params=params(12),
        cost_estimate=cost(3),
        name="pack_feet",
    )(mask, coords, sigma, feet)


def pack_panel_kernel(room, mask_ref, mask_hbm, index_ref, group_ref, member_ref, feet_ref, out_ref, mask_v, rows_buf, head_v, small_sem, sem):
    count = rows_buf.shape[0]
    blocks, obs = mask_ref.shape
    lanes = out_ref.shape[2]
    mask_copy = pltpu.make_async_copy(mask_hbm, mask_v, small_sem.at[0])
    mask_copy.start()
    base = group_ref[0]
    rows = [jnp.clip(index_ref[base * count + j] - base * obs, 0, obs - 1) for j in range(count)]
    copies = [pltpu.make_async_copy(feet_ref.at[rows[j]], rows_buf.at[j], sem.at[j]) for j in range(count)]
    for copy in copies:
        copy.start()
    mask_copy.wait()
    flag = (jnp.sum(mask_v[...].astype(F32), axis=(0, 1), keepdims=True) > room).astype(I32)
    for copy in copies:
        copy.wait()

    def mask_at(o, b):
        return mask_ref[b, jnp.clip(index_ref[base * count + o] - base * obs, 0, obs - 1)]

    carry = pack_rows(
        mask_at, lambda o, b: rows_buf[o, :, b * lanes : (b + 1) * lanes], 0, count, blocks, out_ref, no_rows(1, lanes)
    )
    write_head(carry, count, blocks, out_ref, head_v, flag)


def pack_panel(mask, panel_index, group, member, feet, count, slots, room):
    _, times, cells = feet.shape
    lanes = cells // mask.shape[0]
    return pl.pallas_call(
        functools.partial(pack_panel_kernel, room),
        out_shape=shape_of((slots, times, lanes), BF16),
        in_specs=[SMEM, HBM, SMEM, SMEM, SMEM, HBM],
        out_specs=VMEM,
        scratch_shapes=[
            pltpu.VMEM(mask.shape, I32),
            pltpu.VMEM((count, times, cells), BF16),
            pltpu.VMEM((times, lanes), F32),
            pltpu.SemaphoreType.DMA((1,)),
            pltpu.SemaphoreType.DMA((count,)),
        ],
        compiler_params=params(8),
        cost_estimate=cost(2),
        name="pack_panel",
    )(mask, mask, panel_index, group[None], member[None], feet)


def fetch(chunks, buf, sem):
    copies, first = [], 0
    for k, chunk in enumerate(chunks):
        copies.append(pltpu.make_async_copy(chunk, buf.at[pl.ds(first, chunk.shape[0])], sem.at[k]))
        copies[-1].start()
        first += chunk.shape[0]
    return copies


def read_head(buf, rows, blocks, bits_v, flagged=False):
    slots, _, lanes = buf.shape
    deep = -(-rows * blocks // lanes)
    head = buf[0].astype(F32)
    scale = float(1 << SHIFT)
    bits_v[0:deep, :] = jnp.minimum(head[0:deep] * scale + head[deep : 2 * deep], slots - 1.0).astype(I32)
    bits_v[5:6, :] = (head[2 * deep : 2 * deep + 1] * scale + head[2 * deep + 1 : 2 * deep + 2]).astype(I32)
    if flagged:
        bits_v[6:7, :] = head[2 * deep + 2 : 2 * deep + 3].astype(I32)
    buf[0] = jnp.zeros(buf.shape[1:], buf.dtype)


def copy_in(src, dst, sem):
    copy = pltpu.make_async_copy(src, dst, sem)
    copy.start()
    copy.wait()


def split(number, size):
    if size & (size - 1):
        return lax.div(number, size), lax.rem(number, size)
    return lax.shift_right_logical(number, size.bit_length() - 1), lax.bitwise_and(number, size - 1)


def expand(buf, bits, first, count, blocks, store, unrolled=False):
    lanes = buf.shape[2]
    batch = math.gcd(2, count)

    def some(i, _):
        tiles = []
        for j in range(batch):
            row, col = split(jnp.int32((first + i * batch + j) * blocks), lanes)
            tiles += [buf[bits[row, col + b]] for b in range(blocks)]
        for j in range(batch):
            for b in range(blocks):
                store(i * batch + j, b, tiles[j * blocks + b])
        return 0

    if unrolled:
        for i in range(count // batch):
            some(i, 0)
    else:
        lax.fori_loop(0, count // batch, some, 0)


def into(dense, times, lanes, offset, first=0):
    def store(i, b, tile):
        at = aligned((first + i) * times, times)
        dense[at, offset + b * lanes : offset + (b + 1) * lanes] = tile.astype(dense.dtype)

    return store


def read_info(buf, blocks, row_v, turned):
    _, lanes = buf.shape[1:]
    for b in range(blocks):
        tile = buf[1 + b].astype(F32)[0:INFO]
        sigma = tile[2:3] + tile[3:4] + tile[4:5]
        tile = jnp.where(lax.broadcasted_iota(I32, tile.shape, 0) == 2, sigma, tile)
        at = slice(b * lanes, (b + 1) * lanes)
        if row_v is not None:
            row_v[:, at] = tile
        if turned is not None:
            turned[at, :] = tile.T


def fill_covariance(dst, dst_first, src_first, rows, turned, own):
    x, y, s = own[0:1, :], own[1:2, :], own[2:3, :]
    step = min(32, rows)
    for i in range(rows // step):
        at = aligned(src_first + i * step, step)
        dx = turned[at, 0:1] - x
        dy = turned[at, 1:2] - y
        square = dx * dx + dy * dy + 1.0
        decay = jnp.exp(square * lax.rsqrt(square) * (-1.0 / LENGTH))
        dst[aligned(dst_first + i * step, step), :] = (decay * (turned[at, 2:3] * s)).astype(BF16)


def start_kernel(chunks, *refs):
    msg = refs[:chunks]
    dense, cov, info_ref, buf, bits_v, bits_s, turned, sem = refs[chunks:]
    times, lanes = buf.shape[1:]
    cells = cov.shape[1]
    blocks = cells // lanes
    rows = dense.shape[0] // times
    copies = fetch(msg, buf, sem)
    for copy in copies:
        copy.wait()
    read_info(buf, blocks, info_ref, turned)
    read_head(buf, rows, blocks, bits_v)
    copy = pltpu.make_async_copy(bits_v, bits_s, sem.at[chunks])
    copy.start()
    half = cells // 2
    fine = math.gcd(4, rows // 2)

    @pl.loop(0, fine)
    def _(i):
        fill_covariance(cov, i * (half // fine), i * (half // fine), half // fine, turned, info_ref)

    copy.wait()

    @pl.loop(0, fine)
    def _(i):
        first = half + i * (half // fine)
        fill_covariance(cov, first, first, half // fine, turned, info_ref)
        some = rows // fine
        expand(buf, bits_s, i * some, some, blocks, into(dense, times, lanes, 0, i * some), unrolled=True)


def start_call(own_msg, rows, cells):
    times, lanes = own_msg[0].shape[1:]
    slots = sum(chunk.shape[0] for chunk in own_msg)
    chunks = len(own_msg)
    return pl.pallas_call(
        functools.partial(start_kernel, chunks),
        out_shape=(
            shape_of((rows * times, cells), BF16),
            shape_of((cells, cells), BF16),
            shape_of((INFO, cells), F32),
        ),
        in_specs=[ANY] * chunks,
        out_specs=(VMEM,) * 3,
        scratch_shapes=[
            pltpu.VMEM((slots, times, lanes), BF16),
            pltpu.VMEM((8, lanes), I32),
            pltpu.SMEM((8, lanes), I32),
            pltpu.VMEM((cells, INFO), F32),
            pltpu.SemaphoreType.DMA((chunks + 1,)),
        ],
        compiler_params=params(12),
        cost_estimate=cost(4),
        name="own_start",
    )(*own_msg)


def own_kernel(chunks, *refs):
    msg = refs[:chunks]
    dense, cov, info_ref, out_ref, mate_dense, next_ref, buf, bits_v, bits_s, turned, sem = refs[chunks:]
    times, lanes = buf.shape[1:]
    cells = cov.shape[1]
    blocks = cells // lanes
    rows = dense.shape[0] // times
    tall = min(256, rows * times)
    steps = rows * times // tall
    part = cells // steps
    for copy in fetch(msg, buf, sem):
        copy.wait()
    read_info(buf, blocks, None, turned)
    read_head(buf, rows, blocks, bits_v)
    copy_in(bits_v, bits_s, sem.at[chunks])

    @pl.loop(0, steps)
    def _(u):
        here = aligned(u * tall, tall)
        fill_covariance(next_ref, u * part, u * part, part, turned, info_ref)
        out_ref[here, :] = jnp.dot(dense[here, :], cov[...], preferred_element_type=F32)
        some = rows // steps
        expand(buf, bits_s, u * some, some, blocks, into(mate_dense, times, lanes, 0, u * some), unrolled=True)


def own_call(mate_msg, dense, cov, info):
    times, lanes = mate_msg[0].shape[1:]
    cells = cov.shape[1]
    slots = sum(chunk.shape[0] for chunk in mate_msg)
    chunks = len(mate_msg)
    return pl.pallas_call(
        functools.partial(own_kernel, chunks),
        out_shape=(shape_of(dense.shape, F32), shape_of(dense.shape, BF16), shape_of((cells, cells), BF16)),
        in_specs=[ANY] * chunks + [VMEM] * 3,
        out_specs=(VMEM,) * 3,
        scratch_shapes=[
            pltpu.VMEM((slots, times, lanes), BF16),
            pltpu.VMEM((8, lanes), I32),
            pltpu.SMEM((8, lanes), I32),
            pltpu.VMEM((cells, INFO), F32),
            pltpu.SemaphoreType.DMA((chunks + 1,)),
        ],
        compiler_params=params(16),
        cost_estimate=cost(6),
        name="own_product",
    )(*mate_msg, dense, cov, info)


def mate_kernel(count, *refs):
    firsts = refs[:count]
    near_ref, dense, cov_ref, info_ref, out_ref, far_ref, info_buf, turned, sem = refs[count:]
    _, lanes = info_buf.shape[2:]
    cells = cov_ref.shape[1]
    blocks = cells // lanes
    tall = min(256, dense.shape[0])
    steps = dense.shape[0] // tall
    part = count * cells // steps
    copies = []
    for k in range(count):
        copies.append(pltpu.make_async_copy(firsts[k].at[pl.ds(0, 1 + blocks)], info_buf.at[k], sem.at[k]))
        copies[-1].start()
    for k in range(count):
        copies[k].wait()
        read_info(info_buf.at[k], blocks, None, turned.at[pl.ds(k * cells, cells)])

    @pl.loop(0, steps)
    def _(u):
        here = aligned(u * tall, tall)
        fill_covariance(far_ref, u * part, u * part, part, turned, info_ref)
        out_ref[here, :] = near_ref[here, :] + jnp.dot(dense[here, :], cov_ref[...], preferred_element_type=F32)


def mate_call(firsts, near, mate_dense, cov, info):
    times, lanes = firsts[0].shape[1:]
    cells = cov.shape[1]
    blocks = cells // lanes
    count = len(firsts)
    return pl.pallas_call(
        functools.partial(mate_kernel, count),
        out_shape=(shape_of(near.shape, F32), shape_of((count * cells, cells), BF16)),
        in_specs=[ANY] * count + [VMEM] * 4,
        out_specs=(VMEM, VMEM),
        scratch_shapes=[
            pltpu.VMEM((count, 1 + blocks, times, lanes), BF16),
            pltpu.VMEM((count * cells, INFO), F32),
            pltpu.SemaphoreType.DMA((count,)),
        ],
        input_output_aliases={count: 0},
        compiler_params=params(16),
        cost_estimate=cost(8),
        name="mate_product",
    )(*firsts, near, mate_dense, cov, info)


def mixed_unit(mix_ref, value):
    high = value.astype(BF16)
    low = (value - high.astype(F32)).astype(BF16)
    stacked = jnp.concatenate([high, low, high], axis=0)
    return jnp.dot(mix_ref[...], stacked, preferred_element_type=F32).astype(BF16)


def turn(value, rows, times):
    return jnp.swapaxes(value.reshape(rows, times, value.shape[1]), 0, 1)


def unit_step(u, count, unit, bufs, bits_s, dense_a, dense_b, near_ref, cov_ref, mix_ref, rows):
    times, _ = bufs.shape[2:]
    cells = near_ref.shape[1]
    few = count // 2
    here = aligned(u * unit * times, unit * times)
    place(u, few, count, unit, bufs, bits_s, dense_b, cells)
    value = near_ref[here, :] + jnp.dot(dense_a[...], cov_ref[: few * cells, :], preferred_element_type=F32)
    place(jnp.minimum(u + 1, rows // unit - 1), 0, few, unit, bufs, bits_s, dense_a, cells)
    value = value + jnp.dot(dense_b[...], cov_ref[few * cells :, :], preferred_element_type=F32)
    return mixed_unit(mix_ref, value)


def place(u, begin, end, unit, bufs, bits_s, dense, cells):
    times, lanes = bufs.shape[2:]
    for k in range(begin, end):
        store = into(dense, times, lanes, (k - begin) * cells)
        expand(bufs.at[k], bits_s.at[k], u * unit, unit, cells // lanes, store, unrolled=bufs.shape[0] <= 4)


def first_kernel(count, chunks, unit, *refs):
    msgs = [refs[k * chunks : (k + 1) * chunks] for k in range(count)]
    cov_ref, near_ref, mix_ref, out_ref, next_ref, bufs, bits_v, bits_s, dense_a, dense_b, sem = refs[count * chunks :]
    times, lanes = bufs.shape[2:]
    cells = near_ref.shape[1]
    blocks = cells // lanes
    rows = out_ref.shape[0]
    limit = sum(chunk.shape[0] for chunk in msgs[0])
    copies = [fetch(msgs[k], bufs.at[k], sem.at[k]) for k in range(count)]
    for k in range(count):
        for copy in copies[k]:
            copy.wait()
        read_head(bufs.at[k], rows, blocks, bits_v.at[k])
    copy_in(bits_v, bits_s, sem.at[count, 0])
    ready = jnp.int32(0)
    for u in range(rows // unit):
        whole = jnp.int32(1)
        for k in range(count):
            whole = whole * (bits_s[k, 5, (u + 1) * unit - 1] <= limit).astype(I32)
        ready = ready + whole
    next_ref[0] = ready
    place(jnp.int32(0), 0, count // 2, unit, bufs, bits_s, dense_a, cells)

    def step(u, _):
        mixed = unit_step(u, count, unit, bufs, bits_s, dense_a, dense_b, near_ref, cov_ref, mix_ref, rows)
        out_ref[aligned(u * unit, unit)] = mixed.reshape(unit, times, cells)
        return 0

    lax.fori_loop(0, ready, step, 0)


def rows_scratch(count, chunks, slots, times, lanes, unit, cells, more):
    return [
        pltpu.VMEM((count, slots, times, lanes), BF16),
        pltpu.VMEM((count + more, 8, lanes), I32),
        pltpu.SMEM((count + more, 8, lanes), I32),
        pltpu.VMEM((unit * times, count // 2 * cells), BF16),
        pltpu.VMEM((unit * times, (count - count // 2) * cells), BF16),
        pltpu.SemaphoreType.DMA((count + 1, chunks)),
    ]


def first_rows(msgs, cov, near, mix, rows, unit, slots):
    times, lanes = msgs[0][0].shape[1:]
    cells = near.shape[1]
    count, chunks = len(msgs), len(msgs[0])
    flat = [chunk for msg in msgs for chunk in msg]
    return pl.pallas_call(
        functools.partial(first_kernel, count, chunks, unit),
        out_shape=(shape_of((rows, times, cells), BF16), shape_of((1,), I32)),
        in_specs=[ANY] * len(flat) + [VMEM] * 3,
        out_specs=(VMEM, SMEM),
        scratch_shapes=rows_scratch(count, chunks, slots, times, lanes, unit, cells, 0),
        compiler_params=params(16),
        cost_estimate=cost(7),
        name="first_rows",
    )(*flat, cov, near, mix)


def late_kernel(count, chunks, unit, pieces, each, *refs):
    msgs = [refs[k * chunks : (k + 1) * chunks] for k in range(count)]
    panel_msgs = refs[count * chunks : count * chunks + pieces]
    refs = refs[count * chunks + pieces :]
    cov_ref, near_ref, mix_ref, start_ref, done_ref, out_ref, turned_ref, part_ref, over_ref = refs[:9]
    bufs, bits_v, bits_s, dense_a, dense_b, sem, panel_bufs, stage, panel, panel_sem, out_sem = refs[9:]
    times, lanes = bufs.shape[2:]
    cells = near_ref.shape[1]
    blocks = cells // lanes
    rows = stage.shape[0]
    copies = [fetch(msgs[k], bufs.at[k], sem.at[k]) for k in range(count)]
    panel_copies = [pltpu.make_async_copy(msg, panel_bufs.at[k], panel_sem.at[k]) for k, msg in enumerate(panel_msgs)]
    for copy in panel_copies:
        copy.start()
    for k in range(count):
        for copy in copies[k]:
            copy.wait()
        read_head(bufs.at[k], rows, blocks, bits_v.at[k])
    for k, copy in enumerate(panel_copies):
        copy.wait()
        read_head(panel_bufs.at[k], each, blocks, bits_v.at[count + k], flagged=True)
    bits_copy = pltpu.make_async_copy(bits_v, bits_s, sem.at[count, 0])
    bits_copy.start()
    first = start_ref[0]

    def outgoing(u, src):
        at = aligned(u * unit, unit)
        return pltpu.make_async_copy(src.at[at], out_ref.at[at], out_sem.at[u])

    def carry_over(u, _):
        outgoing(u, done_ref).start()
        at = aligned(u * unit, unit)
        turned_ref[:, at, :] = turn(done_ref[at].reshape(unit * times, cells), unit, times)
        return 0

    lax.fori_loop(0, first, carry_over, 0)
    bits_copy.wait()
    place(jnp.minimum(first, rows // unit - 1), 0, count // 2, unit, bufs, bits_s, dense_a, cells)

    def step(u, _):
        mixed = unit_step(u, count, unit, bufs, bits_s, dense_a, dense_b, near_ref, cov_ref, mix_ref, rows)
        at = aligned(u * unit, unit)
        stage[at] = mixed.reshape(unit, times, cells)
        outgoing(u, stage).start()
        turned_ref[:, at, :] = turn(mixed, unit, times)
        return 0

    lax.fori_loop(first, rows // unit, step, 0)
    over_ref[0] = panel_over(panel_bufs, bits_s, count, pieces, each)
    part_ref[...] = panel_products(panel_bufs, bits_s, count, pieces, each, turned_ref, panel)

    def settle(u, _):
        outgoing(u, stage).wait()
        return 0

    lax.fori_loop(0, rows // unit, settle, 0)


def late_rows(msgs, panel_msgs, each, cov, near, mix, start, done, unit, slots):
    times, lanes = msgs[0][0].shape[1:]
    rows, _, cells = done.shape
    count, chunks, pieces = len(msgs), len(msgs[0]), len(panel_msgs)
    flat = [chunk for msg in msgs for chunk in msg] + list(panel_msgs)
    return pl.pallas_call(
        functools.partial(late_kernel, count, chunks, unit, pieces, each),
        out_shape=(
            shape_of(done.shape, BF16),
            shape_of((times, rows, cells), BF16),
            shape_of((rows, pieces * each), F32),
            shape_of((1,), I32),
        ),
        in_specs=[ANY] * len(flat) + [VMEM] * 3 + [SMEM, VMEM],
        out_specs=(HBM, VMEM, VMEM, SMEM),
        scratch_shapes=rows_scratch(count, chunks, slots, times, lanes, unit, cells, pieces)
        + [
            pltpu.VMEM((pieces, panel_msgs[0].shape[0], times, lanes), BF16),
            pltpu.VMEM((rows, times, cells), BF16),
            pltpu.VMEM((times, pieces * each, cells), BF16),
            pltpu.SemaphoreType.DMA((pieces,)),
            pltpu.SemaphoreType.DMA((rows // unit,)),
        ],
        compiler_params=params(20),
        cost_estimate=cost(9),
        name="late_rows",
    )(*flat, cov, near, mix, start, done)


def mix_kernel(unit, time_ref, out_ref):
    times = time_ref.shape[0]
    size = unit * times
    value = time_ref[...]
    high = value.astype(BF16)
    low = (value - high.astype(F32)).astype(BF16)

    def same(shape, dim):
        index = lax.broadcasted_iota(I32, shape, 1 - dim) % times
        return (index == lax.broadcasted_iota(I32, shape, dim)).astype(F32).astype(BF16)

    row = lax.broadcasted_iota(I32, (size, size), 0)
    col = lax.broadcasted_iota(I32, (size, size), 1)
    for j, part in enumerate((high, high, low)):
        spread = jnp.dot(same((size, times), 1), part, preferred_element_type=F32).astype(BF16)
        spread = jnp.dot(spread, same((times, size), 0), preferred_element_type=F32)
        out_ref[:, j * size : (j + 1) * size] = jnp.where(row // times == col // times, spread, 0.0).astype(BF16)


def mixing(time_cov, unit):
    size = unit * time_cov.shape[0]
    return pl.pallas_call(
        functools.partial(mix_kernel, unit),
        out_shape=shape_of((size, 3 * size), BF16),
        in_specs=[VMEM],
        out_specs=VMEM,
        compiler_params=params(8),
        cost_estimate=cost(1),
        name="mixing",
    )(time_cov)


def panel_over(bufs, bits_s, base, pieces, each):
    slots, _, _ = bufs.shape[1:]
    over = jnp.int32(0)
    for k in range(pieces):
        ends = bits_s.shape[1] - 3
        over = over + (bits_s[base + k, ends, each - 1] > slots - 1).astype(I32) + bits_s[base + k, ends + 1, 0]
    return over


def panel_products(bufs, bits_s, base, pieces, each, turned, panel):
    times, lanes = bufs.shape[2:]
    blocks = panel.shape[2] // lanes
    group = max(1, 16 // each)

    @pl.loop(0, pieces // group)
    def _(g):
        for b in range(blocks):
            tiles = []
            for i in range(group * each):
                k, place = g * group + i // each, i % each * blocks + b
                tiles.append(bufs[k, bits_s[base + k, place // lanes, place % lanes]])
            value = turn(jnp.concatenate(tiles, axis=0), group * each, times)
            panel[:, aligned(g * group * each, group * each), b * lanes : (b + 1) * lanes] = value

    total = None
    for t in range(times):
        value = lax.dot_general(turned[t], panel[t], (((1,), (1,)), ((), ())), preferred_element_type=F32)
        total = value if total is None else total + value
    return total


def last_kernel(pieces, each, *refs):
    msgs = refs[:pieces]
    group_ref, member_ref, index_ref, var_ref, turned, before_ref, over_ref, out_ref, bufs, bits_v, bits_s, panel, sem = refs[pieces:]
    _, lanes = bufs.shape[2:]
    rows, cells = turned.shape[1:]
    copies = [pltpu.make_async_copy(msg, bufs.at[k], sem.at[k]) for k, msg in enumerate(msgs)]
    for copy in copies:
        copy.start()
    for k, copy in enumerate(copies):
        copy.wait()
        read_head(bufs.at[k], each, cells // lanes, bits_v.at[k], flagged=True)
    bits_copy = pltpu.make_async_copy(bits_v, bits_s, sem.at[pieces])
    bits_copy.start()
    size = out_ref.shape[1]
    row = lax.broadcasted_iota(I32, (size, size), 0)
    half = size // each // 2
    hi, lo = split(group_ref[0], 2)
    target = row
    for k in range(size // each):
        back = hi - k // 2
        source = jnp.where(back < 0, back + half, back) * 2 + lax.bitwise_xor(lo, k % 2)
        target = jnp.where((row >= k * each) & (row < (k + 1) * each), row + (source - k) * each, target)
    select = (lax.broadcasted_iota(I32, (size, size), 1) == target).astype(F32).astype(BF16)
    spot = lax.broadcasted_iota(I32, (rows, size), 0) + group_ref[0] * rows
    variance = jnp.broadcast_to(var_ref[...], (8, rows)).T[:, 0:1]
    diagonal = jnp.where((spot == index_ref[...]) & (member_ref[0] == 0), variance, 0.0)
    bits_copy.wait()
    over = over_ref[0] + panel_over(bufs, bits_s, 0, pieces, each)
    total = panel_products(bufs, bits_s, 0, pieces, each, turned, panel)
    value = jnp.concatenate([before_ref[...], total], axis=1)
    total = diagonal
    for _ in range(3):
        high = value.astype(BF16)
        total = total + jnp.dot(high, select, preferred_element_type=F32)
        value = value - high.astype(F32)
    out_ref[0:rows, :] = total
    out_ref[rows:, :] = jnp.broadcast_to(over, (8, size)).astype(F32)


def panel_last(msgs, turned, each, group, member, panel_index, error_var, before, over):
    slots, times, lanes = msgs[0].shape
    rows, cells = turned.shape[1:]
    pieces = len(msgs)
    return pl.pallas_call(
        functools.partial(last_kernel, pieces, each),
        out_shape=shape_of((rows + 8, before.shape[1] + pieces * each), F32),
        in_specs=[ANY] * pieces + [SMEM, SMEM, VMEM, VMEM, VMEM, VMEM, SMEM],
        out_specs=VMEM,
        scratch_shapes=[
            pltpu.VMEM((pieces, slots, times, lanes), BF16),
            pltpu.VMEM((pieces, 8, lanes), I32),
            pltpu.SMEM((pieces, 8, lanes), I32),
            pltpu.VMEM((times, pieces * each, cells), BF16),
            pltpu.SemaphoreType.DMA((pieces + 1,)),
        ],
        compiler_params=params(14),
        cost_estimate=cost(3),
        name="panel_last",
    )(*msgs, group[None], member[None], panel_index[None, :], error_var[None, :], turned, before, over)


def partner(value, axis, count):
    return lax.ppermute(value, axis, [(i, i ^ 1) for i in range(count)])


def shifted(value, axis, count, shift, flip=0):
    return lax.ppermute(value, axis, [(i, ((i + 2 * shift) % count) ^ flip) for i in range(count)])


def row_major(value):
    return with_layout_constraint(value, Layout(tuple(range(value.ndim))))


def add_cells(part, cells):
    total = part
    for shift in range(cells // 2):
        for flip in range(2):
            if shift or flip:
                total = total + shifted(part, "cell", cells, shift, flip)
    return total


def dense_way(cells, observers, footprint, block_mask, own, time_cov, mine, sources):
    obs_rows, times, cell_local = footprint.shape
    blocks = block_mask.shape[1]
    keep = block_mask.astype(BF16)[:, None, :, None]
    feet = (footprint.reshape(obs_rows, times, blocks, cell_local // blocks) * keep).reshape(footprint.shape)

    def add(carry, _):
        total, feet, info = carry
        dx = info[0][:, None] - own[0][None, :]
        dy = info[1][:, None] - own[1][None, :]
        decay = jnp.exp(-jnp.sqrt(dx * dx + dy * dy + 1.0) / LENGTH)
        cov = (decay * (info[2][:, None] * own[2][None, :])).astype(BF16)
        total = total + jnp.dot(feet.reshape(-1, cell_local), cov, preferred_element_type=F32)
        ring = [(i, (i + 1) % cells) for i in range(cells)]
        return (total, lax.ppermute(feet, "cell", ring), lax.ppermute(info, "cell", ring)), None

    zero = jnp.zeros((obs_rows * times, cell_local), F32)
    (total, _, _), _ = lax.scan(add, (zero, feet, own), None, length=cells)
    cov_product = jnp.einsum(
        "ts,ksc->ktc", time_cov, total.reshape(obs_rows, times, cell_local), precision=lax.Precision.HIGHEST
    ).astype(BF16)
    flat = cov_product.reshape(obs_rows, times * cell_local)

    def meet(held, _):
        both = jnp.concatenate([held, partner(held, "obs", observers)], axis=0)
        part = lax.dot_general(
            flat, both.reshape(both.shape[0], -1), (((1,), (1,)), ((), ())), preferred_element_type=F32
        )
        return shifted(held, "obs", observers, 1), part

    _, parts = lax.scan(meet, jnp.take(feet, mine, axis=0), None, length=observers // 2)
    parts = parts.transpose(1, 0, 2).reshape(obs_rows, observers, -1)
    ordered = jnp.zeros_like(parts).at[:, sources].set(parts)
    return cov_product, add_cells(ordered.reshape(obs_rows, -1), cells)


def body(cells, observers, footprint, block_mask, cell_coords, cell_sigma, time_cov, error_var, panel_index):
    obs_rows, _, cell_local = footprint.shape
    blocks = block_mask.shape[1]
    group = lax.axis_index("obs")
    each = panel_index.shape[0] // observers
    half = observers // 2
    member = lax.axis_index("cell")
    unit = math.gcd(16, obs_rows)
    slots = slot_count(obs_rows * blocks, 1 + blocks)
    chunks = chunk_sizes(slots, obs_rows * blocks, 1 + blocks)
    mask = block_mask.T

    room = slots - 2 - blocks - 1
    own_panel = pack_panel(mask, panel_index, group, member, footprint, each, slot_count(each * blocks, 1), room)
    ring = [own_panel]
    for _ in range(1, half):
        ring.append(shifted(ring[-1], "obs", observers, 1))
    messages = []
    for held in ring:
        messages += [held, partner(held, "obs", observers)]
    own_msg = pack_feet(mask, cell_coords, cell_sigma[None, :], footprint, chunks)
    far_msgs = []
    for shift in range(1, cells // 2):
        far_msgs.append([shifted(c, "cell", cells, shift) for c in own_msg])
    mate_msg = [partner(c, "cell", cells) for c in own_msg]
    for shift in range(1, cells // 2):
        far_msgs.append([partner(c, "cell", cells) for c in far_msgs[shift - 1]])

    dense, own_cov, info = start_call(own_msg, obs_rows, cell_local)
    near, mate_dense, mate_cov = own_call(mate_msg, dense, own_cov, info)
    near, far_cov = mate_call([msg[0] for msg in far_msgs], near, mate_dense, mate_cov, info)
    mix = mixing(time_cov, unit)
    first_cov, start = first_rows([msg[:-1] for msg in far_msgs], far_cov, near, mix, obs_rows, unit, slots)
    cut = len(messages) * 3 // 4
    cov_product, turned, before, over = late_rows(
        far_msgs, messages[:cut], each, far_cov, near, mix, start, first_cov, unit, slots
    )
    part = panel_last(messages[cut:], turned, each, group, member, panel_index, error_var, before, over)

    part, late_group, late_mask = lax.optimization_barrier((part, group, mask))
    total = add_cells(part, cells)

    def again(carry):
        wanted = carry[0]
        kept, cell_info, place = (jnp.where(wanted, value, 0) for value in (late_mask, info, late_group))
        order = jnp.arange(observers, dtype=I32)
        from_group = (place // 2 - order // 2) % half * 2 + (place % 2 ^ (order % 2))
        mine = lax.dynamic_slice_in_dim(panel_index, place * each, each) - place * obs_rows
        cov_product, total = dense_way(
            cells, observers, footprint, kept.T, cell_info, time_cov, mine, from_group
        )
        positions = jnp.arange(obs_rows, dtype=I32) + place * obs_rows
        on_diagonal = (positions[:, None] == panel_index[None, :]).astype(F32)
        return jnp.bool_(False), cov_product, row_major(total + error_var[:, None] * on_diagonal)

    carry = (total[obs_rows, 0] > 0, cov_product, row_major(total[:obs_rows]))
    return lax.while_loop(lambda carry: carry[0], again, carry)[1:]


def solution(mesh):
    in_specs = (
        P("obs", None, "cell"),
        P("obs", "cell"),
        P(None, "cell"),
        P("cell"),
        P(),
        P("obs"),
        P(),
    )
    out_specs = (P("obs", None, "cell"), P("obs", None))
    cells, observers = mesh.shape["cell"], mesh.shape["obs"]

    def per_device(*args):
        return body(cells, observers, *args)

    return jax.shard_map(per_device, mesh=mesh, in_specs=in_specs, out_specs=out_specs, check_vma=False)
```

```python
import functools
import math

import jax
import jax.numpy as jnp
from jax import lax
from jax.experimental import pallas as pl
from jax.experimental.pallas import tpu as pltpu
from jax.experimental.layout import Layout, with_layout_constraint
from jax.sharding import PartitionSpec as P


GRID = 64
LENGTH = GRID / 16.0
F32, BF16, I32 = jnp.float32, jnp.bfloat16, jnp.int32
SHIFT = 4
INFO = 8


VMEM = pl.BlockSpec(memory_space=pltpu.VMEM)
SMEM = pl.BlockSpec(memory_space=pltpu.SMEM)
ANY = pl.BlockSpec(memory_space=pl.ANY)
HBM = pl.BlockSpec(memory_space=pltpu.HBM)


def shape_of(shape, dtype):
    return jax.ShapeDtypeStruct(shape, dtype)


def params(mib):
    return pltpu.CompilerParams(vmem_limit_bytes=mib * 2**20)


def cost(micros):
    return pl.CostEstimate(flops=int(micros * 9e8), bytes_accessed=1_000_000, transcendentals=0)


def aligned(start, size):
    return pl.ds(pl.multiple_of(start, size), size)


def slot_count(tiles, extra):
    room = tiles / 2 + 4.0 * math.sqrt(tiles / 4)
    return extra + min(tiles + 1, 2 * math.ceil(room / 2) + 1)


def chunk_sizes(slots, tiles, extra):
    most = min(slots - 2, extra + math.ceil(tiles / 4 + 3 * math.sqrt(tiles / 8)))
    return extra, most - extra, slots - most


def pack_rows(mask_at, feet_at, begin, end, blocks, buf, carry):
    slots, _, lanes = buf.shape
    row_of = lax.broadcasted_iota(I32, (8, lanes), 0)
    lane_of = lax.broadcasted_iota(I32, (8, lanes), 1)
    flat = row_of * lanes + lane_of
    batch = math.gcd(2, end - begin)

    def some(i, carry):
        pos, head, ends = carry
        first = begin + i * batch
        tiles = [[feet_at(first + j, b) for b in range(blocks)] for j in range(batch)]
        kept = [[mask_at(first + j, b) for b in range(blocks)] for j in range(batch)]
        for j in range(batch):
            for b in range(blocks):
                buf[jnp.minimum(pos, slots - 1)] = tiles[j][b]
                head = jnp.where(flat == (first + j) * blocks + b, kept[j][b] * pos, head)
                pos = pos + kept[j][b]
            ends = jnp.where(lane_of == first + j, pos, ends)
        return pos, head, ends

    return lax.fori_loop(0, (end - begin) // batch, some, carry)


def no_rows(first, lanes):
    zeros = jnp.zeros((8, lanes), I32)
    return jnp.int32(first), zeros, zeros


def write_head(carry, rows, blocks, buf, head_v, flag=None):
    lanes = buf.shape[2]
    deep = -(-rows * blocks // lanes)
    _, head, ends = carry
    low = (1 << SHIFT) - 1
    head_v[...] = jnp.zeros_like(head_v)
    head_v[0:deep, :] = (head >> SHIFT)[0:deep].astype(F32)
    head_v[deep : 2 * deep, :] = (head & low)[0:deep].astype(F32)
    head_v[2 * deep : 2 * deep + 1, :] = (ends >> SHIFT)[0:1].astype(F32)
    head_v[2 * deep + 1 : 2 * deep + 2, :] = (ends & low)[0:1].astype(F32)
    if flag is not None:
        head_v[2 * deep + 2 : 2 * deep + 3, :] = jnp.broadcast_to(flag, (1, lanes)).astype(F32)
    buf[0] = head_v[...].astype(BF16)


def pack_feet_kernel(chunks, mask_ref, coords_hbm, sigma_hbm, feet_ref, *rest):
    outs, (coords_ref, sigma_ref, feet, buf, head_v, small_sem, in_sem, sem) = (
        rest[: len(chunks)],
        rest[len(chunks) :],
    )
    blocks, rows = mask_ref.shape
    small = [
        pltpu.make_async_copy(src, dst, small_sem.at[k])
        for k, (src, dst) in enumerate(((coords_hbm, coords_ref), (sigma_hbm, sigma_ref)))
    ]
    for copy in small:
        copy.start()
    times, lanes = buf.shape[1:]
    groups = in_sem.shape[0]
    each = rows // groups
    loads = [
        pltpu.make_async_copy(feet_ref.at[pl.ds(g * each, each)], feet.at[pl.ds(g * each, each)], in_sem.at[g])
        for g in range(groups)
    ]
    for load in loads:
        load.start()
    for copy in small:
        copy.wait()
    sigma = sigma_ref[...]
    high = sigma.astype(BF16).astype(F32)
    middle = (sigma - high).astype(BF16).astype(F32)
    lowest = sigma - high - middle
    at = lax.broadcasted_iota(I32, (times, sigma.shape[1]), 0)
    info = jnp.zeros(at.shape, F32)
    for k, row in enumerate((coords_ref[0:1, :].astype(F32), coords_ref[1:2, :].astype(F32), high, middle, lowest)):
        info = jnp.where(at == k, row, info)
    info = info.astype(BF16)
    for b in range(blocks):
        buf[1 + b] = info[:, b * lanes : (b + 1) * lanes]
    carry = no_rows(1 + blocks, lanes)
    for g in range(groups):
        loads[g].wait()
        carry = pack_rows(
            lambda o, b: mask_ref[b, o],
            lambda o, b: feet[o, :, b * lanes : (b + 1) * lanes],
            g * each,
            (g + 1) * each,
            blocks,
            buf,
            carry,
        )
    write_head(carry, rows, blocks, buf, head_v)
    copies, first = [], 0
    for k, size in enumerate(chunks):
        copies.append(pltpu.make_async_copy(buf.at[pl.ds(first, size)], outs[k], sem.at[k]))
        first += size
    for copy in copies:
        copy.start()
    for copy in copies:
        copy.wait()


def pack_feet(mask, coords, sigma, feet, chunks):
    rows, times, cells = feet.shape
    lanes = cells // mask.shape[0]
    groups = math.gcd(4, rows)
    return pl.pallas_call(
        functools.partial(pack_feet_kernel, chunks),
        out_shape=tuple(shape_of((size, times, lanes), BF16) for size in chunks),
        in_specs=[SMEM, HBM, HBM, HBM],
        out_specs=(ANY,) * len(chunks),
        scratch_shapes=[
            pltpu.VMEM(coords.shape, I32),
            pltpu.VMEM(sigma.shape, F32),
            pltpu.VMEM((rows, times, cells), BF16),
            pltpu.VMEM((sum(chunks), times, lanes), BF16),
            pltpu.VMEM((times, lanes), F32),
            pltpu.SemaphoreType.DMA((2,)),
            pltpu.SemaphoreType.DMA((groups,)),
            pltpu.SemaphoreType.DMA((len(chunks),)),
        ],
        compiler_params=params(12),
        cost_estimate=cost(3),
        name="pack_feet",
    )(mask, coords, sigma, feet)


def pack_panel_kernel(room, mask_ref, mask_hbm, index_ref, group_ref, member_ref, feet_ref, out_ref, mask_v, rows_buf, head_v, small_sem, sem):
    count = rows_buf.shape[0]
    blocks, obs = mask_ref.shape
    lanes = out_ref.shape[2]
    mask_copy = pltpu.make_async_copy(mask_hbm, mask_v, small_sem.at[0])
    mask_copy.start()
    base = group_ref[0]
    rows = [jnp.clip(index_ref[base * count + j] - base * obs, 0, obs - 1) for j in range(count)]
    copies = [pltpu.make_async_copy(feet_ref.at[rows[j]], rows_buf.at[j], sem.at[j]) for j in range(count)]
    for copy in copies:
        copy.start()
    mask_copy.wait()
    flag = (jnp.sum(mask_v[...].astype(F32), axis=(0, 1), keepdims=True) > room).astype(I32)
    for copy in copies:
        copy.wait()

    def mask_at(o, b):
        return mask_ref[b, jnp.clip(index_ref[base * count + o] - base * obs, 0, obs - 1)]

    carry = pack_rows(
        mask_at, lambda o, b: rows_buf[o, :, b * lanes : (b + 1) * lanes], 0, count, blocks, out_ref, no_rows(1, lanes)
    )
    write_head(carry, count, blocks, out_ref, head_v, flag)


def pack_panel(mask, panel_index, group, member, feet, count, slots, room):
    _, times, cells = feet.shape
    lanes = cells // mask.shape[0]
    return pl.pallas_call(
        functools.partial(pack_panel_kernel, room),
        out_shape=shape_of((slots, times, lanes), BF16),
        in_specs=[SMEM, HBM, SMEM, SMEM, SMEM, HBM],
        out_specs=VMEM,
        scratch_shapes=[
            pltpu.VMEM(mask.shape, I32),
            pltpu.VMEM((count, times, cells), BF16),
            pltpu.VMEM((times, lanes), F32),
            pltpu.SemaphoreType.DMA((1,)),
            pltpu.SemaphoreType.DMA((count,)),
        ],
        compiler_params=params(8),
        cost_estimate=cost(2),
        name="pack_panel",
    )(mask, mask, panel_index, group[None], member[None], feet)


def fetch(chunks, buf, sem):
    copies, first = [], 0
    for k, chunk in enumerate(chunks):
        copies.append(pltpu.make_async_copy(chunk, buf.at[pl.ds(first, chunk.shape[0])], sem.at[k]))
        copies[-1].start()
        first += chunk.shape[0]
    return copies


def read_head(buf, rows, blocks, bits_v, flagged=False):
    slots, _, lanes = buf.shape
    deep = -(-rows * blocks // lanes)
    head = buf[0].astype(F32)
    scale = float(1 << SHIFT)
    bits_v[0:deep, :] = jnp.minimum(head[0:deep] * scale + head[deep : 2 * deep], slots - 1.0).astype(I32)
    bits_v[5:6, :] = (head[2 * deep : 2 * deep + 1] * scale + head[2 * deep + 1 : 2 * deep + 2]).astype(I32)
    if flagged:
        bits_v[6:7, :] = head[2 * deep + 2 : 2 * deep + 3].astype(I32)
    buf[0] = jnp.zeros(buf.shape[1:], buf.dtype)


def copy_in(src, dst, sem):
    copy = pltpu.make_async_copy(src, dst, sem)
    copy.start()
    copy.wait()


def split(number, size):
    if size & (size - 1):
        return lax.div(number, size), lax.rem(number, size)
    return lax.shift_right_logical(number, size.bit_length() - 1), lax.bitwise_and(number, size - 1)


def expand(buf, bits, first, count, blocks, store, unrolled=False):
    lanes = buf.shape[2]
    batch = math.gcd(2, count)

    def some(i, _):
        tiles = []
        for j in range(batch):
            row, col = split(jnp.int32((first + i * batch + j) * blocks), lanes)
            tiles += [buf[bits[row, col + b]] for b in range(blocks)]
        for j in range(batch):
            for b in range(blocks):
                store(i * batch + j, b, tiles[j * blocks + b])
        return 0

    if unrolled:
        for i in range(count // batch):
            some(i, 0)
    else:
        lax.fori_loop(0, count // batch, some, 0)


def into(dense, times, lanes, offset, first=0):
    def store(i, b, tile):
        at = aligned((first + i) * times, times)
        dense[at, offset + b * lanes : offset + (b + 1) * lanes] = tile.astype(dense.dtype)

    return store


def read_info(buf, blocks, row_v, turned):
    _, lanes = buf.shape[1:]
    for b in range(blocks):
        tile = buf[1 + b].astype(F32)[0:INFO]
        sigma = tile[2:3] + tile[3:4] + tile[4:5]
        tile = jnp.where(lax.broadcasted_iota(I32, tile.shape, 0) == 2, sigma, tile)
        at = slice(b * lanes, (b + 1) * lanes)
        if row_v is not None:
            row_v[:, at] = tile
        if turned is not None:
            turned[at, :] = tile.T


def fill_covariance(dst, dst_first, src_first, rows, turned, own):
    x, y, s = own[0:1, :], own[1:2, :], own[2:3, :]
    step = min(32, rows)
    for i in range(rows // step):
        at = aligned(src_first + i * step, step)
        dx = turned[at, 0:1] - x
        dy = turned[at, 1:2] - y
        square = dx * dx + dy * dy + 1.0
        decay = jnp.exp2(square * lax.rsqrt(square) * (-math.log2(math.e) / LENGTH))
        dst[aligned(dst_first + i * step, step), :] = (decay * (turned[at, 2:3] * s)).astype(BF16)


def start_kernel(chunks, *refs):
    msg = refs[:chunks]
    dense, cov, info_ref, buf, bits_v, bits_s, turned, sem = refs[chunks:]
    times, lanes = buf.shape[1:]
    cells = cov.shape[1]
    blocks = cells // lanes
    rows = dense.shape[0] // times
    copies = fetch(msg, buf, sem)
    for copy in copies:
        copy.wait()
    read_info(buf, blocks, info_ref, turned)
    read_head(buf, rows, blocks, bits_v)
    copy = pltpu.make_async_copy(bits_v, bits_s, sem.at[chunks])
    copy.start()
    half = cells // 2
    fine = math.gcd(4, rows // 2)

    @pl.loop(0, fine)
    def _(i):
        fill_covariance(cov, i * (half // fine), i * (half // fine), half // fine, turned, info_ref)

    copy.wait()

    @pl.loop(0, fine)
    def _(i):
        first = half + i * (half // fine)
        fill_covariance(cov, first, first, half // fine, turned, info_ref)
        some = rows // fine
        expand(buf, bits_s, i * some, some, blocks, into(dense, times, lanes, 0, i * some), unrolled=True)


def start_call(own_msg, rows, cells):
    times, lanes = own_msg[0].shape[1:]
    slots = sum(chunk.shape[0] for chunk in own_msg)
    chunks = len(own_msg)
    return pl.pallas_call(
        functools.partial(start_kernel, chunks),
        out_shape=(
            shape_of((rows * times, cells), BF16),
            shape_of((cells, cells), BF16),
            shape_of((INFO, cells), F32),
        ),
        in_specs=[ANY] * chunks,
        out_specs=(VMEM,) * 3,
        scratch_shapes=[
            pltpu.VMEM((slots, times, lanes), BF16),
            pltpu.VMEM((8, lanes), I32),
            pltpu.SMEM((8, lanes), I32),
            pltpu.VMEM((cells, INFO), F32),
            pltpu.SemaphoreType.DMA((chunks + 1,)),
        ],
        compiler_params=params(12),
        cost_estimate=cost(4),
        name="own_start",
    )(*own_msg)


def own_kernel(chunks, *refs):
    msg = refs[:chunks]
    dense, cov, info_ref, out_ref, mate_dense, next_ref, buf, bits_v, bits_s, turned, sem = refs[chunks:]
    times, lanes = buf.shape[1:]
    cells = cov.shape[1]
    blocks = cells // lanes
    rows = dense.shape[0] // times
    tall = min(256, rows * times)
    steps = rows * times // tall
    part = cells // steps
    for copy in fetch(msg, buf, sem):
        copy.wait()
    read_info(buf, blocks, None, turned)
    read_head(buf, rows, blocks, bits_v)
    copy_in(bits_v, bits_s, sem.at[chunks])

    @pl.loop(0, steps)
    def _(u):
        here = aligned(u * tall, tall)
        fill_covariance(next_ref, u * part, u * part, part, turned, info_ref)
        out_ref[here, :] = jnp.dot(dense[here, :], cov[...], preferred_element_type=F32)
        some = rows // steps
        expand(buf, bits_s, u * some, some, blocks, into(mate_dense, times, lanes, 0, u * some), unrolled=True)


def own_call(mate_msg, dense, cov, info):
    times, lanes = mate_msg[0].shape[1:]
    cells = cov.shape[1]
    slots = sum(chunk.shape[0] for chunk in mate_msg)
    chunks = len(mate_msg)
    return pl.pallas_call(
        functools.partial(own_kernel, chunks),
        out_shape=(shape_of(dense.shape, F32), shape_of(dense.shape, BF16), shape_of((cells, cells), BF16)),
        in_specs=[ANY] * chunks + [VMEM] * 3,
        out_specs=(VMEM,) * 3,
        scratch_shapes=[
            pltpu.VMEM((slots, times, lanes), BF16),
            pltpu.VMEM((8, lanes), I32),
            pltpu.SMEM((8, lanes), I32),
            pltpu.VMEM((cells, INFO), F32),
            pltpu.SemaphoreType.DMA((chunks + 1,)),
        ],
        compiler_params=params(16),
        cost_estimate=cost(6),
        name="own_product",
    )(*mate_msg, dense, cov, info)


def far_info(firsts, info_buf, turned, sem):
    blocks = info_buf.shape[1] - 1
    cells = turned.shape[0] // len(firsts)
    copies = []
    for k, first in enumerate(firsts):
        copies.append(pltpu.make_async_copy(first.at[pl.ds(0, 1 + blocks)], info_buf.at[k], sem.at[k]))
        copies[-1].start()
    for k, copy in enumerate(copies):
        copy.wait()
        read_info(info_buf.at[k], blocks, None, turned.at[pl.ds(k * cells, cells)])


def far_start_kernel(count, *refs):
    firsts = refs[:count]
    info_ref, far_ref, info_buf, turned, sem = refs[count:]
    far_info(firsts, info_buf, turned, sem)
    cells = info_ref.shape[1]
    piece = min(128, cells)

    @pl.loop(0, count * cells // piece)
    def _(i):
        fill_covariance(far_ref, i * piece, i * piece, piece, turned, info_ref)


def far_scratch(firsts, cells):
    times, lanes = firsts[0].shape[1:]
    return [
        pltpu.VMEM((len(firsts), 1 + cells // lanes, times, lanes), BF16),
        pltpu.VMEM((len(firsts) * cells, INFO), F32),
        pltpu.SemaphoreType.DMA((len(firsts),)),
    ]


def far_start(firsts, info):
    cells = info.shape[1]
    count = len(firsts)
    return pl.pallas_call(
        functools.partial(far_start_kernel, count),
        out_shape=shape_of((count * cells, cells), BF16),
        in_specs=[ANY] * count + [VMEM],
        out_specs=VMEM,
        scratch_shapes=far_scratch(firsts, cells),
        compiler_params=params(10),
        cost_estimate=cost(4),
        name="far_start",
    )(*firsts, info)


def mate_kernel(count, *refs):
    firsts = refs[:count]
    near_ref, dense, cov_ref, info_ref, out_ref, far_ref, info_buf, turned, sem = refs[count:]
    cells = cov_ref.shape[1]
    tall = min(256, dense.shape[0])
    steps = dense.shape[0] // tall
    part = count * cells // steps
    far_info(firsts, info_buf, turned, sem)

    @pl.loop(0, steps)
    def _(u):
        here = aligned(u * tall, tall)
        fill_covariance(far_ref, u * part, u * part, part, turned, info_ref)
        out_ref[here, :] = near_ref[here, :] + jnp.dot(dense[here, :], cov_ref[...], preferred_element_type=F32)


def mate_call(firsts, near, mate_dense, cov, info):
    cells = cov.shape[1]
    count = len(firsts)
    return pl.pallas_call(
        functools.partial(mate_kernel, count),
        out_shape=(shape_of(near.shape, F32), shape_of((count * cells, cells), BF16)),
        in_specs=[ANY] * count + [VMEM] * 4,
        out_specs=(VMEM, VMEM),
        scratch_shapes=far_scratch(firsts, cells),
        input_output_aliases={count: 0},
        compiler_params=params(16),
        cost_estimate=cost(5),
        name="mate_product",
    )(*firsts, near, mate_dense, cov, info)


def mixed_unit(mix_ref, value):
    high = value.astype(BF16)
    low = (value - high.astype(F32)).astype(BF16)
    stacked = jnp.concatenate([high, low, high], axis=0)
    return jnp.dot(mix_ref[...], stacked, preferred_element_type=F32).astype(BF16)


def turn(value, rows, times):
    return jnp.swapaxes(value.reshape(rows, times, value.shape[1]), 0, 1)


def unit_step(u, count, unit, bufs, bits_s, dense_a, dense_b, near_ref, cov_refs, mix_ref, rows):
    times, _ = bufs.shape[2:]
    cells = near_ref.shape[1]
    few = count // 2
    here = aligned(u * unit * times, unit * times)
    place(u, few, count, unit, bufs, bits_s, dense_b, cells)
    value = near_ref[here, :] + jnp.dot(dense_a[...], cov_refs[0][...], preferred_element_type=F32)
    place(jnp.minimum(u + 1, rows // unit - 1), 0, few, unit, bufs, bits_s, dense_a, cells)
    value = value + jnp.dot(dense_b[...], cov_refs[1][...], preferred_element_type=F32)
    return mixed_unit(mix_ref, value)


def place(u, begin, end, unit, bufs, bits_s, dense, cells):
    times, lanes = bufs.shape[2:]
    for k in range(begin, end):
        store = into(dense, times, lanes, (k - begin) * cells)
        expand(bufs.at[k], bits_s.at[k], u * unit, unit, cells // lanes, store, unrolled=bufs.shape[0] <= 4)


def first_kernel(count, chunks, unit, *refs):
    msgs = [refs[k * chunks : (k + 1) * chunks] for k in range(count)]
    *cov_refs, near_ref, mix_ref, out_ref, next_ref, bufs, bits_v, bits_s, dense_a, dense_b, sem = refs[count * chunks :]
    times, lanes = bufs.shape[2:]
    cells = near_ref.shape[1]
    blocks = cells // lanes
    rows = out_ref.shape[0]
    limit = sum(chunk.shape[0] for chunk in msgs[0])
    copies = [fetch(msgs[k], bufs.at[k], sem.at[k]) for k in range(count)]
    for k in range(count):
        for copy in copies[k]:
            copy.wait()
        read_head(bufs.at[k], rows, blocks, bits_v.at[k])
    copy_in(bits_v, bits_s, sem.at[count, 0])
    ready = jnp.int32(0)
    for u in range(rows // unit):
        whole = jnp.int32(1)
        for k in range(count):
            whole = whole * (bits_s[k, 5, (u + 1) * unit - 1] <= limit).astype(I32)
        ready = ready + whole
    next_ref[0] = ready
    place(jnp.int32(0), 0, count // 2, unit, bufs, bits_s, dense_a, cells)

    def step(u, _):
        mixed = unit_step(u, count, unit, bufs, bits_s, dense_a, dense_b, near_ref, cov_refs, mix_ref, rows)
        out_ref[aligned(u * unit, unit)] = mixed.reshape(unit, times, cells)
        return 0

    lax.fori_loop(0, ready, step, 0)


def rows_scratch(count, chunks, slots, times, lanes, unit, cells, more):
    return [
        pltpu.VMEM((count, slots, times, lanes), BF16),
        pltpu.VMEM((count + more, 8, lanes), I32),
        pltpu.SMEM((count + more, 8, lanes), I32),
        pltpu.VMEM((unit * times, count // 2 * cells), BF16),
        pltpu.VMEM((unit * times, (count - count // 2) * cells), BF16),
        pltpu.SemaphoreType.DMA((count + 1, chunks)),
    ]


def first_rows(msgs, covs, near, mix, rows, unit, slots):
    times, lanes = msgs[0][0].shape[1:]
    cells = near.shape[1]
    count, chunks = len(msgs), len(msgs[0])
    flat = [chunk for msg in msgs for chunk in msg]
    return pl.pallas_call(
        functools.partial(first_kernel, count, chunks, unit),
        out_shape=(shape_of((rows, times, cells), BF16), shape_of((1,), I32)),
        in_specs=[ANY] * len(flat) + [VMEM] * 4,
        out_specs=(VMEM, SMEM),
        scratch_shapes=rows_scratch(count, chunks, slots, times, lanes, unit, cells, 0),
        compiler_params=params(16),
        cost_estimate=cost(7),
        name="first_rows",
    )(*flat, *covs, near, mix)


def late_kernel(count, chunks, unit, pieces, each, *refs):
    msgs = [refs[k * chunks : (k + 1) * chunks] for k in range(count)]
    panel_msgs = refs[count * chunks : count * chunks + pieces]
    refs = refs[count * chunks + pieces :]
    *cov_refs, near_ref, mix_ref, start_ref, done_ref, out_ref, turned_ref, part_ref, over_ref = refs[:10]
    bufs, bits_v, bits_s, dense_a, dense_b, sem, panel_bufs, stage, panel, panel_sem, out_sem = refs[10:]
    times, lanes = bufs.shape[2:]
    cells = near_ref.shape[1]
    blocks = cells // lanes
    rows = stage.shape[0]
    copies = [fetch(msgs[k], bufs.at[k], sem.at[k]) for k in range(count)]
    panel_copies = [pltpu.make_async_copy(msg, panel_bufs.at[k], panel_sem.at[k]) for k, msg in enumerate(panel_msgs)]
    for copy in panel_copies:
        copy.start()
    for k in range(count):
        for copy in copies[k]:
            copy.wait()
        read_head(bufs.at[k], rows, blocks, bits_v.at[k])
    for k, copy in enumerate(panel_copies):
        copy.wait()
        read_head(panel_bufs.at[k], each, blocks, bits_v.at[count + k], flagged=True)
    bits_copy = pltpu.make_async_copy(bits_v, bits_s, sem.at[count, 0])
    bits_copy.start()
    first = start_ref[0]

    def outgoing(u, src):
        at = aligned(u * unit, unit)
        return pltpu.make_async_copy(src.at[at], out_ref.at[at], out_sem.at[u])

    def carry_over(u, _):
        outgoing(u, done_ref).start()
        at = aligned(u * unit, unit)
        turned_ref[:, at, :] = turn(done_ref[at].reshape(unit * times, cells), unit, times)
        return 0

    lax.fori_loop(0, first, carry_over, 0)
    bits_copy.wait()
    place(jnp.minimum(first, rows // unit - 1), 0, count // 2, unit, bufs, bits_s, dense_a, cells)

    def step(u, _):
        mixed = unit_step(u, count, unit, bufs, bits_s, dense_a, dense_b, near_ref, cov_refs, mix_ref, rows)
        at = aligned(u * unit, unit)
        stage[at] = mixed.reshape(unit, times, cells)
        outgoing(u, stage).start()
        turned_ref[:, at, :] = turn(mixed, unit, times)
        return 0

    lax.fori_loop(first, rows // unit, step, 0)
    over_ref[0] = panel_over(panel_bufs, bits_s, count, pieces, each)
    part_ref[...] = panel_products(panel_bufs, bits_s, count, pieces, each, turned_ref, panel)

    def settle(u, _):
        outgoing(u, stage).wait()
        return 0

    lax.fori_loop(0, rows // unit, settle, 0)


def late_rows(msgs, panel_msgs, each, covs, near, mix, start, done, unit, slots):
    times, lanes = msgs[0][0].shape[1:]
    rows, _, cells = done.shape
    count, chunks, pieces = len(msgs), len(msgs[0]), len(panel_msgs)
    flat = [chunk for msg in msgs for chunk in msg] + list(panel_msgs)
    return pl.pallas_call(
        functools.partial(late_kernel, count, chunks, unit, pieces, each),
        out_shape=(
            shape_of(done.shape, BF16),
            shape_of((times, rows, cells), BF16),
            shape_of((rows, pieces * each), F32),
            shape_of((1,), I32),
        ),
        in_specs=[ANY] * len(flat) + [VMEM] * 4 + [SMEM, VMEM],
        out_specs=(HBM, VMEM, VMEM, SMEM),
        scratch_shapes=rows_scratch(count, chunks, slots, times, lanes, unit, cells, pieces)
        + [
            pltpu.VMEM((pieces, panel_msgs[0].shape[0], times, lanes), BF16),
            pltpu.VMEM((rows, times, cells), BF16),
            pltpu.VMEM((times, pieces * each, cells), BF16),
            pltpu.SemaphoreType.DMA((pieces,)),
            pltpu.SemaphoreType.DMA((rows // unit,)),
        ],
        compiler_params=params(20),
        cost_estimate=cost(9),
        name="late_rows",
    )(*flat, *covs, near, mix, start, done)


def mix_kernel(unit, time_ref, out_ref):
    times = time_ref.shape[0]
    size = unit * times
    value = time_ref[...]
    high = value.astype(BF16)
    low = (value - high.astype(F32)).astype(BF16)

    def same(shape, dim):
        index = lax.broadcasted_iota(I32, shape, 1 - dim) % times
        return (index == lax.broadcasted_iota(I32, shape, dim)).astype(F32).astype(BF16)

    row = lax.broadcasted_iota(I32, (size, size), 0)
    col = lax.broadcasted_iota(I32, (size, size), 1)
    for j, part in enumerate((high, high, low)):
        spread = jnp.dot(same((size, times), 1), part, preferred_element_type=F32).astype(BF16)
        spread = jnp.dot(spread, same((times, size), 0), preferred_element_type=F32)
        out_ref[:, j * size : (j + 1) * size] = jnp.where(row // times == col // times, spread, 0.0).astype(BF16)


def mixing(time_cov, unit):
    size = unit * time_cov.shape[0]
    return pl.pallas_call(
        functools.partial(mix_kernel, unit),
        out_shape=shape_of((size, 3 * size), BF16),
        in_specs=[VMEM],
        out_specs=VMEM,
        compiler_params=params(8),
        cost_estimate=cost(1),
        name="mixing",
    )(time_cov)


def panel_over(bufs, bits_s, base, pieces, each):
    slots, _, _ = bufs.shape[1:]
    over = jnp.int32(0)
    for k in range(pieces):
        ends = bits_s.shape[1] - 3
        over = over + (bits_s[base + k, ends, each - 1] > slots - 1).astype(I32) + bits_s[base + k, ends + 1, 0]
    return over


def panel_products(bufs, bits_s, base, pieces, each, turned, panel):
    times, lanes = bufs.shape[2:]
    blocks = panel.shape[2] // lanes
    group = max(1, 16 // each)

    @pl.loop(0, pieces // group)
    def _(g):
        for b in range(blocks):
            tiles = []
            for i in range(group * each):
                k, place = g * group + i // each, i % each * blocks + b
                tiles.append(bufs[k, bits_s[base + k, place // lanes, place % lanes]])
            value = turn(jnp.concatenate(tiles, axis=0), group * each, times)
            panel[:, aligned(g * group * each, group * each), b * lanes : (b + 1) * lanes] = value

    total = None
    for t in range(times):
        value = lax.dot_general(turned[t], panel[t], (((1,), (1,)), ((), ())), preferred_element_type=F32)
        total = value if total is None else total + value
    return total


def last_kernel(pieces, each, *refs):
    msgs = refs[:pieces]
    group_ref, member_ref, index_ref, var_ref, turned, before_ref, over_ref, out_ref, bufs, bits_v, bits_s, panel, sem = refs[pieces:]
    _, lanes = bufs.shape[2:]
    rows, cells = turned.shape[1:]
    copies = [pltpu.make_async_copy(msg, bufs.at[k], sem.at[k]) for k, msg in enumerate(msgs)]
    for copy in copies:
        copy.start()
    for k, copy in enumerate(copies):
        copy.wait()
        read_head(bufs.at[k], each, cells // lanes, bits_v.at[k], flagged=True)
    bits_copy = pltpu.make_async_copy(bits_v, bits_s, sem.at[pieces])
    bits_copy.start()
    size = out_ref.shape[1]
    row = lax.broadcasted_iota(I32, (size, size), 0)
    half = size // each // 2
    hi, lo = split(group_ref[0], 2)
    target = row
    for k in range(size // each):
        back = hi - k // 2
        source = jnp.where(back < 0, back + half, back) * 2 + lax.bitwise_xor(lo, k % 2)
        target = jnp.where((row >= k * each) & (row < (k + 1) * each), row + (source - k) * each, target)
    select = (lax.broadcasted_iota(I32, (size, size), 1) == target).astype(F32).astype(BF16)
    spot = lax.broadcasted_iota(I32, (rows, size), 0) + group_ref[0] * rows
    variance = jnp.broadcast_to(var_ref[...], (8, rows)).T[:, 0:1]
    diagonal = jnp.where((spot == index_ref[...]) & (member_ref[0] == 0), variance, 0.0)
    bits_copy.wait()
    over = over_ref[0] + panel_over(bufs, bits_s, 0, pieces, each)
    total = panel_products(bufs, bits_s, 0, pieces, each, turned, panel)
    value = jnp.concatenate([before_ref[...], total], axis=1)
    total = diagonal
    for _ in range(3):
        high = value.astype(BF16)
        total = total + jnp.dot(high, select, preferred_element_type=F32)
        value = value - high.astype(F32)
    out_ref[0:rows, :] = total
    out_ref[rows:, :] = jnp.broadcast_to(over, (8, size)).astype(F32)


def panel_last(msgs, turned, each, group, member, panel_index, error_var, before, over):
    slots, times, lanes = msgs[0].shape
    rows, cells = turned.shape[1:]
    pieces = len(msgs)
    return pl.pallas_call(
        functools.partial(last_kernel, pieces, each),
        out_shape=shape_of((rows + 8, before.shape[1] + pieces * each), F32),
        in_specs=[ANY] * pieces + [SMEM, SMEM, VMEM, VMEM, VMEM, VMEM, SMEM],
        out_specs=VMEM,
        scratch_shapes=[
            pltpu.VMEM((pieces, slots, times, lanes), BF16),
            pltpu.VMEM((pieces, 8, lanes), I32),
            pltpu.SMEM((pieces, 8, lanes), I32),
            pltpu.VMEM((times, pieces * each, cells), BF16),
            pltpu.SemaphoreType.DMA((pieces + 1,)),
        ],
        compiler_params=params(14),
        cost_estimate=cost(3),
        name="panel_last",
    )(*msgs, group[None], member[None], panel_index[None, :], error_var[None, :], turned, before, over)


def partner(value, axis, count):
    return lax.ppermute(value, axis, [(i, i ^ 1) for i in range(count)])


def shifted(value, axis, count, shift, flip=0):
    return lax.ppermute(value, axis, [(i, ((i + 2 * shift) % count) ^ flip) for i in range(count)])


def row_major(value):
    return with_layout_constraint(value, Layout(tuple(range(value.ndim))))


def add_cells(part, cells):
    total = part
    for shift in range(cells // 2):
        for flip in range(2):
            if shift or flip:
                total = total + shifted(part, "cell", cells, shift, flip)
    return total


def dense_way(cells, observers, footprint, block_mask, own, time_cov, mine, sources):
    obs_rows, times, cell_local = footprint.shape
    blocks = block_mask.shape[1]
    keep = block_mask.astype(BF16)[:, None, :, None]
    feet = (footprint.reshape(obs_rows, times, blocks, cell_local // blocks) * keep).reshape(footprint.shape)

    def add(carry, _):
        total, feet, info = carry
        dx = info[0][:, None] - own[0][None, :]
        dy = info[1][:, None] - own[1][None, :]
        decay = jnp.exp(-jnp.sqrt(dx * dx + dy * dy + 1.0) / LENGTH)
        cov = (decay * (info[2][:, None] * own[2][None, :])).astype(BF16)
        total = total + jnp.dot(feet.reshape(-1, cell_local), cov, preferred_element_type=F32)
        ring = [(i, (i + 1) % cells) for i in range(cells)]
        return (total, lax.ppermute(feet, "cell", ring), lax.ppermute(info, "cell", ring)), None

    zero = jnp.zeros((obs_rows * times, cell_local), F32)
    (total, _, _), _ = lax.scan(add, (zero, feet, own), None, length=cells)
    cov_product = jnp.einsum(
        "ts,ksc->ktc", time_cov, total.reshape(obs_rows, times, cell_local), precision=lax.Precision.HIGHEST
    ).astype(BF16)
    flat = cov_product.reshape(obs_rows, times * cell_local)

    def meet(held, _):
        both = jnp.concatenate([held, partner(held, "obs", observers)], axis=0)
        part = lax.dot_general(
            flat, both.reshape(both.shape[0], -1), (((1,), (1,)), ((), ())), preferred_element_type=F32
        )
        return shifted(held, "obs", observers, 1), part

    _, parts = lax.scan(meet, jnp.take(feet, mine, axis=0), None, length=observers // 2)
    parts = parts.transpose(1, 0, 2).reshape(obs_rows, observers, -1)
    ordered = jnp.zeros_like(parts).at[:, sources].set(parts)
    return cov_product, add_cells(ordered.reshape(obs_rows, -1), cells)


def body(cells, observers, footprint, block_mask, cell_coords, cell_sigma, time_cov, error_var, panel_index):
    obs_rows, _, cell_local = footprint.shape
    blocks = block_mask.shape[1]
    group = lax.axis_index("obs")
    each = panel_index.shape[0] // observers
    half = observers // 2
    member = lax.axis_index("cell")
    unit = math.gcd(16, obs_rows)
    slots = slot_count(obs_rows * blocks, 1 + blocks)
    chunks = chunk_sizes(slots, obs_rows * blocks, 1 + blocks)
    mask = block_mask.T

    room = slots - 2 - blocks - 1
    own_panel = pack_panel(mask, panel_index, group, member, footprint, each, slot_count(each * blocks, 1), room)
    ring = [own_panel]
    for _ in range(1, half):
        ring.append(shifted(ring[-1], "obs", observers, 1))
    messages = []
    for held in ring:
        messages += [held, partner(held, "obs", observers)]
    own_msg = pack_feet(mask, cell_coords, cell_sigma[None, :], footprint, chunks)
    far_msgs = []
    for shift in range(1, cells // 2):
        far_msgs.append([shifted(c, "cell", cells, shift) for c in own_msg])
    mate_msg = [partner(c, "cell", cells) for c in own_msg]
    for shift in range(1, cells // 2):
        far_msgs.append([partner(c, "cell", cells) for c in far_msgs[shift - 1]])

    dense, own_cov, info = start_call(own_msg, obs_rows, cell_local)
    near, mate_dense, mate_cov = own_call(mate_msg, dense, own_cov, info)
    firsts = [msg[0] for msg in far_msgs]
    few = len(firsts) // 2
    some_cov = far_start(firsts[:few], info)
    near, more_cov = mate_call(firsts[few:], near, mate_dense, mate_cov, info)
    far_cov = (some_cov, more_cov)
    mix = mixing(time_cov, unit)
    first_cov, start = first_rows([msg[:-1] for msg in far_msgs], far_cov, near, mix, obs_rows, unit, slots)
    cut = len(messages) * 3 // 4
    cov_product, turned, before, over = late_rows(
        far_msgs, messages[:cut], each, far_cov, near, mix, start, first_cov, unit, slots
    )
    part = panel_last(messages[cut:], turned, each, group, member, panel_index, error_var, before, over)

    part, late_group, late_mask = lax.optimization_barrier((part, group, mask))
    total = add_cells(part, cells)

    def again(carry):
        wanted = carry[0]
        kept, cell_info, place = (jnp.where(wanted, value, 0) for value in (late_mask, info, late_group))
        order = jnp.arange(observers, dtype=I32)
        from_group = (place // 2 - order // 2) % half * 2 + (place % 2 ^ (order % 2))
        mine = lax.dynamic_slice_in_dim(panel_index, place * each, each) - place * obs_rows
        cov_product, total = dense_way(
            cells, observers, footprint, kept.T, cell_info, time_cov, mine, from_group
        )
        positions = jnp.arange(obs_rows, dtype=I32) + place * obs_rows
        on_diagonal = (positions[:, None] == panel_index[None, :]).astype(F32)
        return jnp.bool_(False), cov_product, row_major(total + error_var[:, None] * on_diagonal)

    carry = (total[obs_rows, 0] > 0, cov_product, row_major(total[:obs_rows]))
    return lax.while_loop(lambda carry: carry[0], again, carry)[1:]


def solution(mesh):
    in_specs = (
        P("obs", None, "cell"),
        P("obs", "cell"),
        P(None, "cell"),
        P("cell"),
        P(),
        P("obs"),
        P(),
    )
    out_specs = (P("obs", None, "cell"), P("obs", None))
    cells, observers = mesh.shape["cell"], mesh.shape["obs"]

    def per_device(*args):
        return body(cells, observers, *args)

    return jax.shard_map(per_device, mesh=mesh, in_specs=in_specs, out_specs=out_specs, check_vma=False)
```

```python
import functools
import math

import jax
import jax.numpy as jnp
from jax import lax
from jax.experimental import pallas as pl
from jax.experimental.pallas import tpu as pltpu
from jax.experimental.layout import Layout, with_layout_constraint
from jax.sharding import PartitionSpec as P


GRID = 64
LENGTH = GRID / 16.0
F32, BF16, I32 = jnp.float32, jnp.bfloat16, jnp.int32
SHIFT = 4
INFO = 8


VMEM = pl.BlockSpec(memory_space=pltpu.VMEM)
SMEM = pl.BlockSpec(memory_space=pltpu.SMEM)
ANY = pl.BlockSpec(memory_space=pl.ANY)
HBM = pl.BlockSpec(memory_space=pltpu.HBM)


def shape_of(shape, dtype):
    return jax.ShapeDtypeStruct(shape, dtype)


def params(mib):
    return pltpu.CompilerParams(vmem_limit_bytes=mib * 2**20)


def cost(micros):
    return pl.CostEstimate(flops=int(micros * 9e8), bytes_accessed=1_000_000, transcendentals=0)


def aligned(start, size):
    return pl.ds(pl.multiple_of(start, size), size)


def slot_count(tiles, extra):
    room = tiles / 2 + 4.0 * math.sqrt(tiles / 4)
    return extra + min(tiles + 1, 2 * math.ceil(room / 2) + 1)


def chunk_sizes(slots, tiles, extra):
    most = min(slots - 2, extra + math.ceil(tiles / 4 + 3 * math.sqrt(tiles / 8)))
    return extra, most - extra, slots - most


def pack_rows(mask_at, feet_at, begin, end, blocks, buf, carry):
    slots, _, lanes = buf.shape
    row_of = lax.broadcasted_iota(I32, (8, lanes), 0)
    lane_of = lax.broadcasted_iota(I32, (8, lanes), 1)
    flat = row_of * lanes + lane_of
    batch = math.gcd(2, end - begin)

    def some(i, carry):
        pos, head, ends = carry
        first = begin + i * batch
        tiles = [[feet_at(first + j, b) for b in range(blocks)] for j in range(batch)]
        kept = [[mask_at(first + j, b) for b in range(blocks)] for j in range(batch)]
        for j in range(batch):
            for b in range(blocks):
                buf[jnp.minimum(pos, slots - 1)] = tiles[j][b]
                head = jnp.where(flat == (first + j) * blocks + b, kept[j][b] * pos, head)
                pos = pos + kept[j][b]
            ends = jnp.where(lane_of == first + j, pos, ends)
        return pos, head, ends

    return lax.fori_loop(0, (end - begin) // batch, some, carry)


def no_rows(first, lanes):
    zeros = jnp.zeros((8, lanes), I32)
    return jnp.int32(first), zeros, zeros


def write_head(carry, rows, blocks, buf, head_v, flag=None):
    lanes = buf.shape[2]
    deep = -(-rows * blocks // lanes)
    _, head, ends = carry
    low = (1 << SHIFT) - 1
    head_v[...] = jnp.zeros_like(head_v)
    head_v[0:deep, :] = (head >> SHIFT)[0:deep].astype(F32)
    head_v[deep : 2 * deep, :] = (head & low)[0:deep].astype(F32)
    head_v[2 * deep : 2 * deep + 1, :] = (ends >> SHIFT)[0:1].astype(F32)
    head_v[2 * deep + 1 : 2 * deep + 2, :] = (ends & low)[0:1].astype(F32)
    if flag is not None:
        head_v[2 * deep + 2 : 2 * deep + 3, :] = jnp.broadcast_to(flag, (1, lanes)).astype(F32)
    buf[0] = head_v[...].astype(BF16)


def pack_feet_kernel(chunks, mask_ref, coords_hbm, sigma_hbm, feet_ref, *rest):
    outs, (coords_ref, sigma_ref, feet, buf, head_v, small_sem, in_sem, sem) = (
        rest[: len(chunks)],
        rest[len(chunks) :],
    )
    blocks, rows = mask_ref.shape
    small = [
        pltpu.make_async_copy(src, dst, small_sem.at[k])
        for k, (src, dst) in enumerate(((coords_hbm, coords_ref), (sigma_hbm, sigma_ref)))
    ]
    for copy in small:
        copy.start()
    times, lanes = buf.shape[1:]
    groups = in_sem.shape[0]
    each = rows // groups
    loads = [
        pltpu.make_async_copy(feet_ref.at[pl.ds(g * each, each)], feet.at[pl.ds(g * each, each)], in_sem.at[g])
        for g in range(groups)
    ]
    for load in loads:
        load.start()
    for copy in small:
        copy.wait()
    sigma = sigma_ref[...]
    high = sigma.astype(BF16).astype(F32)
    middle = (sigma - high).astype(BF16).astype(F32)
    lowest = sigma - high - middle
    at = lax.broadcasted_iota(I32, (times, sigma.shape[1]), 0)
    info = jnp.zeros(at.shape, F32)
    for k, row in enumerate((coords_ref[0:1, :].astype(F32), coords_ref[1:2, :].astype(F32), high, middle, lowest)):
        info = jnp.where(at == k, row, info)
    info = info.astype(BF16)
    for b in range(blocks):
        buf[1 + b] = info[:, b * lanes : (b + 1) * lanes]
    carry = no_rows(1 + blocks, lanes)
    for g in range(groups):
        loads[g].wait()
        carry = pack_rows(
            lambda o, b: mask_ref[b, o],
            lambda o, b: feet[o, :, b * lanes : (b + 1) * lanes],
            g * each,
            (g + 1) * each,
            blocks,
            buf,
            carry,
        )
    write_head(carry, rows, blocks, buf, head_v)
    copies, first = [], 0
    for k, size in enumerate(chunks):
        copies.append(pltpu.make_async_copy(buf.at[pl.ds(first, size)], outs[k], sem.at[k]))
        first += size
    for copy in copies:
        copy.start()
    for copy in copies:
        copy.wait()


def pack_feet(mask, coords, sigma, feet, chunks):
    rows, times, cells = feet.shape
    lanes = cells // mask.shape[0]
    groups = math.gcd(4, rows)
    return pl.pallas_call(
        functools.partial(pack_feet_kernel, chunks),
        out_shape=tuple(shape_of((size, times, lanes), BF16) for size in chunks),
        in_specs=[SMEM, HBM, HBM, HBM],
        out_specs=(ANY,) * len(chunks),
        scratch_shapes=[
            pltpu.VMEM(coords.shape, I32),
            pltpu.VMEM(sigma.shape, F32),
            pltpu.VMEM((rows, times, cells), BF16),
            pltpu.VMEM((sum(chunks), times, lanes), BF16),
            pltpu.VMEM((times, lanes), F32),
            pltpu.SemaphoreType.DMA((2,)),
            pltpu.SemaphoreType.DMA((groups,)),
            pltpu.SemaphoreType.DMA((len(chunks),)),
        ],
        compiler_params=params(12),
        cost_estimate=cost(3),
        name="pack_feet",
    )(mask, coords, sigma, feet)


def pack_panel_kernel(room, mask_ref, mask_hbm, index_ref, group_ref, member_ref, feet_ref, out_ref, mask_v, rows_buf, head_v, small_sem, sem):
    count = rows_buf.shape[0]
    blocks, obs = mask_ref.shape
    lanes = out_ref.shape[2]
    mask_copy = pltpu.make_async_copy(mask_hbm, mask_v, small_sem.at[0])
    mask_copy.start()
    base = group_ref[0]
    rows = [jnp.clip(index_ref[base * count + j] - base * obs, 0, obs - 1) for j in range(count)]
    copies = [pltpu.make_async_copy(feet_ref.at[rows[j]], rows_buf.at[j], sem.at[j]) for j in range(count)]
    for copy in copies:
        copy.start()
    mask_copy.wait()
    flag = (jnp.sum(mask_v[...].astype(F32), axis=(0, 1), keepdims=True) > room).astype(I32)
    for copy in copies:
        copy.wait()

    def mask_at(o, b):
        return mask_ref[b, jnp.clip(index_ref[base * count + o] - base * obs, 0, obs - 1)]

    carry = pack_rows(
        mask_at, lambda o, b: rows_buf[o, :, b * lanes : (b + 1) * lanes], 0, count, blocks, out_ref, no_rows(1, lanes)
    )
    write_head(carry, count, blocks, out_ref, head_v, flag)


def pack_panel(mask, panel_index, group, member, feet, count, slots, room):
    _, times, cells = feet.shape
    lanes = cells // mask.shape[0]
    return pl.pallas_call(
        functools.partial(pack_panel_kernel, room),
        out_shape=shape_of((slots, times, lanes), BF16),
        in_specs=[SMEM, HBM, SMEM, SMEM, SMEM, HBM],
        out_specs=VMEM,
        scratch_shapes=[
            pltpu.VMEM(mask.shape, I32),
            pltpu.VMEM((count, times, cells), BF16),
            pltpu.VMEM((times, lanes), F32),
            pltpu.SemaphoreType.DMA((1,)),
            pltpu.SemaphoreType.DMA((count,)),
        ],
        compiler_params=params(8),
        cost_estimate=cost(2),
        name="pack_panel",
    )(mask, mask, panel_index, group[None], member[None], feet)


def fetch(chunks, buf, sem):
    copies, first = [], 0
    for k, chunk in enumerate(chunks):
        copies.append(pltpu.make_async_copy(chunk, buf.at[pl.ds(first, chunk.shape[0])], sem.at[k]))
        copies[-1].start()
        first += chunk.shape[0]
    return copies


def read_head(buf, rows, blocks, bits_v, flagged=False):
    slots, _, lanes = buf.shape
    deep = -(-rows * blocks // lanes)
    head = buf[0].astype(F32)
    scale = float(1 << SHIFT)
    bits_v[0:deep, :] = jnp.minimum(head[0:deep] * scale + head[deep : 2 * deep], slots - 1.0).astype(I32)
    bits_v[5:6, :] = (head[2 * deep : 2 * deep + 1] * scale + head[2 * deep + 1 : 2 * deep + 2]).astype(I32)
    if flagged:
        bits_v[6:7, :] = head[2 * deep + 2 : 2 * deep + 3].astype(I32)
    buf[0] = jnp.zeros(buf.shape[1:], buf.dtype)


def split(number, size):
    if size & (size - 1):
        return lax.div(number, size), lax.rem(number, size)
    return lax.shift_right_logical(number, size.bit_length() - 1), lax.bitwise_and(number, size - 1)


def expand(buf, bits, first, count, blocks, store, unrolled=False):
    lanes = buf.shape[2]
    batch = math.gcd(2, count)

    def some(i, _):
        tiles = []
        for j in range(batch):
            row, col = split(jnp.int32((first + i * batch + j) * blocks), lanes)
            tiles += [buf[bits[row, col + b]] for b in range(blocks)]
        for j in range(batch):
            for b in range(blocks):
                store(i * batch + j, b, tiles[j * blocks + b])
        return 0

    if unrolled:
        for i in range(count // batch):
            some(i, 0)
    else:
        lax.fori_loop(0, count // batch, some, 0)


def into(dense, times, lanes, offset, first=0):
    def store(i, b, tile):
        at = aligned((first + i) * times, times)
        dense[at, offset + b * lanes : offset + (b + 1) * lanes] = tile.astype(dense.dtype)

    return store


def read_info(buf, blocks, row_v, turned):
    _, lanes = buf.shape[1:]
    for b in range(blocks):
        tile = buf[1 + b].astype(F32)[0:INFO]
        sigma = tile[2:3] + tile[3:4] + tile[4:5]
        tile = jnp.where(lax.broadcasted_iota(I32, tile.shape, 0) == 2, sigma, tile)
        at = slice(b * lanes, (b + 1) * lanes)
        if row_v is not None:
            row_v[:, at] = tile
        if turned is not None:
            turned[at, :] = tile.T


def fill_covariance(dst, dst_first, src_first, rows, turned, own):
    x, y, s = own[0:1, :], own[1:2, :], own[2:3, :]
    step = min(32, rows)
    for i in range(rows // step):
        at = aligned(src_first + i * step, step)
        dx = turned[at, 0:1] - x
        dy = turned[at, 1:2] - y
        square = dx * dx + dy * dy + 1.0
        decay = jnp.exp2(square * lax.rsqrt(square) * (-math.log2(math.e) / LENGTH))
        dst[aligned(dst_first + i * step, step), :] = (decay * (turned[at, 2:3] * s)).astype(BF16)


def start_kernel(chunks, *refs):
    msg = refs[:chunks]
    dense, cov, info_ref, buf, bits_v, bits_s, turned, sem = refs[chunks:]
    times, lanes = buf.shape[1:]
    cells = cov.shape[1]
    blocks = cells // lanes
    rows = dense.shape[0] // times
    copies = fetch(msg, buf, sem)
    copies[0].wait()
    read_head(buf, rows, blocks, bits_v)
    copy = pltpu.make_async_copy(bits_v, bits_s, sem.at[chunks])
    copy.start()
    read_info(buf, blocks, info_ref, turned)
    for other in copies[1:]:
        other.wait()
    half = cells // 2
    fine = math.gcd(4, rows // 2)

    @pl.loop(0, fine)
    def _(i):
        fill_covariance(cov, i * (half // fine), i * (half // fine), half // fine, turned, info_ref)

    copy.wait()

    @pl.loop(0, fine)
    def _(i):
        first = half + i * (half // fine)
        fill_covariance(cov, first, first, half // fine, turned, info_ref)
        some = rows // fine
        expand(buf, bits_s, i * some, some, blocks, into(dense, times, lanes, 0, i * some), unrolled=True)


def start_call(own_msg, rows, cells):
    times, lanes = own_msg[0].shape[1:]
    slots = sum(chunk.shape[0] for chunk in own_msg)
    chunks = len(own_msg)
    return pl.pallas_call(
        functools.partial(start_kernel, chunks),
        out_shape=(
            shape_of((rows * times, cells), BF16),
            shape_of((cells, cells), BF16),
            shape_of((INFO, cells), F32),
        ),
        in_specs=[ANY] * chunks,
        out_specs=(VMEM,) * 3,
        scratch_shapes=[
            pltpu.VMEM((slots, times, lanes), BF16),
            pltpu.VMEM((8, lanes), I32),
            pltpu.SMEM((8, lanes), I32),
            pltpu.VMEM((cells, INFO), F32),
            pltpu.SemaphoreType.DMA((chunks + 1,)),
        ],
        compiler_params=params(12),
        cost_estimate=cost(4),
        name="own_start",
    )(*own_msg)


def own_kernel(chunks, *refs):
    msg = refs[:chunks]
    dense, cov, info_ref, out_ref, mate_dense, next_ref, buf, bits_v, bits_s, turned, sem = refs[chunks:]
    times, lanes = buf.shape[1:]
    cells = cov.shape[1]
    blocks = cells // lanes
    rows = dense.shape[0] // times
    tall = min(256, rows * times)
    steps = rows * times // tall
    part = cells // steps
    copies = fetch(msg, buf, sem)
    copies[0].wait()
    read_head(buf, rows, blocks, bits_v)
    bits_copy = pltpu.make_async_copy(bits_v, bits_s, sem.at[chunks])
    bits_copy.start()
    read_info(buf, blocks, None, turned)
    for copy in copies[1:]:
        copy.wait()
    bits_copy.wait()

    @pl.loop(0, steps)
    def _(u):
        here = aligned(u * tall, tall)
        fill_covariance(next_ref, u * part, u * part, part, turned, info_ref)
        out_ref[here, :] = jnp.dot(dense[here, :], cov[...], preferred_element_type=F32)
        some = rows // steps
        expand(buf, bits_s, u * some, some, blocks, into(mate_dense, times, lanes, 0, u * some), unrolled=True)


def own_call(mate_msg, dense, cov, info):
    times, lanes = mate_msg[0].shape[1:]
    cells = cov.shape[1]
    slots = sum(chunk.shape[0] for chunk in mate_msg)
    chunks = len(mate_msg)
    return pl.pallas_call(
        functools.partial(own_kernel, chunks),
        out_shape=(shape_of(dense.shape, F32), shape_of(dense.shape, BF16), shape_of((cells, cells), BF16)),
        in_specs=[ANY] * chunks + [VMEM] * 3,
        out_specs=(VMEM,) * 3,
        scratch_shapes=[
            pltpu.VMEM((slots, times, lanes), BF16),
            pltpu.VMEM((8, lanes), I32),
            pltpu.SMEM((8, lanes), I32),
            pltpu.VMEM((cells, INFO), F32),
            pltpu.SemaphoreType.DMA((chunks + 1,)),
        ],
        compiler_params=params(16),
        cost_estimate=cost(6),
        name="own_product",
    )(*mate_msg, dense, cov, info)


def far_info(firsts, info_buf, turned, sem):
    blocks = info_buf.shape[1] - 1
    cells = turned.shape[0] // len(firsts)
    copies = []
    for k, first in enumerate(firsts):
        copies.append(pltpu.make_async_copy(first.at[pl.ds(0, 1 + blocks)], info_buf.at[k], sem.at[k]))
        copies[-1].start()
    for k, copy in enumerate(copies):
        copy.wait()
        read_info(info_buf.at[k], blocks, None, turned.at[pl.ds(k * cells, cells)])


def far_start_kernel(count, *refs):
    firsts = refs[:count]
    info_ref, far_ref, info_buf, turned, sem = refs[count:]
    far_info(firsts, info_buf, turned, sem)
    cells = info_ref.shape[1]
    piece = min(128, cells)

    @pl.loop(0, count * cells // piece)
    def _(i):
        fill_covariance(far_ref, i * piece, i * piece, piece, turned, info_ref)


def far_scratch(firsts, cells):
    times, lanes = firsts[0].shape[1:]
    return [
        pltpu.VMEM((len(firsts), 1 + cells // lanes, times, lanes), BF16),
        pltpu.VMEM((len(firsts) * cells, INFO), F32),
        pltpu.SemaphoreType.DMA((len(firsts),)),
    ]


def far_start(firsts, info):
    cells = info.shape[1]
    count = len(firsts)
    return pl.pallas_call(
        functools.partial(far_start_kernel, count),
        out_shape=shape_of((count * cells, cells), BF16),
        in_specs=[ANY] * count + [VMEM],
        out_specs=VMEM,
        scratch_shapes=far_scratch(firsts, cells),
        compiler_params=params(10),
        cost_estimate=cost(4),
        name="far_start",
    )(*firsts, info)


def mate_kernel(count, *refs):
    firsts = refs[:count]
    near_ref, dense, cov_ref, info_ref, out_ref, far_ref, info_buf, turned, sem = refs[count:]
    cells = cov_ref.shape[1]
    tall = min(256, dense.shape[0])
    steps = dense.shape[0] // tall
    part = count * cells // steps
    far_info(firsts, info_buf, turned, sem)

    @pl.loop(0, steps)
    def _(u):
        here = aligned(u * tall, tall)
        fill_covariance(far_ref, u * part, u * part, part, turned, info_ref)
        out_ref[here, :] = near_ref[here, :] + jnp.dot(dense[here, :], cov_ref[...], preferred_element_type=F32)


def mate_call(firsts, near, mate_dense, cov, info):
    cells = cov.shape[1]
    count = len(firsts)
    return pl.pallas_call(
        functools.partial(mate_kernel, count),
        out_shape=(shape_of(near.shape, F32), shape_of((count * cells, cells), BF16)),
        in_specs=[ANY] * count + [VMEM] * 4,
        out_specs=(VMEM, VMEM),
        scratch_shapes=far_scratch(firsts, cells),
        input_output_aliases={count: 0},
        compiler_params=params(16),
        cost_estimate=cost(5),
        name="mate_product",
    )(*firsts, near, mate_dense, cov, info)


def mixed_unit(mix_ref, value):
    high = value.astype(BF16)
    low = (value - high.astype(F32)).astype(BF16)
    stacked = jnp.concatenate([high, low, high], axis=0)
    return jnp.dot(mix_ref[...], stacked, preferred_element_type=F32).astype(BF16)


def turn(value, rows, times):
    return jnp.swapaxes(value.reshape(rows, times, value.shape[1]), 0, 1)


def unit_step(u, count, unit, bufs, bits_s, dense_a, dense_b, near_ref, cov_refs, mix_ref, rows):
    times, _ = bufs.shape[2:]
    cells = near_ref.shape[1]
    few = count // 2
    here = aligned(u * unit * times, unit * times)
    place(u, few, count, unit, bufs, bits_s, dense_b, cells)
    value = near_ref[here, :] + jnp.dot(dense_a[...], cov_refs[0][...], preferred_element_type=F32)
    place(jnp.minimum(u + 1, rows // unit - 1), 0, few, unit, bufs, bits_s, dense_a, cells)
    value = value + jnp.dot(dense_b[...], cov_refs[1][...], preferred_element_type=F32)
    return mixed_unit(mix_ref, value)


def place(u, begin, end, unit, bufs, bits_s, dense, cells):
    times, lanes = bufs.shape[2:]
    for k in range(begin, end):
        store = into(dense, times, lanes, (k - begin) * cells)
        expand(bufs.at[k], bits_s.at[k], u * unit, unit, cells // lanes, store, unrolled=bufs.shape[0] <= 4)


def first_kernel(count, chunks, unit, *refs):
    msgs = [refs[k * chunks : (k + 1) * chunks] for k in range(count)]
    *cov_refs, near_ref, mix_ref, out_ref, next_ref, bufs, bits_v, bits_s, dense_a, dense_b, sem = refs[count * chunks :]
    times, lanes = bufs.shape[2:]
    cells = near_ref.shape[1]
    blocks = cells // lanes
    rows = out_ref.shape[0]
    limit = sum(chunk.shape[0] for chunk in msgs[0])
    copies = [fetch(msgs[k], bufs.at[k], sem.at[k]) for k in range(count)]
    for k in range(count):
        copies[k][0].wait()
        read_head(bufs.at[k], rows, blocks, bits_v.at[k])
    bits_copy = pltpu.make_async_copy(bits_v, bits_s, sem.at[count, 0])
    bits_copy.start()
    for k in range(count):
        for copy in copies[k][1:]:
            copy.wait()
    bits_copy.wait()
    ready = jnp.int32(0)
    for u in range(rows // unit):
        whole = jnp.int32(1)
        for k in range(count):
            whole = whole * (bits_s[k, 5, (u + 1) * unit - 1] <= limit).astype(I32)
        ready = ready + whole
    next_ref[0] = ready
    place(jnp.int32(0), 0, count // 2, unit, bufs, bits_s, dense_a, cells)

    def step(u, _):
        mixed = unit_step(u, count, unit, bufs, bits_s, dense_a, dense_b, near_ref, cov_refs, mix_ref, rows)
        out_ref[aligned(u * unit, unit)] = mixed.reshape(unit, times, cells)
        return 0

    lax.fori_loop(0, ready, step, 0)


def rows_scratch(count, chunks, slots, times, lanes, unit, cells, more):
    return [
        pltpu.VMEM((count, slots, times, lanes), BF16),
        pltpu.VMEM((count + more, 8, lanes), I32),
        pltpu.SMEM((count + more, 8, lanes), I32),
        pltpu.VMEM((unit * times, count // 2 * cells), BF16),
        pltpu.VMEM((unit * times, (count - count // 2) * cells), BF16),
        pltpu.SemaphoreType.DMA((count + 1, chunks)),
    ]


def first_rows(msgs, covs, near, mix, rows, unit, slots):
    times, lanes = msgs[0][0].shape[1:]
    cells = near.shape[1]
    count, chunks = len(msgs), len(msgs[0])
    flat = [chunk for msg in msgs for chunk in msg]
    return pl.pallas_call(
        functools.partial(first_kernel, count, chunks, unit),
        out_shape=(shape_of((rows, times, cells), BF16), shape_of((1,), I32)),
        in_specs=[ANY] * len(flat) + [VMEM] * 4,
        out_specs=(VMEM, SMEM),
        scratch_shapes=rows_scratch(count, chunks, slots, times, lanes, unit, cells, 0),
        compiler_params=params(16),
        cost_estimate=cost(7),
        name="first_rows",
    )(*flat, *covs, near, mix)


def late_kernel(count, chunks, unit, pieces, each, *refs):
    msgs = [refs[k * chunks : (k + 1) * chunks] for k in range(count)]
    panel_msgs = refs[count * chunks : count * chunks + pieces]
    refs = refs[count * chunks + pieces :]
    *cov_refs, near_ref, mix_ref, start_ref, done_ref, out_ref, turned_ref, part_ref, over_ref = refs[:10]
    bufs, bits_v, bits_s, dense_a, dense_b, sem, panel_bufs, stage, panel, panel_sem, out_sem = refs[10:]
    times, lanes = bufs.shape[2:]
    cells = near_ref.shape[1]
    blocks = cells // lanes
    rows = stage.shape[0]
    copies = [fetch(msgs[k], bufs.at[k], sem.at[k]) for k in range(count)]
    panel_copies = [pltpu.make_async_copy(msg, panel_bufs.at[k], panel_sem.at[k]) for k, msg in enumerate(panel_msgs)]
    for copy in panel_copies:
        copy.start()
    for k in range(count):
        copies[k][0].wait()
        read_head(bufs.at[k], rows, blocks, bits_v.at[k])
    for k, copy in enumerate(panel_copies):
        copy.wait()
        read_head(panel_bufs.at[k], each, blocks, bits_v.at[count + k], flagged=True)
    bits_copy = pltpu.make_async_copy(bits_v, bits_s, sem.at[count, 0])
    bits_copy.start()
    first = start_ref[0]

    def outgoing(u, src):
        at = aligned(u * unit, unit)
        return pltpu.make_async_copy(src.at[at], out_ref.at[at], out_sem.at[u])

    def carry_over(u, _):
        outgoing(u, done_ref).start()
        at = aligned(u * unit, unit)
        turned_ref[:, at, :] = turn(done_ref[at].reshape(unit * times, cells), unit, times)
        return 0

    lax.fori_loop(0, first, carry_over, 0)
    for k in range(count):
        for copy in copies[k][1:]:
            copy.wait()
    bits_copy.wait()
    place(jnp.minimum(first, rows // unit - 1), 0, count // 2, unit, bufs, bits_s, dense_a, cells)

    def step(u, _):
        mixed = unit_step(u, count, unit, bufs, bits_s, dense_a, dense_b, near_ref, cov_refs, mix_ref, rows)
        at = aligned(u * unit, unit)
        stage[at] = mixed.reshape(unit, times, cells)
        outgoing(u, stage).start()
        turned_ref[:, at, :] = turn(mixed, unit, times)
        return 0

    lax.fori_loop(first, rows // unit, step, 0)
    over_ref[0] = panel_over(panel_bufs, bits_s, count, pieces, each)
    part_ref[...] = panel_products(panel_bufs, bits_s, count, pieces, each, turned_ref, panel)

    def settle(u, _):
        outgoing(u, stage).wait()
        return 0

    lax.fori_loop(0, rows // unit, settle, 0)


def late_rows(msgs, panel_msgs, each, covs, near, mix, start, done, unit, slots):
    times, lanes = msgs[0][0].shape[1:]
    rows, _, cells = done.shape
    count, chunks, pieces = len(msgs), len(msgs[0]), len(panel_msgs)
    flat = [chunk for msg in msgs for chunk in msg] + list(panel_msgs)
    return pl.pallas_call(
        functools.partial(late_kernel, count, chunks, unit, pieces, each),
        out_shape=(
            shape_of(done.shape, BF16),
            shape_of((times, rows, cells), BF16),
            shape_of((rows, pieces * each), F32),
            shape_of((1,), I32),
        ),
        in_specs=[ANY] * len(flat) + [VMEM] * 4 + [SMEM, VMEM],
        out_specs=(HBM, VMEM, VMEM, SMEM),
        scratch_shapes=rows_scratch(count, chunks, slots, times, lanes, unit, cells, pieces)
        + [
            pltpu.VMEM((pieces, panel_msgs[0].shape[0], times, lanes), BF16),
            pltpu.VMEM((rows, times, cells), BF16),
            pltpu.VMEM((times, pieces * each, cells), BF16),
            pltpu.SemaphoreType.DMA((pieces,)),
            pltpu.SemaphoreType.DMA((rows // unit,)),
        ],
        compiler_params=params(20),
        cost_estimate=cost(9),
        name="late_rows",
    )(*flat, *covs, near, mix, start, done)


def mix_kernel(unit, time_ref, out_ref):
    times = time_ref.shape[0]
    size = unit * times
    value = time_ref[...]
    high = value.astype(BF16)
    low = (value - high.astype(F32)).astype(BF16)

    def same(shape, dim):
        index = lax.broadcasted_iota(I32, shape, 1 - dim) % times
        return (index == lax.broadcasted_iota(I32, shape, dim)).astype(F32).astype(BF16)

    row = lax.broadcasted_iota(I32, (size, size), 0)
    col = lax.broadcasted_iota(I32, (size, size), 1)
    for j, part in enumerate((high, high, low)):
        spread = jnp.dot(same((size, times), 1), part, preferred_element_type=F32).astype(BF16)
        spread = jnp.dot(spread, same((times, size), 0), preferred_element_type=F32)
        out_ref[:, j * size : (j + 1) * size] = jnp.where(row // times == col // times, spread, 0.0).astype(BF16)


def mixing(time_cov, unit):
    size = unit * time_cov.shape[0]
    return pl.pallas_call(
        functools.partial(mix_kernel, unit),
        out_shape=shape_of((size, 3 * size), BF16),
        in_specs=[VMEM],
        out_specs=VMEM,
        compiler_params=params(8),
        cost_estimate=cost(1),
        name="mixing",
    )(time_cov)


def panel_over(bufs, bits_s, base, pieces, each):
    slots, _, _ = bufs.shape[1:]
    over = jnp.int32(0)
    for k in range(pieces):
        ends = bits_s.shape[1] - 3
        over = over + (bits_s[base + k, ends, each - 1] > slots - 1).astype(I32) + bits_s[base + k, ends + 1, 0]
    return over


def panel_products(bufs, bits_s, base, pieces, each, turned, panel):
    times, lanes = bufs.shape[2:]
    blocks = panel.shape[2] // lanes
    group = max(1, 16 // each)

    @pl.loop(0, pieces // group)
    def _(g):
        for b in range(blocks):
            tiles = []
            for i in range(group * each):
                k, place = g * group + i // each, i % each * blocks + b
                tiles.append(bufs[k, bits_s[base + k, place // lanes, place % lanes]])
            value = turn(jnp.concatenate(tiles, axis=0), group * each, times)
            panel[:, aligned(g * group * each, group * each), b * lanes : (b + 1) * lanes] = value

    total = None
    for t in range(times):
        value = lax.dot_general(turned[t], panel[t], (((1,), (1,)), ((), ())), preferred_element_type=F32)
        total = value if total is None else total + value
    return total


def last_kernel(pieces, each, *refs):
    msgs = refs[:pieces]
    group_ref, member_ref, index_ref, var_ref, turned, before_ref, over_ref, out_ref, bufs, bits_v, bits_s, panel, sem = refs[pieces:]
    _, lanes = bufs.shape[2:]
    rows, cells = turned.shape[1:]
    copies = [pltpu.make_async_copy(msg, bufs.at[k], sem.at[k]) for k, msg in enumerate(msgs)]
    for copy in copies:
        copy.start()
    for k, copy in enumerate(copies):
        copy.wait()
        read_head(bufs.at[k], each, cells // lanes, bits_v.at[k], flagged=True)
    bits_copy = pltpu.make_async_copy(bits_v, bits_s, sem.at[pieces])
    bits_copy.start()
    size = out_ref.shape[1]
    row = lax.broadcasted_iota(I32, (size, size), 0)
    half = size // each // 2
    hi, lo = split(group_ref[0], 2)
    target = row
    for k in range(size // each):
        back = hi - k // 2
        source = jnp.where(back < 0, back + half, back) * 2 + lax.bitwise_xor(lo, k % 2)
        target = jnp.where((row >= k * each) & (row < (k + 1) * each), row + (source - k) * each, target)
    select = (lax.broadcasted_iota(I32, (size, size), 1) == target).astype(F32).astype(BF16)
    spot = lax.broadcasted_iota(I32, (rows, size), 0) + group_ref[0] * rows
    variance = jnp.broadcast_to(var_ref[...], (8, rows)).T[:, 0:1]
    diagonal = jnp.where((spot == index_ref[...]) & (member_ref[0] == 0), variance, 0.0)
    bits_copy.wait()
    over = over_ref[0] + panel_over(bufs, bits_s, 0, pieces, each)
    total = panel_products(bufs, bits_s, 0, pieces, each, turned, panel)
    value = jnp.concatenate([before_ref[...], total], axis=1)
    total = diagonal
    for _ in range(3):
        high = value.astype(BF16)
        total = total + jnp.dot(high, select, preferred_element_type=F32)
        value = value - high.astype(F32)
    out_ref[0:rows, :] = total
    out_ref[rows:, :] = jnp.broadcast_to(over, (8, size)).astype(F32)


def panel_last(msgs, turned, each, group, member, panel_index, error_var, before, over):
    slots, times, lanes = msgs[0].shape
    rows, cells = turned.shape[1:]
    pieces = len(msgs)
    return pl.pallas_call(
        functools.partial(last_kernel, pieces, each),
        out_shape=shape_of((rows + 8, before.shape[1] + pieces * each), F32),
        in_specs=[ANY] * pieces + [SMEM, SMEM, VMEM, VMEM, VMEM, VMEM, SMEM],
        out_specs=VMEM,
        scratch_shapes=[
            pltpu.VMEM((pieces, slots, times, lanes), BF16),
            pltpu.VMEM((pieces, 8, lanes), I32),
            pltpu.SMEM((pieces, 8, lanes), I32),
            pltpu.VMEM((times, pieces * each, cells), BF16),
            pltpu.SemaphoreType.DMA((pieces + 1,)),
        ],
        compiler_params=params(14),
        cost_estimate=cost(3),
        name="panel_last",
    )(*msgs, group[None], member[None], panel_index[None, :], error_var[None, :], turned, before, over)


def partner(value, axis, count):
    return lax.ppermute(value, axis, [(i, i ^ 1) for i in range(count)])


def shifted(value, axis, count, shift, flip=0):
    return lax.ppermute(value, axis, [(i, ((i + 2 * shift) % count) ^ flip) for i in range(count)])


def row_major(value):
    return with_layout_constraint(value, Layout(tuple(range(value.ndim))))


def cell_parts(part, cells):
    moves = [(shift, flip) for shift in range(cells // 2) for flip in range(2)]
    return [part] + [shifted(part, "cell", cells, shift, flip) for shift, flip in moves[1:]]


def add_up(parts):
    return functools.reduce(jnp.add, parts)


def dense_way(cells, observers, footprint, block_mask, own, time_cov, mine, sources):
    obs_rows, times, cell_local = footprint.shape
    blocks = block_mask.shape[1]
    keep = block_mask.astype(BF16)[:, None, :, None]
    feet = (footprint.reshape(obs_rows, times, blocks, cell_local // blocks) * keep).reshape(footprint.shape)

    def add(carry, _):
        total, feet, info = carry
        dx = info[0][:, None] - own[0][None, :]
        dy = info[1][:, None] - own[1][None, :]
        decay = jnp.exp(-jnp.sqrt(dx * dx + dy * dy + 1.0) / LENGTH)
        cov = (decay * (info[2][:, None] * own[2][None, :])).astype(BF16)
        total = total + jnp.dot(feet.reshape(-1, cell_local), cov, preferred_element_type=F32)
        ring = [(i, (i + 1) % cells) for i in range(cells)]
        return (total, lax.ppermute(feet, "cell", ring), lax.ppermute(info, "cell", ring)), None

    zero = jnp.zeros((obs_rows * times, cell_local), F32)
    (total, _, _), _ = lax.scan(add, (zero, feet, own), None, length=cells)
    cov_product = jnp.einsum(
        "ts,ksc->ktc", time_cov, total.reshape(obs_rows, times, cell_local), precision=lax.Precision.HIGHEST
    ).astype(BF16)
    flat = cov_product.reshape(obs_rows, times * cell_local)

    def meet(held, _):
        both = jnp.concatenate([held, partner(held, "obs", observers)], axis=0)
        part = lax.dot_general(
            flat, both.reshape(both.shape[0], -1), (((1,), (1,)), ((), ())), preferred_element_type=F32
        )
        return shifted(held, "obs", observers, 1), part

    _, parts = lax.scan(meet, jnp.take(feet, mine, axis=0), None, length=observers // 2)
    parts = parts.transpose(1, 0, 2).reshape(obs_rows, observers, -1)
    ordered = jnp.zeros_like(parts).at[:, sources].set(parts)
    return cov_product, add_up(cell_parts(ordered.reshape(obs_rows, -1), cells))


def body(cells, observers, footprint, block_mask, cell_coords, cell_sigma, time_cov, error_var, panel_index):
    obs_rows, _, cell_local = footprint.shape
    blocks = block_mask.shape[1]
    group = lax.axis_index("obs")
    each = panel_index.shape[0] // observers
    half = observers // 2
    member = lax.axis_index("cell")
    unit = math.gcd(16, obs_rows)
    slots = slot_count(obs_rows * blocks, 1 + blocks)
    chunks = chunk_sizes(slots, obs_rows * blocks, 1 + blocks)
    mask = block_mask.T

    room = slots - 2 - blocks - 1
    own_panel = pack_panel(mask, panel_index, group, member, footprint, each, slot_count(each * blocks, 1), room)
    ring = [own_panel]
    for _ in range(1, half):
        ring.append(shifted(ring[-1], "obs", observers, 1))
    messages = []
    for held in ring:
        messages += [held, partner(held, "obs", observers)]
    own_msg = pack_feet(mask, cell_coords, cell_sigma[None, :], footprint, chunks)
    far_msgs = []
    for shift in range(1, cells // 2):
        far_msgs.append([shifted(c, "cell", cells, shift) for c in own_msg])
    mate_msg = [partner(c, "cell", cells) for c in own_msg]
    for shift in range(1, cells // 2):
        far_msgs.append([partner(c, "cell", cells) for c in far_msgs[shift - 1]])

    dense, own_cov, info = start_call(own_msg, obs_rows, cell_local)
    near, mate_dense, mate_cov = own_call(mate_msg, dense, own_cov, info)
    firsts = [msg[0] for msg in far_msgs]
    few = len(firsts) // 2
    some_cov = far_start(firsts[:few], info)
    near, more_cov = mate_call(firsts[few:], near, mate_dense, mate_cov, info)
    far_cov = (some_cov, more_cov)
    mix = mixing(time_cov, unit)
    first_cov, start = first_rows([msg[:-1] for msg in far_msgs], far_cov, near, mix, obs_rows, unit, slots)
    cut = len(messages) * 3 // 4
    cov_product, turned, before, over = late_rows(
        far_msgs, messages[:cut], each, far_cov, near, mix, start, first_cov, unit, slots
    )
    part = panel_last(messages[cut:], turned, each, group, member, panel_index, error_var, before, over)

    part, late_group, late_mask = lax.optimization_barrier((part, group, mask))
    parts = cell_parts(part, cells)
    total = add_up([value[:obs_rows] for value in parts])
    over = add_up([value[obs_rows, 0] for value in parts])

    def again(carry):
        wanted = carry[0]
        kept, cell_info, place = (jnp.where(wanted, value, 0) for value in (late_mask, info, late_group))
        order = jnp.arange(observers, dtype=I32)
        from_group = (place // 2 - order // 2) % half * 2 + (place % 2 ^ (order % 2))
        mine = lax.dynamic_slice_in_dim(panel_index, place * each, each) - place * obs_rows
        cov_product, total = dense_way(
            cells, observers, footprint, kept.T, cell_info, time_cov, mine, from_group
        )
        positions = jnp.arange(obs_rows, dtype=I32) + place * obs_rows
        on_diagonal = (positions[:, None] == panel_index[None, :]).astype(F32)
        return jnp.bool_(False), cov_product, row_major(total + error_var[:, None] * on_diagonal)

    carry = (over > 0, cov_product, row_major(total))
    return lax.while_loop(lambda carry: carry[0], again, carry)[1:]


def solution(mesh):
    in_specs = (
        P("obs", None, "cell"),
        P("obs", "cell"),
        P(None, "cell"),
        P("cell"),
        P(),
        P("obs"),
        P(),
    )
    out_specs = (P("obs", None, "cell"), P("obs", None))
    cells, observers = mesh.shape["cell"], mesh.shape["obs"]

    def per_device(*args):
        return body(cells, observers, *args)

    return jax.shard_map(per_device, mesh=mesh, in_specs=in_specs, out_specs=out_specs, check_vma=False)
```

```python
import functools
import math

import jax
import jax.numpy as jnp
from jax import lax
from jax.experimental import pallas as pl
from jax.experimental.pallas import tpu as pltpu
from jax.experimental.layout import Layout, with_layout_constraint
from jax.sharding import PartitionSpec as P


GRID = 64
LENGTH = GRID / 16.0
F32, BF16, I32 = jnp.float32, jnp.bfloat16, jnp.int32
SHIFT = 4
INFO = 8


VMEM = pl.BlockSpec(memory_space=pltpu.VMEM)
SMEM = pl.BlockSpec(memory_space=pltpu.SMEM)
ANY = pl.BlockSpec(memory_space=pl.ANY)
HBM = pl.BlockSpec(memory_space=pltpu.HBM)


def shape_of(shape, dtype):
    return jax.ShapeDtypeStruct(shape, dtype)


def params(mib):
    return pltpu.CompilerParams(vmem_limit_bytes=mib * 2**20)


def cost(micros):
    return pl.CostEstimate(flops=int(micros * 9e8), bytes_accessed=1_000_000, transcendentals=0)


def aligned(start, size):
    return pl.ds(pl.multiple_of(start, size), size)


def slot_count(tiles, extra):
    room = tiles / 2 + 4.0 * math.sqrt(tiles / 4)
    return extra + min(tiles + 1, 2 * math.ceil(room / 2) + 1)


def chunk_sizes(slots, tiles, extra):
    most = min(slots - 2, extra + math.ceil(tiles / 4 + 3 * math.sqrt(tiles / 8)))
    return extra, most - extra, slots - most


def pack_rows(mask_at, feet_at, begin, end, blocks, buf, carry):
    slots, _, lanes = buf.shape
    row_of = lax.broadcasted_iota(I32, (8, lanes), 0)
    lane_of = lax.broadcasted_iota(I32, (8, lanes), 1)
    flat = row_of * lanes + lane_of
    batch = math.gcd(2, end - begin)

    def some(i, carry):
        pos, head, ends = carry
        first = begin + i * batch
        tiles = [[feet_at(first + j, b) for b in range(blocks)] for j in range(batch)]
        kept = [[mask_at(first + j, b) for b in range(blocks)] for j in range(batch)]
        for j in range(batch):
            for b in range(blocks):
                buf[jnp.minimum(pos, slots - 1)] = tiles[j][b]
                head = jnp.where(flat == (first + j) * blocks + b, kept[j][b] * pos, head)
                pos = pos + kept[j][b]
            ends = jnp.where(lane_of == first + j, pos, ends)
        return pos, head, ends

    return lax.fori_loop(0, (end - begin) // batch, some, carry)


def no_rows(first, lanes):
    zeros = jnp.zeros((8, lanes), I32)
    return jnp.int32(first), zeros, zeros


def write_head(carry, rows, blocks, buf, head_v, flag=None):
    lanes = buf.shape[2]
    deep = -(-rows * blocks // lanes)
    _, head, ends = carry
    low = (1 << SHIFT) - 1
    head_v[...] = jnp.zeros_like(head_v)
    head_v[0:deep, :] = (head >> SHIFT)[0:deep].astype(F32)
    head_v[deep : 2 * deep, :] = (head & low)[0:deep].astype(F32)
    head_v[2 * deep : 2 * deep + 1, :] = (ends >> SHIFT)[0:1].astype(F32)
    head_v[2 * deep + 1 : 2 * deep + 2, :] = (ends & low)[0:1].astype(F32)
    if flag is not None:
        head_v[2 * deep + 2 : 2 * deep + 3, :] = jnp.broadcast_to(flag, (1, lanes)).astype(F32)
    buf[0] = head_v[...].astype(BF16)


def pack_feet_kernel(chunks, mask_ref, coords_hbm, sigma_hbm, feet_ref, *rest):
    outs, (coords_ref, sigma_ref, feet, buf, head_v, small_sem, in_sem, sem) = (
        rest[: len(chunks)],
        rest[len(chunks) :],
    )
    blocks, rows = mask_ref.shape
    small = [
        pltpu.make_async_copy(src, dst, small_sem.at[k])
        for k, (src, dst) in enumerate(((coords_hbm, coords_ref), (sigma_hbm, sigma_ref)))
    ]
    for copy in small:
        copy.start()
    times, lanes = buf.shape[1:]
    groups = in_sem.shape[0]
    each = rows // groups
    loads = [
        pltpu.make_async_copy(feet_ref.at[pl.ds(g * each, each)], feet.at[pl.ds(g * each, each)], in_sem.at[g])
        for g in range(groups)
    ]
    for load in loads:
        load.start()
    for copy in small:
        copy.wait()
    sigma = sigma_ref[...]
    high = sigma.astype(BF16).astype(F32)
    middle = (sigma - high).astype(BF16).astype(F32)
    lowest = sigma - high - middle
    at = lax.broadcasted_iota(I32, (times, sigma.shape[1]), 0)
    info = jnp.zeros(at.shape, F32)
    for k, row in enumerate((coords_ref[0:1, :].astype(F32), coords_ref[1:2, :].astype(F32), high, middle, lowest)):
        info = jnp.where(at == k, row, info)
    info = info.astype(BF16)
    for b in range(blocks):
        buf[1 + b] = info[:, b * lanes : (b + 1) * lanes]
    carry = no_rows(1 + blocks, lanes)
    for g in range(groups):
        loads[g].wait()
        carry = pack_rows(
            lambda o, b: mask_ref[b, o],
            lambda o, b: feet[o, :, b * lanes : (b + 1) * lanes],
            g * each,
            (g + 1) * each,
            blocks,
            buf,
            carry,
        )
    write_head(carry, rows, blocks, buf, head_v)
    copies, first = [], 0
    for k, size in enumerate(chunks):
        copies.append(pltpu.make_async_copy(buf.at[pl.ds(first, size)], outs[k], sem.at[k]))
        first += size
    for copy in copies:
        copy.start()
    for copy in copies:
        copy.wait()


def pack_feet(mask, coords, sigma, feet, chunks):
    rows, times, cells = feet.shape
    lanes = cells // mask.shape[0]
    groups = math.gcd(4, rows)
    return pl.pallas_call(
        functools.partial(pack_feet_kernel, chunks),
        out_shape=tuple(shape_of((size, times, lanes), BF16) for size in chunks),
        in_specs=[SMEM, HBM, HBM, HBM],
        out_specs=(ANY,) * len(chunks),
        scratch_shapes=[
            pltpu.VMEM(coords.shape, I32),
            pltpu.VMEM(sigma.shape, F32),
            pltpu.VMEM((rows, times, cells), BF16),
            pltpu.VMEM((sum(chunks), times, lanes), BF16),
            pltpu.VMEM((times, lanes), F32),
            pltpu.SemaphoreType.DMA((2,)),
            pltpu.SemaphoreType.DMA((groups,)),
            pltpu.SemaphoreType.DMA((len(chunks),)),
        ],
        compiler_params=params(12),
        cost_estimate=cost(3),
        name="pack_feet",
    )(mask, coords, sigma, feet)


def pack_panel_kernel(room, mask_ref, mask_hbm, index_ref, group_ref, member_ref, feet_ref, out_ref, mask_v, rows_buf, head_v, small_sem, sem):
    count = rows_buf.shape[0]
    blocks, obs = mask_ref.shape
    lanes = out_ref.shape[2]
    mask_copy = pltpu.make_async_copy(mask_hbm, mask_v, small_sem.at[0])
    mask_copy.start()
    base = group_ref[0]
    rows = [jnp.clip(index_ref[base * count + j] - base * obs, 0, obs - 1) for j in range(count)]
    copies = [pltpu.make_async_copy(feet_ref.at[rows[j]], rows_buf.at[j], sem.at[j]) for j in range(count)]
    for copy in copies:
        copy.start()
    mask_copy.wait()
    flag = (jnp.sum(mask_v[...].astype(F32), axis=(0, 1), keepdims=True) > room).astype(I32)
    for copy in copies:
        copy.wait()

    def mask_at(o, b):
        return mask_ref[b, jnp.clip(index_ref[base * count + o] - base * obs, 0, obs - 1)]

    carry = pack_rows(
        mask_at, lambda o, b: rows_buf[o, :, b * lanes : (b + 1) * lanes], 0, count, blocks, out_ref, no_rows(1, lanes)
    )
    write_head(carry, count, blocks, out_ref, head_v, flag)


def pack_panel(mask, panel_index, group, member, feet, count, slots, room):
    _, times, cells = feet.shape
    lanes = cells // mask.shape[0]
    return pl.pallas_call(
        functools.partial(pack_panel_kernel, room),
        out_shape=shape_of((slots, times, lanes), BF16),
        in_specs=[SMEM, HBM, SMEM, SMEM, SMEM, HBM],
        out_specs=VMEM,
        scratch_shapes=[
            pltpu.VMEM(mask.shape, I32),
            pltpu.VMEM((count, times, cells), BF16),
            pltpu.VMEM((times, lanes), F32),
            pltpu.SemaphoreType.DMA((1,)),
            pltpu.SemaphoreType.DMA((count,)),
        ],
        compiler_params=params(8),
        cost_estimate=cost(2),
        name="pack_panel",
    )(mask, mask, panel_index, group[None], member[None], feet)


def fetch(chunks, buf, sem):
    copies, first = [], 0
    for k, chunk in enumerate(chunks):
        copies.append(pltpu.make_async_copy(chunk, buf.at[pl.ds(first, chunk.shape[0])], sem.at[k]))
        copies[-1].start()
        first += chunk.shape[0]
    return copies


def read_head(buf, rows, blocks, bits_v, flagged=False):
    slots, _, lanes = buf.shape
    deep = -(-rows * blocks // lanes)
    head = buf[0].astype(F32)
    scale = float(1 << SHIFT)
    bits_v[0:deep, :] = jnp.minimum(head[0:deep] * scale + head[deep : 2 * deep], slots - 1.0).astype(I32)
    bits_v[5:6, :] = (head[2 * deep : 2 * deep + 1] * scale + head[2 * deep + 1 : 2 * deep + 2]).astype(I32)
    if flagged:
        bits_v[6:7, :] = head[2 * deep + 2 : 2 * deep + 3].astype(I32)
    buf[0] = jnp.zeros(buf.shape[1:], buf.dtype)


def split(number, size):
    if size & (size - 1):
        return lax.div(number, size), lax.rem(number, size)
    return lax.shift_right_logical(number, size.bit_length() - 1), lax.bitwise_and(number, size - 1)


def expand(buf, bits, first, count, blocks, store, unrolled=False):
    lanes = buf.shape[2]
    batch = math.gcd(2, count)

    def some(i, _):
        tiles = []
        for j in range(batch):
            row, col = split(jnp.int32((first + i * batch + j) * blocks), lanes)
            tiles += [buf[bits[row, col + b]] for b in range(blocks)]
        for j in range(batch):
            for b in range(blocks):
                store(i * batch + j, b, tiles[j * blocks + b])
        return 0

    if unrolled:
        for i in range(count // batch):
            some(i, 0)
    else:
        lax.fori_loop(0, count // batch, some, 0)


def into(dense, times, lanes, offset, first=0):
    def store(i, b, tile):
        at = aligned((first + i) * times, times)
        dense[at, offset + b * lanes : offset + (b + 1) * lanes] = tile.astype(dense.dtype)

    return store


def read_info(buf, blocks, row_v, turned):
    _, lanes = buf.shape[1:]
    for b in range(blocks):
        tile = buf[1 + b].astype(F32)[0:INFO]
        sigma = tile[2:3] + tile[3:4] + tile[4:5]
        tile = jnp.where(lax.broadcasted_iota(I32, tile.shape, 0) == 2, sigma, tile)
        at = slice(b * lanes, (b + 1) * lanes)
        if row_v is not None:
            row_v[:, at] = tile
        if turned is not None:
            turned[at, :] = tile.T


def fill_covariance(dst, dst_first, src_first, rows, turned, own):
    x, y, s = own[0:1, :], own[1:2, :], own[2:3, :]
    step = min(32, rows)
    for i in range(rows // step):
        at = aligned(src_first + i * step, step)
        dx = turned[at, 0:1] - x
        dy = turned[at, 1:2] - y
        square = dx * dx + dy * dy + 1.0
        decay = jnp.exp2(square * lax.rsqrt(square) * (-math.log2(math.e) / LENGTH))
        dst[aligned(dst_first + i * step, step), :] = (decay * (turned[at, 2:3] * s)).astype(BF16)


def start_kernel(chunks, *refs):
    msg = refs[:chunks]
    dense, cov, info_ref, buf, bits_v, bits_s, turned, sem = refs[chunks:]
    times, lanes = buf.shape[1:]
    cells = cov.shape[1]
    blocks = cells // lanes
    rows = dense.shape[0] // times
    copies = fetch(msg, buf, sem)
    copies[0].wait()
    read_head(buf, rows, blocks, bits_v)
    copy = pltpu.make_async_copy(bits_v, bits_s, sem.at[chunks])
    copy.start()
    read_info(buf, blocks, info_ref, turned)
    for other in copies[1:]:
        other.wait()
    half = cells // 2
    fine = math.gcd(4, rows // 2)

    @pl.loop(0, fine)
    def _(i):
        fill_covariance(cov, i * (half // fine), i * (half // fine), half // fine, turned, info_ref)

    copy.wait()

    @pl.loop(0, fine)
    def _(i):
        first = half + i * (half // fine)
        fill_covariance(cov, first, first, half // fine, turned, info_ref)
        some = rows // fine
        expand(buf, bits_s, i * some, some, blocks, into(dense, times, lanes, 0, i * some), unrolled=True)


def start_call(own_msg, rows, cells):
    times, lanes = own_msg[0].shape[1:]
    slots = sum(chunk.shape[0] for chunk in own_msg)
    chunks = len(own_msg)
    return pl.pallas_call(
        functools.partial(start_kernel, chunks),
        out_shape=(
            shape_of((rows * times, cells), BF16),
            shape_of((cells, cells), BF16),
            shape_of((INFO, cells), F32),
        ),
        in_specs=[ANY] * chunks,
        out_specs=(VMEM,) * 3,
        scratch_shapes=[
            pltpu.VMEM((slots, times, lanes), BF16),
            pltpu.VMEM((8, lanes), I32),
            pltpu.SMEM((8, lanes), I32),
            pltpu.VMEM((cells, INFO), F32),
            pltpu.SemaphoreType.DMA((chunks + 1,)),
        ],
        compiler_params=params(12),
        cost_estimate=cost(4),
        name="own_start",
    )(*own_msg)


def own_kernel(chunks, *refs):
    msg = refs[:chunks]
    dense, cov, info_ref, out_ref, mate_dense, next_ref, buf, bits_v, bits_s, turned, sem = refs[chunks:]
    times, lanes = buf.shape[1:]
    cells = cov.shape[1]
    blocks = cells // lanes
    rows = dense.shape[0] // times
    tall = min(256, rows * times)
    steps = rows * times // tall
    part = cells // steps
    copies = fetch(msg, buf, sem)
    copies[0].wait()
    read_head(buf, rows, blocks, bits_v)
    bits_copy = pltpu.make_async_copy(bits_v, bits_s, sem.at[chunks])
    bits_copy.start()
    read_info(buf, blocks, None, turned)
    for copy in copies[1:]:
        copy.wait()
    bits_copy.wait()

    @pl.loop(0, steps)
    def _(u):
        here = aligned(u * tall, tall)
        fill_covariance(next_ref, u * part, u * part, part, turned, info_ref)
        out_ref[here, :] = jnp.dot(dense[here, :], cov[...], preferred_element_type=F32)
        some = rows // steps
        expand(buf, bits_s, u * some, some, blocks, into(mate_dense, times, lanes, 0, u * some), unrolled=True)


def own_call(mate_msg, dense, cov, info):
    times, lanes = mate_msg[0].shape[1:]
    cells = cov.shape[1]
    slots = sum(chunk.shape[0] for chunk in mate_msg)
    chunks = len(mate_msg)
    return pl.pallas_call(
        functools.partial(own_kernel, chunks),
        out_shape=(shape_of(dense.shape, F32), shape_of(dense.shape, BF16), shape_of((cells, cells), BF16)),
        in_specs=[ANY] * chunks + [VMEM] * 3,
        out_specs=(VMEM,) * 3,
        scratch_shapes=[
            pltpu.VMEM((slots, times, lanes), BF16),
            pltpu.VMEM((8, lanes), I32),
            pltpu.SMEM((8, lanes), I32),
            pltpu.VMEM((cells, INFO), F32),
            pltpu.SemaphoreType.DMA((chunks + 1,)),
        ],
        compiler_params=params(16),
        cost_estimate=cost(6),
        name="own_product",
    )(*mate_msg, dense, cov, info)


def far_info(firsts, info_buf, turned, sem):
    blocks = info_buf.shape[1] - 1
    cells = turned.shape[0] // len(firsts)
    copies = []
    for k, first in enumerate(firsts):
        copies.append(pltpu.make_async_copy(first.at[pl.ds(0, 1 + blocks)], info_buf.at[k], sem.at[k]))
        copies[-1].start()
    for k, copy in enumerate(copies):
        copy.wait()
        read_info(info_buf.at[k], blocks, None, turned.at[pl.ds(k * cells, cells)])


def far_start_kernel(count, *refs):
    firsts = refs[:count]
    info_ref, far_ref, info_buf, turned, sem = refs[count:]
    far_info(firsts, info_buf, turned, sem)
    cells = info_ref.shape[1]
    piece = min(128, cells)

    @pl.loop(0, count * cells // piece)
    def _(i):
        fill_covariance(far_ref, i * piece, i * piece, piece, turned, info_ref)


def far_scratch(firsts, cells):
    times, lanes = firsts[0].shape[1:]
    return [
        pltpu.VMEM((len(firsts), 1 + cells // lanes, times, lanes), BF16),
        pltpu.VMEM((len(firsts) * cells, INFO), F32),
        pltpu.SemaphoreType.DMA((len(firsts),)),
    ]


def far_start(firsts, info):
    cells = info.shape[1]
    count = len(firsts)
    return pl.pallas_call(
        functools.partial(far_start_kernel, count),
        out_shape=shape_of((count * cells, cells), BF16),
        in_specs=[ANY] * count + [VMEM],
        out_specs=VMEM,
        scratch_shapes=far_scratch(firsts, cells),
        compiler_params=params(10),
        cost_estimate=cost(4),
        name="far_start",
    )(*firsts, info)


def mate_kernel(count, *refs):
    firsts = refs[:count]
    near_ref, dense, cov_ref, info_ref, out_ref, far_ref, info_buf, turned, sem = refs[count:]
    cells = cov_ref.shape[1]
    tall = min(256, dense.shape[0])
    steps = dense.shape[0] // tall
    part = count * cells // steps
    far_info(firsts, info_buf, turned, sem)

    @pl.loop(0, steps)
    def _(u):
        here = aligned(u * tall, tall)
        fill_covariance(far_ref, u * part, u * part, part, turned, info_ref)
        out_ref[here, :] = near_ref[here, :] + jnp.dot(dense[here, :], cov_ref[...], preferred_element_type=F32)


def mate_call(firsts, near, mate_dense, cov, info):
    cells = cov.shape[1]
    count = len(firsts)
    return pl.pallas_call(
        functools.partial(mate_kernel, count),
        out_shape=(shape_of(near.shape, F32), shape_of((count * cells, cells), BF16)),
        in_specs=[ANY] * count + [VMEM] * 4,
        out_specs=(VMEM, VMEM),
        scratch_shapes=far_scratch(firsts, cells),
        input_output_aliases={count: 0},
        compiler_params=params(16),
        cost_estimate=cost(5),
        name="mate_product",
    )(*firsts, near, mate_dense, cov, info)


def mixed_unit(mix_ref, value):
    high = value.astype(BF16)
    low = (value - high.astype(F32)).astype(BF16)
    stacked = jnp.concatenate([high, low, high], axis=0)
    return jnp.dot(mix_ref[...], stacked, preferred_element_type=F32).astype(BF16)


def turn(value, rows, times):
    return jnp.swapaxes(value.reshape(rows, times, value.shape[1]), 0, 1)


def unit_step(u, count, unit, bufs, bits_s, dense_a, dense_b, near_ref, cov_refs, mix_ref, rows):
    times, _ = bufs.shape[2:]
    cells = near_ref.shape[1]
    few = count // 2
    here = aligned(u * unit * times, unit * times)
    place(u, few, count, unit, bufs, bits_s, dense_b, cells)
    value = near_ref[here, :] + jnp.dot(dense_a[...], cov_refs[0][...], preferred_element_type=F32)
    place(jnp.minimum(u + 1, rows // unit - 1), 0, few, unit, bufs, bits_s, dense_a, cells)
    value = value + jnp.dot(dense_b[...], cov_refs[1][...], preferred_element_type=F32)
    return mixed_unit(mix_ref, value)


def place(u, begin, end, unit, bufs, bits_s, dense, cells):
    times, lanes = bufs.shape[2:]
    for k in range(begin, end):
        store = into(dense, times, lanes, (k - begin) * cells)
        expand(bufs.at[k], bits_s.at[k], u * unit, unit, cells // lanes, store, unrolled=bufs.shape[0] <= 4)


def first_kernel(count, chunks, unit, *refs):
    msgs = [refs[k * chunks : (k + 1) * chunks] for k in range(count)]
    *cov_refs, near_ref, mix_ref, out_ref, next_ref, bufs, bits_v, bits_s, dense_a, dense_b, sem = refs[count * chunks :]
    times, lanes = bufs.shape[2:]
    cells = near_ref.shape[1]
    blocks = cells // lanes
    rows = out_ref.shape[0]
    limit = sum(chunk.shape[0] for chunk in msgs[0])
    copies = [fetch(msgs[k], bufs.at[k], sem.at[k]) for k in range(count)]
    for k in range(count):
        copies[k][0].wait()
        read_head(bufs.at[k], rows, blocks, bits_v.at[k])
    bits_copy = pltpu.make_async_copy(bits_v, bits_s, sem.at[count, 0])
    bits_copy.start()
    for k in range(count):
        for copy in copies[k][1:]:
            copy.wait()
    bits_copy.wait()
    ready = jnp.int32(0)
    for u in range(rows // unit):
        whole = jnp.int32(1)
        for k in range(count):
            whole = whole * (bits_s[k, 5, (u + 1) * unit - 1] <= limit).astype(I32)
        ready = ready + whole
    next_ref[0] = ready
    place(jnp.int32(0), 0, count // 2, unit, bufs, bits_s, dense_a, cells)

    def step(u, _):
        mixed = unit_step(u, count, unit, bufs, bits_s, dense_a, dense_b, near_ref, cov_refs, mix_ref, rows)
        out_ref[aligned(u * unit, unit)] = mixed.reshape(unit, times, cells)
        return 0

    lax.fori_loop(0, ready, step, 0)


def rows_scratch(count, chunks, slots, times, lanes, unit, cells, more):
    return [
        pltpu.VMEM((count, slots, times, lanes), BF16),
        pltpu.VMEM((count + more, 8, lanes), I32),
        pltpu.SMEM((count + more, 8, lanes), I32),
        pltpu.VMEM((unit * times, count // 2 * cells), BF16),
        pltpu.VMEM((unit * times, (count - count // 2) * cells), BF16),
        pltpu.SemaphoreType.DMA((count + 1, chunks)),
    ]


def first_rows(msgs, covs, near, mix, rows, unit, slots):
    times, lanes = msgs[0][0].shape[1:]
    cells = near.shape[1]
    count, chunks = len(msgs), len(msgs[0])
    flat = [chunk for msg in msgs for chunk in msg]
    return pl.pallas_call(
        functools.partial(first_kernel, count, chunks, unit),
        out_shape=(shape_of((rows, times, cells), BF16), shape_of((1,), I32)),
        in_specs=[ANY] * len(flat) + [VMEM] * 4,
        out_specs=(VMEM, SMEM),
        scratch_shapes=rows_scratch(count, chunks, slots, times, lanes, unit, cells, 0),
        compiler_params=params(16),
        cost_estimate=cost(7),
        name="first_rows",
    )(*flat, *covs, near, mix)


def late_kernel(count, chunks, unit, pieces, each, *refs):
    msgs = [refs[k * chunks : (k + 1) * chunks] for k in range(count)]
    panel_msgs = refs[count * chunks : count * chunks + pieces]
    refs = refs[count * chunks + pieces :]
    *cov_refs, near_ref, mix_ref, start_ref, done_ref, out_ref, turned_ref, part_ref, over_ref = refs[:10]
    bufs, bits_v, bits_s, dense_a, dense_b, sem, panel_bufs, stage, panel, panel_sem, out_sem = refs[10:]
    times, lanes = bufs.shape[2:]
    cells = near_ref.shape[1]
    blocks = cells // lanes
    rows = stage.shape[0]
    copies = [fetch(msgs[k], bufs.at[k], sem.at[k]) for k in range(count)]
    panel_copies = [pltpu.make_async_copy(msg, panel_bufs.at[k], panel_sem.at[k]) for k, msg in enumerate(panel_msgs)]
    for copy in panel_copies:
        copy.start()
    for k in range(count):
        copies[k][0].wait()
        read_head(bufs.at[k], rows, blocks, bits_v.at[k])
    for k, copy in enumerate(panel_copies):
        copy.wait()
        read_head(panel_bufs.at[k], each, blocks, bits_v.at[count + k], flagged=True)
    bits_copy = pltpu.make_async_copy(bits_v, bits_s, sem.at[count, 0])
    bits_copy.start()
    first = start_ref[0]

    def outgoing(u, src):
        at = aligned(u * unit, unit)
        return pltpu.make_async_copy(src.at[at], out_ref.at[at], out_sem.at[u])

    def carry_over(u, _):
        outgoing(u, done_ref).start()
        at = aligned(u * unit, unit)
        turned_ref[:, at, :] = turn(done_ref[at].reshape(unit * times, cells), unit, times)
        return 0

    lax.fori_loop(0, first, carry_over, 0)
    for k in range(count):
        for copy in copies[k][1:]:
            copy.wait()
    bits_copy.wait()
    place(jnp.minimum(first, rows // unit - 1), 0, count // 2, unit, bufs, bits_s, dense_a, cells)

    def step(u, _):
        mixed = unit_step(u, count, unit, bufs, bits_s, dense_a, dense_b, near_ref, cov_refs, mix_ref, rows)
        at = aligned(u * unit, unit)
        stage[at] = mixed.reshape(unit, times, cells)
        outgoing(u, stage).start()
        turned_ref[:, at, :] = turn(mixed, unit, times)
        return 0

    lax.fori_loop(first, rows // unit, step, 0)
    over_ref[0] = panel_over(panel_bufs, bits_s, count, pieces, each)
    part_ref[...] = panel_products(panel_bufs, bits_s, count, pieces, each, turned_ref, panel)

    def settle(u, _):
        outgoing(u, stage).wait()
        return 0

    lax.fori_loop(0, rows // unit, settle, 0)


def late_rows(msgs, panel_msgs, each, covs, near, mix, start, done, unit, slots):
    times, lanes = msgs[0][0].shape[1:]
    rows, _, cells = done.shape
    count, chunks, pieces = len(msgs), len(msgs[0]), len(panel_msgs)
    flat = [chunk for msg in msgs for chunk in msg] + list(panel_msgs)
    return pl.pallas_call(
        functools.partial(late_kernel, count, chunks, unit, pieces, each),
        out_shape=(
            shape_of(done.shape, BF16),
            shape_of((times, rows, cells), BF16),
            shape_of((rows, pieces * each), F32),
            shape_of((1,), I32),
        ),
        in_specs=[ANY] * len(flat) + [VMEM] * 4 + [SMEM, VMEM],
        out_specs=(HBM, VMEM, VMEM, SMEM),
        scratch_shapes=rows_scratch(count, chunks, slots, times, lanes, unit, cells, pieces)
        + [
            pltpu.VMEM((pieces, panel_msgs[0].shape[0], times, lanes), BF16),
            pltpu.VMEM((rows, times, cells), BF16),
            pltpu.VMEM((times, pieces * each, cells), BF16),
            pltpu.SemaphoreType.DMA((pieces,)),
            pltpu.SemaphoreType.DMA((rows // unit,)),
        ],
        compiler_params=params(20),
        cost_estimate=cost(9),
        name="late_rows",
    )(*flat, *covs, near, mix, start, done)


def mix_kernel(unit, time_ref, out_ref):
    times = time_ref.shape[0]
    size = unit * times
    value = time_ref[...]
    high = value.astype(BF16)
    low = (value - high.astype(F32)).astype(BF16)

    def same(shape, dim):
        index = lax.broadcasted_iota(I32, shape, 1 - dim) % times
        return (index == lax.broadcasted_iota(I32, shape, dim)).astype(F32).astype(BF16)

    row = lax.broadcasted_iota(I32, (size, size), 0)
    col = lax.broadcasted_iota(I32, (size, size), 1)
    for j, part in enumerate((high, high, low)):
        spread = jnp.dot(same((size, times), 1), part, preferred_element_type=F32).astype(BF16)
        spread = jnp.dot(spread, same((times, size), 0), preferred_element_type=F32)
        out_ref[:, j * size : (j + 1) * size] = jnp.where(row // times == col // times, spread, 0.0).astype(BF16)


def mixing(time_cov, unit):
    size = unit * time_cov.shape[0]
    return pl.pallas_call(
        functools.partial(mix_kernel, unit),
        out_shape=shape_of((size, 3 * size), BF16),
        in_specs=[VMEM],
        out_specs=VMEM,
        compiler_params=params(8),
        cost_estimate=cost(1),
        name="mixing",
    )(time_cov)


def panel_over(bufs, bits_s, base, pieces, each):
    slots, _, _ = bufs.shape[1:]
    over = jnp.int32(0)
    for k in range(pieces):
        ends = bits_s.shape[1] - 3
        over = over + (bits_s[base + k, ends, each - 1] > slots - 1).astype(I32) + bits_s[base + k, ends + 1, 0]
    return over


def panel_products(bufs, bits_s, base, pieces, each, turned, panel):
    times, lanes = bufs.shape[2:]
    blocks = panel.shape[2] // lanes
    group = max(1, 16 // each)

    @pl.loop(0, pieces // group)
    def _(g):
        for b in range(blocks):
            tiles = []
            for i in range(group * each):
                k, place = g * group + i // each, i % each * blocks + b
                tiles.append(bufs[k, bits_s[base + k, place // lanes, place % lanes]])
            value = turn(jnp.concatenate(tiles, axis=0), group * each, times)
            panel[:, aligned(g * group * each, group * each), b * lanes : (b + 1) * lanes] = value

    total = None
    for t in range(times):
        value = lax.dot_general(turned[t], panel[t], (((1,), (1,)), ((), ())), preferred_element_type=F32)
        total = value if total is None else total + value
    return total


def last_kernel(pieces, each, *refs):
    msgs = refs[:pieces]
    group_ref, member_ref, index_ref, var_ref, turned, before_ref, over_ref, out_ref, bufs, bits_v, bits_s, panel, sem = refs[pieces:]
    _, lanes = bufs.shape[2:]
    rows, cells = turned.shape[1:]
    copies = [pltpu.make_async_copy(msg, bufs.at[k], sem.at[k]) for k, msg in enumerate(msgs)]
    for copy in copies:
        copy.start()
    for k, copy in enumerate(copies):
        copy.wait()
        read_head(bufs.at[k], each, cells // lanes, bits_v.at[k], flagged=True)
    bits_copy = pltpu.make_async_copy(bits_v, bits_s, sem.at[pieces])
    bits_copy.start()
    size = out_ref.shape[1]
    row = lax.broadcasted_iota(I32, (size, size), 0)
    half = size // each // 2
    hi, lo = split(group_ref[0], 2)
    target = row
    for k in range(size // each):
        back = hi - k // 2
        source = jnp.where(back < 0, back + half, back) * 2 + lax.bitwise_xor(lo, k % 2)
        target = jnp.where((row >= k * each) & (row < (k + 1) * each), row + (source - k) * each, target)
    select = (lax.broadcasted_iota(I32, (size, size), 1) == target).astype(F32).astype(BF16)
    spot = lax.broadcasted_iota(I32, (rows, size), 0) + group_ref[0] * rows
    variance = jnp.broadcast_to(var_ref[...], (8, rows)).T[:, 0:1]
    diagonal = jnp.where((spot == index_ref[...]) & (member_ref[0] == 0), variance, 0.0)
    bits_copy.wait()
    over = over_ref[0] + panel_over(bufs, bits_s, 0, pieces, each)
    total = panel_products(bufs, bits_s, 0, pieces, each, turned, panel)
    value = jnp.concatenate([before_ref[...], total], axis=1)
    total = diagonal
    for _ in range(3):
        high = value.astype(BF16)
        total = total + jnp.dot(high, select, preferred_element_type=F32)
        value = value - high.astype(F32)
    out_ref[0:rows, :] = total
    out_ref[rows:, :] = jnp.broadcast_to(over, (8, size)).astype(F32)


def panel_last(msgs, turned, each, group, member, panel_index, error_var, before, over):
    slots, times, lanes = msgs[0].shape
    rows, cells = turned.shape[1:]
    pieces = len(msgs)
    return pl.pallas_call(
        functools.partial(last_kernel, pieces, each),
        out_shape=shape_of((rows + 8, before.shape[1] + pieces * each), F32),
        in_specs=[ANY] * pieces + [SMEM, SMEM, VMEM, VMEM, VMEM, VMEM, SMEM],
        out_specs=VMEM,
        scratch_shapes=[
            pltpu.VMEM((pieces, slots, times, lanes), BF16),
            pltpu.VMEM((pieces, 8, lanes), I32),
            pltpu.SMEM((pieces, 8, lanes), I32),
            pltpu.VMEM((times, pieces * each, cells), BF16),
            pltpu.SemaphoreType.DMA((pieces + 1,)),
        ],
        compiler_params=params(14),
        cost_estimate=cost(3),
        name="panel_last",
    )(*msgs, group[None], member[None], panel_index[None, :], error_var[None, :], turned, before, over)


def finish_kernel(*refs):
    *parts, out_ref, over_ref = refs
    rows = out_ref.shape[0]
    total = functools.reduce(jnp.add, [part[...] for part in parts])
    out_ref[...] = total[:rows]
    over_ref[0] = jnp.max(total[rows:]).astype(I32)


def finish(parts, rows):
    return pl.pallas_call(
        finish_kernel,
        out_shape=(shape_of((rows, parts[0].shape[1]), F32), shape_of((1,), I32)),
        in_specs=[VMEM] * len(parts),
        out_specs=(VMEM, SMEM),
        compiler_params=params(8),
        cost_estimate=cost(1),
        name="finish",
    )(*parts)


def partner(value, axis, count):
    return lax.ppermute(value, axis, [(i, i ^ 1) for i in range(count)])


def shifted(value, axis, count, shift, flip=0):
    return lax.ppermute(value, axis, [(i, ((i + 2 * shift) % count) ^ flip) for i in range(count)])


def row_major(value):
    return with_layout_constraint(value, Layout(tuple(range(value.ndim))))


def cell_parts(part, cells):
    moves = [(shift, flip) for shift in range(cells // 2) for flip in range(2)]
    return [part] + [shifted(part, "cell", cells, shift, flip) for shift, flip in moves[1:]]


def add_up(parts):
    return functools.reduce(jnp.add, parts)


def dense_way(cells, observers, footprint, block_mask, own, time_cov, mine, sources):
    obs_rows, times, cell_local = footprint.shape
    blocks = block_mask.shape[1]
    keep = block_mask.astype(BF16)[:, None, :, None]
    feet = (footprint.reshape(obs_rows, times, blocks, cell_local // blocks) * keep).reshape(footprint.shape)

    def add(carry, _):
        total, feet, info = carry
        dx = info[0][:, None] - own[0][None, :]
        dy = info[1][:, None] - own[1][None, :]
        decay = jnp.exp(-jnp.sqrt(dx * dx + dy * dy + 1.0) / LENGTH)
        cov = (decay * (info[2][:, None] * own[2][None, :])).astype(BF16)
        total = total + jnp.dot(feet.reshape(-1, cell_local), cov, preferred_element_type=F32)
        ring = [(i, (i + 1) % cells) for i in range(cells)]
        return (total, lax.ppermute(feet, "cell", ring), lax.ppermute(info, "cell", ring)), None

    zero = jnp.zeros((obs_rows * times, cell_local), F32)
    (total, _, _), _ = lax.scan(add, (zero, feet, own), None, length=cells)
    cov_product = jnp.einsum(
        "ts,ksc->ktc", time_cov, total.reshape(obs_rows, times, cell_local), precision=lax.Precision.HIGHEST
    ).astype(BF16)
    flat = cov_product.reshape(obs_rows, times * cell_local)

    def meet(held, _):
        both = jnp.concatenate([held, partner(held, "obs", observers)], axis=0)
        part = lax.dot_general(
            flat, both.reshape(both.shape[0], -1), (((1,), (1,)), ((), ())), preferred_element_type=F32
        )
        return shifted(held, "obs", observers, 1), part

    _, parts = lax.scan(meet, jnp.take(feet, mine, axis=0), None, length=observers // 2)
    parts = parts.transpose(1, 0, 2).reshape(obs_rows, observers, -1)
    ordered = jnp.zeros_like(parts).at[:, sources].set(parts)
    return cov_product, add_up(cell_parts(ordered.reshape(obs_rows, -1), cells))


def body(cells, observers, footprint, block_mask, cell_coords, cell_sigma, time_cov, error_var, panel_index):
    obs_rows, _, cell_local = footprint.shape
    blocks = block_mask.shape[1]
    group = lax.axis_index("obs")
    each = panel_index.shape[0] // observers
    half = observers // 2
    member = lax.axis_index("cell")
    unit = math.gcd(16, obs_rows)
    slots = slot_count(obs_rows * blocks, 1 + blocks)
    chunks = chunk_sizes(slots, obs_rows * blocks, 1 + blocks)
    mask = block_mask.T

    room = slots - 2 - blocks - 1
    own_panel = pack_panel(mask, panel_index, group, member, footprint, each, slot_count(each * blocks, 1), room)
    ring = [own_panel]
    for _ in range(1, half):
        ring.append(shifted(ring[-1], "obs", observers, 1))
    messages = []
    for held in ring:
        messages += [held, partner(held, "obs", observers)]
    own_msg = pack_feet(mask, cell_coords, cell_sigma[None, :], footprint, chunks)
    far_msgs = []
    for shift in range(1, cells // 2):
        far_msgs.append([shifted(c, "cell", cells, shift) for c in own_msg])
    mate_msg = [partner(c, "cell", cells) for c in own_msg]
    for shift in range(1, cells // 2):
        far_msgs.append([partner(c, "cell", cells) for c in far_msgs[shift - 1]])

    dense, own_cov, info = start_call(own_msg, obs_rows, cell_local)
    near, mate_dense, mate_cov = own_call(mate_msg, dense, own_cov, info)
    firsts = [msg[0] for msg in far_msgs]
    few = len(firsts) // 2
    some_cov = far_start(firsts[:few], info)
    near, more_cov = mate_call(firsts[few:], near, mate_dense, mate_cov, info)
    far_cov = (some_cov, more_cov)
    mix = mixing(time_cov, unit)
    first_cov, start = first_rows([msg[:-1] for msg in far_msgs], far_cov, near, mix, obs_rows, unit, slots)
    cut = len(messages) * 3 // 4
    cov_product, turned, before, over = late_rows(
        far_msgs, messages[:cut], each, far_cov, near, mix, start, first_cov, unit, slots
    )
    part = panel_last(messages[cut:], turned, each, group, member, panel_index, error_var, before, over)

    part, late_group, late_mask = lax.optimization_barrier((part, group, mask))
    total, over = finish(cell_parts(part, cells), obs_rows)

    def again(carry):
        wanted = carry[0]
        kept, cell_info, place = (jnp.where(wanted, value, 0) for value in (late_mask, info, late_group))
        order = jnp.arange(observers, dtype=I32)
        from_group = (place // 2 - order // 2) % half * 2 + (place % 2 ^ (order % 2))
        mine = lax.dynamic_slice_in_dim(panel_index, place * each, each) - place * obs_rows
        cov_product, total = dense_way(
            cells, observers, footprint, kept.T, cell_info, time_cov, mine, from_group
        )
        positions = jnp.arange(obs_rows, dtype=I32) + place * obs_rows
        on_diagonal = (positions[:, None] == panel_index[None, :]).astype(F32)
        return jnp.bool_(False), cov_product, row_major(total + error_var[:, None] * on_diagonal)

    carry = (over[0] > 0, cov_product, total)
    return lax.while_loop(lambda carry: carry[0], again, carry)[1:]


def solution(mesh):
    in_specs = (
        P("obs", None, "cell"),
        P("obs", "cell"),
        P(None, "cell"),
        P("cell"),
        P(),
        P("obs"),
        P(),
    )
    out_specs = (P("obs", None, "cell"), P("obs", None))
    cells, observers = mesh.shape["cell"], mesh.shape["obs"]

    def per_device(*args):
        return body(cells, observers, *args)

    return jax.shard_map(per_device, mesh=mesh, in_specs=in_specs, out_specs=out_specs, check_vma=False)
```
